256 devices in a mesh: seg: 64 (over z_hi, x, y, core), row: 4 (over z_lo).
Axes of the slice: x: 4, y: 4, z: 8 (z_hi: 2, z_lo: 4; z = z_hi * 4 + z_lo), core: 2. Of those that a mesh axis runs over, the one named last changes fastest.
Arguments:
- fill_blocks: int32 [128, 4], P('seg'), may hold values from 0 to 7, all different within a row
- fill_mask: int32 [128, 4], P('seg'), may hold values 0 or 1
- inv_diag: float32 [128, 512, 512], P('seg'), as said below
- factor_off: float32 [128, 256, 512], P('seg', 'row'), may hold values from -1.4375 to 1.4375
Outputs:
- cov_diag: float32 [128, 512, 512], P('seg', 'row')
- cov_off: float32 [128, 256, 512], P('seg', 'row')
The draws below stay inside these ranges and needn't reach their ends.
Inputs may be any that keep to these rules, and one draw needn't show every extreme that they name: The 4 entries of a row of fill_blocks are different. Each inv_diag[k] is lower triangular with a positive diagonal.
All inputs are finite; a program needn't handle non-finite values. No bound on the sum of `fill_mask` on one device may be relied on, other than what follows from the above.
Results may differ from the reference program's by a relative error of at most 0.0003.
Values sent between devices are 32-bit elements; how exact they have to be, the bound alone decides.
A program may use at most 64 MiB of HBM per device.

```python
import jax
import jax.numpy as jnp
from jax import lax

BLOCK = 64
W = 512
FILL = 4
K = 128
FILL_ROWS = 256


def draw_inv_diag(key, part):
    key_scale, key_noise = jax.random.split(jax.random.fold_in(key, 17))
    rows_at = lax.broadcasted_iota(jnp.int32, (W, W), 0)
    cols_at = lax.broadcasted_iota(jnp.int32, (W, W), 1)
    spread = jnp.exp(jax.random.uniform(key_scale, (K, 1, W), jnp.float32, jnp.log(0.14), jnp.log(0.28)))
    noise = jax.random.normal(key_noise, (K, W, W), jnp.float32)
    lower_part = noise * spread * (0.3 / W ** 0.5)
    result = jnp.where(rows_at == cols_at, spread, jnp.where(rows_at > cols_at, lower_part, 0.0))
    return result.astype(jnp.float32)


def draw_factor_off(key, part):
    key_noise = jax.random.fold_in(key, 29)
    sigma = 5.04 / FILL_ROWS ** 0.5
    values = jnp.clip(jax.random.normal(key_noise, (K, FILL_ROWS, W), jnp.float32) * sigma, -4.5 * sigma, 4.5 * sigma)
    return values.astype(jnp.float32)


def place_ends(values, rng, least, high):
    shape = values.shape
    index_at = [jax.random.randint(jax.random.fold_in(rng, axis), (), 0, shape[axis]) for axis in range(len(shape))]
    values = values.at[tuple(index_at)].set(least)
    longest = shape.index(max(shape))
    index_at[longest] = (index_at[longest] + 1) % shape[longest]
    return values.at[tuple(index_at)].set(high)


def different_ones(stream_key, rows, number_of, top, lift):
    order = jax.random.permutation(jax.random.fold_in(stream_key, 1), number_of)
    pull = order
    for power in range(3):
        pull = pull * pull // number_of
    pull = pull * lift // number_of
    lots = jax.random.randint(jax.random.fold_in(stream_key, 2), (rows, number_of), 0, 4096) + pull
    sure = jax.random.permutation(jax.random.fold_in(stream_key, 3), rows)[jnp.arange(number_of) % rows]
    lots = jnp.where(jnp.arange(rows)[:, None] == sure[None, :], 1 << 14, lots)
    score = lots * number_of + jnp.arange(number_of)
    return lax.top_k(score.astype(jnp.int32), top)[1].astype(jnp.int32)


def setup_inputs(seed: int = 0) -> dict:
    seeds = jax.random.split(jax.random.key(seed), 5)
    fill_blocks = different_ones(seeds[0], K, W // BLOCK, FILL, 0)
    fill_mask = place_ends((jax.random.randint(seeds[1], (K, FILL), 0, 8) < 7).astype(jnp.int32), jax.random.fold_in(seeds[1], 1), 0, 1)
    inv_diag = draw_inv_diag(jax.random.fold_in(seeds[4], 71), 0)
    factor_off = draw_factor_off(jax.random.fold_in(seeds[4], 71), 0)
    return {"fill_blocks": fill_blocks, "fill_mask": fill_mask, "inv_diag": inv_diag, "factor_off": factor_off}


def product(left, right):
    return jnp.dot(left, right, precision=lax.Precision.HIGHEST, preferred_element_type=jnp.float32)


def select_blocks(matrix, chosen_blocks):
    row_blocks = matrix.shape[0] // BLOCK
    col_blocks = matrix.shape[1] // BLOCK
    tiles = matrix.reshape(row_blocks, BLOCK, col_blocks, BLOCK)
    tiles = jnp.take(tiles, chosen_blocks, axis=0)
    tiles = jnp.take(tiles, chosen_blocks, axis=2)
    count = chosen_blocks.shape[0] * BLOCK
    return tiles.reshape(count, count)


def reference(fill_blocks, fill_mask, inv_diag, factor_off):
    panels = inv_diag.shape[0]
    slot_live = fill_mask.astype(jnp.float32)
    not_last = (jnp.arange(panels) < panels - 1).astype(jnp.float32)
    row_keep = jnp.repeat(slot_live * not_last[:, None], BLOCK, axis=1)
    slot_keep = jnp.repeat(slot_live, BLOCK, axis=1)
    before_fill = jnp.concatenate([fill_blocks[:1], fill_blocks[:-1]], 0)

    def advance(carried, inputs):
        inverse, factor, keep_rows, keep_slots, earlier_fill = inputs
        factor_map = product(factor * keep_rows[:, None], inverse)
        weighted = product(carried, factor_map)
        prior_term = product(inverse.T, inverse)
        covariance = prior_term + product(factor_map.T, weighted)
        cross_cov = -weighted * keep_slots[:, None]
        following = select_blocks(covariance, earlier_fill)
        return following, (covariance, cross_cov)

    starting = jnp.zeros((FILL_ROWS, FILL_ROWS), jnp.float32)
    finished, outputs = lax.scan(advance, starting, (inv_diag, factor_off, row_keep, slot_keep, before_fill), reverse=True)
    return outputs[0], outputs[1]
```

```python
import jax
import jax.numpy as jnp
from jax import lax
from jax.experimental import pallas as pl
from jax.experimental.pallas import tpu as pltpu
from jax.sharding import Mesh
from jax.sharding import PartitionSpec as P

BLOCK = 64
SEG = ("seg_0", "seg_1", "seg_2", "seg_3")
F32 = jnp.float32
BF16 = jnp.bfloat16
N_IDS = 100

ID_IDX = 0
ID_ZL = 1
ID_ZF = 13
ID_CL = 25
ID_CA = 26
ID_YL = 27
ID_YA = 39
ID_XL = 51
ID_XA = 63
ID_ZH = 75


def split(v):
    hi = v.astype(BF16)
    return hi, (v - hi.astype(F32)).astype(BF16)


def dot(a, b):
    return lax.dot_general(a, b, (((1,), (0,)), ((), ())), preferred_element_type=F32)


def mm(a, b):
    (ah, al), (bh, bl) = a, b
    return dot(ah, bh) + (dot(ah, bl) + dot(al, bh))


def sandwich(link, inner, added):
    left = mm(split(link.T), split(inner))
    return added + mm(split(left), split(link))


def kernel(
    blocks, mask, inv, fac, cov, off,
    idx_out, idx_in, inv_h, inv_l, lp, fg, base, cl, ca, yl, ya, xl, xa,
    el, ea, ph, th, pb, ss, rs,
):
    h, x, y, c = (lax.axis_index(a) for a in SEG)
    r = lax.axis_index("row")
    z = 4 * h + r
    seg = ((h * 4 + x) * 4 + y) * 2 + c

    def z_at(d):
        zz = lax.rem(z + d + 8, 8)
        return {"seg_0": zz // 4, "row": lax.rem(zz, 4)}

    def seg_at(d):
        s = lax.rem(seg + d + 64, 64)
        return {
            "seg_0": s // 32,
            "seg_1": lax.rem(s // 8, 4),
            "seg_2": lax.rem(s // 2, 4),
            "seg_3": lax.rem(s, 2),
        }

    def y_at(d):
        return {"seg_2": lax.rem(y + d + 4, 4)}

    def x_at(d):
        return {"seg_1": lax.rem(x + d + 4, 4)}

    mate = {"seg_3": 1 - c}

    barrier = pltpu.get_barrier_semaphore()
    greeted = (mate, z_at(1), z_at(-1), y_at(1), y_at(-1), x_at(1), x_at(-1), seg_at(1), seg_at(-1))
    for who in greeted:
        pl.semaphore_signal(barrier, 1, device_id=who, device_id_type=pl.DeviceIdType.MESH)

    started = []

    def copy(src, dst, number, who):
        return pltpu.make_async_remote_copy(
            src_ref=src, dst_ref=dst, send_sem=ss.at[number], recv_sem=rs.at[number],
            device_id=who, device_id_type=pl.DeviceIdType.MESH,
        )

    lane = lax.broadcasted_iota(jnp.int32, (8, 256), 1)
    slot = lane // BLOCK

    def targets(panel):
        t = jnp.zeros((8, 256), jnp.int32)
        for s in range(4):
            t = jnp.where(slot == s, blocks[panel, s], t)
        return t * BLOCK + (lane - slot * BLOCK)

    idx_out[...] = targets(1)
    target_1 = targets(0)

    row_at = lax.broadcasted_iota(jnp.int32, (512, 256), 0)

    def chooser(t):
        return jnp.where(row_at == t[0:1, :], 1.0, 0.0).astype(BF16)

    def keep(panel):
        live = mask[panel, r].astype(F32)
        return jnp.where(seg * 2 + panel < 127, live, 0.0)

    frows = [None, None]
    for p in (1, 0):
        ih, il = split(inv[p])
        inv_h[p] = ih
        inv_l[p] = il
        frows[p] = mm(split(fac[p] * keep(p)), (ih, il))
        fg[p, pl.ds(r * 64, 64), :] = frows[p]

    def local_link(p, choose):
        fh, fl = split(fg[p, pl.ds(r * 64, 64), :])
        lp[p, pl.ds(r * 64, 64), :] = dot(fh, choose) + dot(fl, choose)

    def local_base(p, choose):
        ch = dot(inv_h[p], choose)
        cl_ = dot(inv_l[p], choose)
        chh, cll = ch.astype(BF16), cl_.astype(BF16)
        cth, ctl = ch.T.astype(BF16), cl_.T.astype(BF16)
        base[p] = mm((cth, ctl), (chh, cll))

    choose_1 = chooser(target_1)
    local_link(1, choose_1)

    pl.semaphore_wait(barrier, 9)

    idx_copy = copy(idx_out, idx_in, ID_IDX, seg_at(1))
    idx_copy.start()
    started.append((None, idx_copy))

    def z_parts(buf, ids, p, k, up):
        block = (r - k) if up else (r + k)
        block_in = (r - 1 - k) if up else (r + 1 + k)
        sends = jnp.logical_and(r < 3, r - k >= 0) if up else jnp.logical_and(r > 0, r + k <= 3)
        takes = (r - 1 - k >= 0) if up else (r + 1 + k <= 3)
        number = ids + p * 6 + (0 if up else 3) + k
        who = z_at(1 if up else -1)

        def made(b):
            part = buf.at[p, pl.ds(b * 64, 64), :]
            return copy(part, part, number, who)

        return sends, takes, lambda: made(block), lambda: made(block_in)

    def z_send(buf, ids, p, k):
        for up in (True, False):
            sends, _, out, _ = z_parts(buf, ids, p, k, up)

            @pl.when(sends)
            def _():
                out().start()

            started.append((sends, out))

    def z_take(buf, ids, p, k):
        for up in (True, False):
            _, takes, _, into = z_parts(buf, ids, p, k, up)

            @pl.when(takes)
            def _():
                into().wait_recv()

    z_send(lp, ID_ZL, 1, 0)
    idx_copy.wait_recv()
    choose_0 = chooser(idx_in[...])
    local_link(0, choose_0)
    z_send(lp, ID_ZL, 0, 0)
    local_base(1, choose_1)
    local_base(0, choose_0)
    for k in range(3):
        for p in (1, 0):
            z_take(lp, ID_ZL, p, k)
            if k < 2:
                z_send(lp, ID_ZL, p, k + 1)
    for p in (1, 0):
        z_send(fg, ID_ZF, p, 0)

    link_0 = split(lp[0])
    cl[c] = mm(split(lp[1]), link_0)
    cl_copy = copy(cl.at[c], cl.at[c], ID_CL, mate)
    cl_copy.start()
    ca[c] = sandwich(lp[0], base[1], base[0])
    ca_copy = copy(ca.at[c], ca.at[c], ID_CA, mate)
    ca_copy.start()
    started.append((None, cl_copy))
    started.append((None, ca_copy))

    def half(j):
        return pl.ds(c * 128 + j * 64, 64)

    def ring_send(buf, ids, at, where):
        for step, (way, j) in enumerate(((0, 0), (1, 1), (0, 1), (1, 0))):
            part = buf.at[at, half(j), :]
            one = copy(part, part, ids + way * 2 + j, where(1 if way == 0 else -1))
            one.start()
            started.append((None, one))

    def ring_pass(buf, ids, at, where):
        def mated(place, j, number):
            part = buf.at[place, half(j), :]
            one = copy(part, part, number, mate)
            one.start()
            started.append((None, one))
            return one

        mates = []
        behind, ahead, across = (lax.rem(at + d, 4) for d in (3, 1, 2))
        for way, j in ((0, 0), (1, 1), (0, 1), (1, 0)):
            place = behind if way == 0 else ahead
            part = buf.at[place, half(j), :]
            copy(part, part, ids + way * 2 + j, where(1)).wait_recv()
            if way == j:
                onward = copy(part, part, ids + 4 + way, where(1 if way == 0 else -1))
                onward.start()
                started.append((None, onward))
            mates.append(mated(place, j, ids + 6 + way * 2 + j))
        for way in (0, 1):
            part = buf.at[across, half(way), :]
            copy(part, part, ids + 4 + way, where(1)).wait_recv()
            mates.append(mated(across, way, ids + 10 + way))
        for one in mates:
            one.wait_recv()

    def scan_links(buf, at, own, out):
        eye = lax.broadcasted_iota(jnp.int32, (256, 256), 0) == lax.broadcasted_iota(jnp.int32, (256, 256), 1)

        @pl.when(at == 3)
        def _():
            own[...] = eye.astype(F32)

        total = buf[3]
        for i in (2, 1, 0):

            @pl.when(at == i)
            def _():
                own[...] = total

            total = mm(split(total), split(buf[i]))
        if out is not None:
            out[0][out[1]] = total

    def scan_constants(links, buf, at, own):
        @pl.when(at == 3)
        def _():
            own[...] = jnp.zeros((256, 256), F32)

        total = buf[3]
        for i in (2, 1, 0):

            @pl.when(at == i)
            def _():
                own[...] = total

            total = sandwich(links[i], total, buf[i])
        return total

    cl_copy.wait_recv()
    yl[y] = mm(split(cl[1]), split(cl[0]))
    ring_send(yl, ID_YL, y, y_at)
    ca_copy.wait_recv()
    ya[y] = sandwich(cl[0], ca[1], ca[0])
    ring_send(ya, ID_YA, y, y_at)

    for p in (0, 1):
        mine = inv[p, :, pl.ds(pl.multiple_of(r * 128, 128), 128)]
        cov[p] = mm(split(mine.T), (inv_h[p], inv_l[p]))

    ring_pass(yl, ID_YL, y, y_at)
    scan_links(yl, y, el.at[0], (xl, x))
    ring_send(xl, ID_XL, x, x_at)
    for p in (1, 0):
        z_take(fg, ID_ZF, p, 0)
        z_send(fg, ID_ZF, p, 1)
    ring_pass(ya, ID_YA, y, y_at)
    xa[x] = scan_constants(yl, ya, y, ea.at[0])
    ring_send(xa, ID_XA, x, x_at)

    ring_pass(xl, ID_XL, x, x_at)
    scan_links(xl, x, el.at[1], None)
    for p in (1, 0):
        z_take(fg, ID_ZF, p, 1)
        z_send(fg, ID_ZF, p, 2)
    ring_pass(xa, ID_XA, x, x_at)
    th[...] = scan_constants(xl, xa, x, ea.at[1])

    edge = jnp.logical_or(r == 0, r == 3)
    hop = z_at(jnp.where(r == 0, -1, 1))
    inward = z_at(jnp.where(r == 0, 1, -1))

    def zh(j, kind):
        part = ph.at[half(j), :]
        if kind == 0:
            return copy(th.at[half(j), :], part, ID_ZH + j, hop)
        if kind == 1:
            return copy(part, part, ID_ZH + 2 + j, inward)
        return copy(part, part, ID_ZH + 4 + j, mate)

    later = h == 1

    @pl.when(jnp.logical_and(later, edge))
    def _():
        for j in (0, 1):
            zh(j, 0).start()

    link = mm(split(el[1]), split(el[0]))
    constant = sandwich(el[0], ea[1], ea[0])
    el[2] = link
    ea[2] = constant

    @pl.when(c == 0)
    def _():
        el[2] = mm(split(link), split(cl[1]))
        ea[2] = sandwich(cl[1], constant, ca[1])

    for p in (1, 0):
        z_take(fg, ID_ZF, p, 2)

    @pl.when(later)
    def _():
        pb[1] = ea[2]

    @pl.when(jnp.logical_and(h == 0, edge))
    def _():
        for j in (0, 1):
            zh(j, 0).wait_recv()
            zh(j, 1).start()
            zh(j, 2).start()

    @pl.when(jnp.logical_and(h == 0, jnp.logical_not(edge)))
    def _():
        for j in (0, 1):
            zh(j, 1).wait_recv()
            zh(j, 2).start()

    @pl.when(h == 0)
    def _():
        for j in (0, 1):
            zh(j, 2).wait_recv()
        pb[1] = sandwich(el[2], ph[...], ea[2])

    pb[0] = sandwich(lp[1], pb[1], base[1])

    for p in (1, 0):
        full = split(fg[p])
        mine = fg[p, :, pl.ds(pl.multiple_of(r * 128, 128), 128)]
        middle = mm(split(pb[p]), split(mine))
        cov[p] += mm(split(middle.T), full)
        rows = mm(split(pb[p, pl.ds(r * 64, 64), :]), full)
        off[p] = rows * (-mask[p, r].astype(F32))

    for sends, one in started:
        if sends is None:
            one.wait_send()
        else:

            @pl.when(sends)
            def _():
                one().wait_send()

    @pl.when(jnp.logical_and(later, edge))
    def _():
        for j in (0, 1):
            zh(j, 0).wait_send()

    @pl.when(jnp.logical_and(h == 0, edge))
    def _():
        for j in (0, 1):
            zh(j, 1).wait_send()

    @pl.when(h == 0)
    def _():
        for j in (0, 1):
            zh(j, 2).wait_send()


def body(fill_blocks, fill_mask, inv_diag, factor_off):
    vmem = pl.BlockSpec(memory_space=pltpu.VMEM)
    smem = pl.BlockSpec(memory_space=pltpu.SMEM)

    def sq(n):
        return pltpu.VMEM((n, 256, 256), F32)

    return pl.pallas_call(
        kernel,
        name="chain",
        out_shape=(
            jax.ShapeDtypeStruct((2, 128, 512), F32),
            jax.ShapeDtypeStruct((2, 64, 512), F32),
        ),
        in_specs=[smem, smem, vmem, vmem],
        out_specs=(vmem, vmem),
        scratch_shapes=[
            pltpu.VMEM((8, 256), jnp.int32),
            pltpu.VMEM((8, 256), jnp.int32),
            pltpu.VMEM((2, 512, 512), BF16),
            pltpu.VMEM((2, 512, 512), BF16),
            sq(2),
            pltpu.VMEM((2, 256, 512), F32),
            sq(2),
            sq(2),
            sq(2),
            sq(4),
            sq(4),
            sq(4),
            sq(4),
            sq(3),
            sq(3),
            pltpu.VMEM((256, 256), F32),
            pltpu.VMEM((256, 256), F32),
            sq(2),
            pltpu.SemaphoreType.DMA((N_IDS,)),
            pltpu.SemaphoreType.DMA((N_IDS,)),
        ],
        compiler_params=pltpu.CompilerParams(
            collective_id=0, has_side_effects=True, vmem_limit_bytes=48 << 20
        ),
    )(fill_blocks, fill_mask, inv_diag, factor_off)


def solution(mesh):
    torus = Mesh(mesh.devices.reshape(2, 4, 4, 2, mesh.shape["row"]), (*SEG, "row"))
    placed = (P(SEG, None), P(SEG, None), P(SEG, None, None), P(SEG, "row", None))
    return jax.shard_map(
        body,
        mesh=torus,
        in_specs=placed,
        out_specs=(P(SEG, "row", None), P(SEG, "row", None)),
        check_vma=False,
    )
```

```python
import jax
import jax.numpy as jnp
from jax import lax
from jax.experimental import pallas as pl
from jax.experimental.pallas import tpu as pltpu
from jax.sharding import Mesh
from jax.sharding import PartitionSpec as P

BLOCK = 64
SEG = ("seg_0", "seg_1", "seg_2", "seg_3")
F32 = jnp.float32
BF16 = jnp.bfloat16
N_IDS = 100

ID_IDX = 0
ID_ZL = 1
ID_ZF = 13
ID_CL = 25
ID_CA = 26
ID_YL = 27
ID_YA = 39
ID_XL = 51
ID_XA = 63
ID_RELAY = 99
ID_ZH = 75


def split(v):
    hi = v.astype(BF16)
    return hi, (v - hi.astype(F32)).astype(BF16)


def dot(a, b):
    return lax.dot_general(a, b, (((1,), (0,)), ((), ())), preferred_element_type=F32)


def mm(a, b):
    (ah, al), (bh, bl) = a, b
    return dot(ah, bh) + (dot(ah, bl) + dot(al, bh))


def sandwich(link, inner, added):
    left = mm(split(link.T), split(inner))
    return added + mm(split(left), split(link))


def kernel(
    blocks_hbm, mask_hbm, inv_hbm, fac_hbm, cov, off,
    blocks, mask, inv, fac, local, idx_out, idx_in, inv_h, inv_l, lp, fg, base, cl, ca, yl, ya, xl, xa,
    el, ea, ph, th, pb, rb, gg, kk, ss, rs,
):
    h, x, y, c = (lax.axis_index(a) for a in SEG)
    r = lax.axis_index("row")
    z = 4 * h + r
    seg = ((h * 4 + x) * 4 + y) * 2 + c

    def z_at(d):
        zz = lax.rem(z + d + 8, 8)
        return {"seg_0": zz // 4, "row": lax.rem(zz, 4)}

    def seg_at(d):
        s = lax.rem(seg + d + 64, 64)
        return {
            "seg_0": s // 32,
            "seg_1": lax.rem(s // 8, 4),
            "seg_2": lax.rem(s // 2, 4),
            "seg_3": lax.rem(s, 2),
        }

    def y_at(d):
        return {"seg_2": lax.rem(y + d + 4, 4)}

    def x_at(d):
        return {"seg_1": lax.rem(x + d + 4, 4)}

    mate = {"seg_3": 1 - c}

    barrier = pltpu.get_barrier_semaphore()

    def greet(who):
        pl.semaphore_signal(barrier, 1, device_id=who, device_id_type=pl.DeviceIdType.MESH)

    for who in (mate, z_at(1), z_at(-1), y_at(1), y_at(-1), x_at(1), x_at(-1)):
        greet(who)

    both = jnp.logical_and
    later = h == 1
    edge = jnp.logical_or(r == 0, r == 3)
    tail = both(both(x == 3, y == 3), c == 1)
    head = both(both(x == 0, y == 0), c == 0)
    plain_out, plain_in = jnp.logical_not(tail), jnp.logical_not(head)
    far_out = both(both(tail, h == 0), edge)
    far_in = both(both(head, later), edge)
    relay_in = both(both(head, later), jnp.logical_not(edge))
    across_half = {
        "seg_0": 1 - h, "seg_1": lax.rem(x + 1 + 2 * h, 4), "seg_2": lax.rem(y + 1 + 2 * h, 4),
        "seg_3": 1 - c, "row": 3 - r,
    }
    for cond, who in (
        (plain_out, seg_at(1)), (plain_in, seg_at(-1)), (far_out, across_half), (far_in, across_half),
    ):

        @pl.when(cond)
        def _():
            greet(who)

    greetings = 7
    for cond in (plain_out, plain_in, far_out, far_in):
        greetings = greetings + jnp.where(cond, 1, 0)

    loads = [
        pltpu.make_async_copy(src, dst, local.at[i])
        for i, (src, dst) in enumerate((
            (blocks_hbm, blocks), (mask_hbm, mask), (fac_hbm, fac),
            (inv_hbm.at[1], inv.at[1]), (inv_hbm.at[0], inv.at[0]),
        ))
    ]
    for load in loads:
        load.start()

    started = []

    def copy(src, dst, number, who):
        return pltpu.make_async_remote_copy(
            src_ref=src, dst_ref=dst, send_sem=ss.at[number], recv_sem=rs.at[number],
            device_id=who, device_id_type=pl.DeviceIdType.MESH,
        )

    for load in loads[:3]:
        load.wait()

    lane = lax.broadcasted_iota(jnp.int32, (8, 256), 1)
    slot = lane // BLOCK

    def targets(panel):
        t = jnp.zeros((8, 256), jnp.int32)
        for s in range(4):
            t = jnp.where(slot == s, blocks[panel, s], t)
        return t * BLOCK + (lane - slot * BLOCK)

    idx_out[...] = targets(1)
    target_1 = targets(0)

    row_at = lax.broadcasted_iota(jnp.int32, (512, 256), 0)

    def chooser(t):
        return jnp.where(row_at == t[0:1, :], 1.0, 0.0).astype(BF16)

    def keep(panel):
        live = mask[panel, r].astype(F32)
        return jnp.where(seg * 2 + panel < 127, live, 0.0)

    frows = [None, None]
    for p in (1, 0):
        loads[4 - p].wait()
        ih, il = split(inv[p])
        inv_h[p] = ih
        inv_l[p] = il
        frows[p] = mm(split(fac[p] * keep(p)), (ih, il))
        fg[p, pl.ds(r * 64, 64), :] = frows[p]

    def local_link(p, choose):
        fh, fl = split(fg[p, pl.ds(r * 64, 64), :])
        lp[p, pl.ds(r * 64, 64), :] = dot(fh, choose) + dot(fl, choose)

    def local_base(p, choose):
        ch = dot(inv_h[p], choose)
        cl_ = dot(inv_l[p], choose)
        chh, cll = ch.astype(BF16), cl_.astype(BF16)
        cth, ctl = ch.T.astype(BF16), cl_.T.astype(BF16)
        base[p] = mm((cth, ctl), (chh, cll))

    choose_1 = chooser(target_1)
    local_link(1, choose_1)

    pl.semaphore_wait(barrier, greetings)

    def begin(cond, made):
        @pl.when(cond)
        def _():
            made().start()

        started.append((cond, made))

    begin(plain_out, lambda: copy(idx_out, idx_in, ID_IDX, seg_at(1)))
    begin(far_out, lambda: copy(idx_out, idx_in, ID_IDX, across_half))
    inward = z_at(jnp.where(r == 0, 1, -1))
    relay = lambda: copy(idx_in, idx_in, ID_RELAY, inward)

    def z_parts(buf, ids, p, k, up):
        block = (r - k) if up else (r + k)
        block_in = (r - 1 - k) if up else (r + 1 + k)
        sends = jnp.logical_and(r < 3, r - k >= 0) if up else jnp.logical_and(r > 0, r + k <= 3)
        takes = (r - 1 - k >= 0) if up else (r + 1 + k <= 3)
        number = ids + p * 6 + (0 if up else 3) + k
        who = z_at(1 if up else -1)

        def made(b):
            part = buf.at[p, pl.ds(b * 64, 64), :]
            return copy(part, part, number, who)

        return sends, takes, lambda: made(block), lambda: made(block_in)

    def z_send(buf, ids, p, k):
        for up in (True, False):
            sends, _, out, _ = z_parts(buf, ids, p, k, up)

            @pl.when(sends)
            def _():
                out().start()

            started.append((sends, out))

    def z_take(buf, ids, p, k):
        for up in (True, False):
            _, takes, _, into = z_parts(buf, ids, p, k, up)

            @pl.when(takes)
            def _():
                into().wait_recv()

    z_send(lp, ID_ZL, 1, 0)
    local_base(1, choose_1)

    @pl.when(jnp.logical_or(plain_in, far_in))
    def _():
        copy(idx_out, idx_in, ID_IDX, mate).wait_recv()

    begin(far_in, relay)

    @pl.when(relay_in)
    def _():
        relay().wait_recv()

    @pl.when(both(head, h == 0))
    def _():
        idx_in[...] = target_1

    choose_0 = chooser(idx_in[...])
    local_link(0, choose_0)
    z_send(lp, ID_ZL, 0, 0)
    local_base(0, choose_0)
    for k in range(3):
        for p in (1, 0):
            z_take(lp, ID_ZL, p, k)
            if k < 2:
                z_send(lp, ID_ZL, p, k + 1)
        if k == 0:
            for p in (0, 1):
                mine = inv[p, :, pl.ds(pl.multiple_of(r * 128, 128), 128)]
                cov[p] = mm(split(mine.T), (inv_h[p], inv_l[p]))
    for p in (1, 0):
        z_send(fg, ID_ZF, p, 0)

    link_0 = split(lp[0])
    cl[c] = mm(split(lp[1]), link_0)
    cl_copy = copy(cl.at[c], cl.at[c], ID_CL, mate)
    cl_copy.start()
    ca[c] = sandwich(lp[0], base[1], base[0])
    ca_copy = copy(ca.at[c], ca.at[c], ID_CA, mate)
    ca_copy.start()
    started.append((None, cl_copy))
    started.append((None, ca_copy))

    turn = 1 - 2 * c

    def link_part(j):
        return pl.ds(c * 128 + j * 64, 64), slice(None)

    def constant_part(j):
        if j == 0:
            at = pl.ds(pl.multiple_of(c * 128, 128), 128)
            return at, at
        return pl.ds(c * 64, 64), pl.ds(128, 128)

    def ring_send(buf, ids, at, where, part):
        for way, j in ((0, 0), (1, 1), (0, 1), (1, 0)):
            piece = buf.at[at, *part(j)]
            one = copy(piece, piece, ids + way * 2 + j, where(turn if way == 0 else -turn))
            one.start()
            started.append((None, one))

    def places(at):
        return tuple(lax.rem(at + d + 4, 4) for d in (-turn, turn, 2))

    def mated(buf, place, j, number, part):
        piece = buf.at[place, *part(j)]
        one = copy(piece, piece, number, mate)
        one.start()
        started.append((None, one))
        return one

    def ring_pass(buf, ids, at, where, part):
        behind, ahead, across = places(at)
        mates = []
        for way, j in ((0, 0), (1, 1), (0, 1), (1, 0)):
            place = behind if way == 0 else ahead
            piece = buf.at[place, *part(j)]
            copy(piece, piece, ids + way * 2 + j, mate).wait_recv()
            if way == j:
                onward = copy(piece, piece, ids + 4 + way, where(turn if way == 0 else -turn))
                onward.start()
                started.append((None, onward))
            mates.append(mated(buf, place, j, ids + 6 + way * 2 + j, part))
        for one in mates:
            one.wait_recv()

    def ring_end(buf, ids, at, part):
        across = places(at)[2]
        mates = []
        for way in (0, 1):
            piece = buf.at[across, *part(way)]
            copy(piece, piece, ids + 4 + way, mate).wait_recv()
            mates.append(mated(buf, across, way, ids + 10 + way, part))
        return mates

    def done(mates):
        for one in mates:
            one.wait_recv()

    def whole(v):
        return jnp.concatenate([v[:128], jnp.concatenate([v[:128, 128:].T, v[128:, 128:]], 1)], 0)

    rows_256 = lax.broadcasted_iota(jnp.int32, (256, 256), 0)
    eye = (rows_256 == lax.broadcasted_iota(jnp.int32, (256, 256), 1)).astype(F32)

    def near_products(buf):
        rb[0] = eye
        rb[1] = buf[0]
        low = mm(split(buf[1]), split(buf[0]))
        rb[2] = low
        rb[3] = mm(split(buf[2]), split(low))

    def total_constant(buf, ring_mates, at):
        behind, ahead, across = places(at)
        total = jnp.zeros((256, 256), F32)
        for place in (at, behind, ahead):
            total = sandwich(rb[place], whole(buf[place]), total)
        done(ring_mates)
        return sandwich(rb[across], whole(buf[across]), total)

    def exclusive(links, consts, at, l_out, a_out):
        @pl.when(at == 3)
        def _():
            l_out[...] = eye
            a_out[...] = jnp.zeros((256, 256), F32)

        @pl.when(at < 3)
        def _():
            l_out[...] = links[3]
            a_out[...] = whole(consts[3])

        for i in (2, 1):

            @pl.when(at < i)
            def _():
                a_out[...] = sandwich(links[i], a_out[...], whole(consts[i]))
                l_out[...] = mm(split(l_out[...]), split(links[i]))

    cl_copy.wait_recv()
    yl[y] = mm(split(cl[1]), split(cl[0]))
    ring_send(yl, ID_YL, y, y_at, link_part)
    ca_copy.wait_recv()
    ya[y] = sandwich(cl[0], ca[1], ca[0])
    ring_send(ya, ID_YA, y, y_at, constant_part)

    ring_pass(yl, ID_YL, y, y_at, link_part)
    done(ring_end(yl, ID_YL, y, link_part))
    high = mm(split(yl[3]), split(yl[2]))
    low = mm(split(yl[1]), split(yl[0]))
    xl[x] = mm(split(high), split(low))
    ring_send(xl, ID_XL, x, x_at, link_part)
    near_products(yl)
    for p in (1, 0):
        z_take(fg, ID_ZF, p, 0)
        z_send(fg, ID_ZF, p, 1)
    ring_pass(ya, ID_YA, y, y_at, constant_part)
    xa[x] = total_constant(ya, ring_end(ya, ID_YA, y, constant_part), y)
    ring_send(xa, ID_XA, x, x_at, constant_part)

    ring_pass(xl, ID_XL, x, x_at, link_part)

    exclusive(yl, ya, y, el.at[1], ea.at[1])

    @pl.when(c == 0)
    def _():
        ea[1] = sandwich(cl[1], ea[1], ca[1])
        el[1] = mm(split(el[1]), split(cl[1]))

    ea[0] = sandwich(lp[1], ea[1], base[1])
    el[0] = mm(split(el[1]), split(lp[1]))

    done(ring_end(xl, ID_XL, x, link_part))
    for p in (1, 0):
        z_take(fg, ID_ZF, p, 1)
        z_send(fg, ID_ZF, p, 2)
    near_products(xl)
    ring_pass(xa, ID_XA, x, x_at, constant_part)

    hop = z_at(jnp.where(r == 0, -1, 1))

    def zh(j, kind):
        piece = ph.at[*constant_part(j)]
        if kind == 0:
            return copy(th.at[*constant_part(j)], piece, ID_ZH + j, hop)
        if kind == 1:
            return copy(piece, piece, ID_ZH + 2 + j, inward)
        return copy(piece, piece, ID_ZH + 4 + j, mate)

    sends_half = both(later, edge)
    xa_mates = ring_end(xa, ID_XA, x, constant_part)

    @pl.when(sends_half)
    def _():
        th[...] = total_constant(xa, xa_mates, x)
        for j in (0, 1):
            zh(j, 0).start()

    @pl.when(jnp.logical_not(sends_half))
    def _():
        done(xa_mates)

    for p in (1, 0):
        z_take(fg, ID_ZF, p, 2)
    exclusive(xl, xa, x, el.at[2], ea.at[2])
    for p in (1, 0):
        l_in = split(el[p])
        constant = sandwich(el[p], ea[2], ea[p])
        full = split(fg[p])
        mine = fg[p, :, pl.ds(pl.multiple_of(r * 128, 128), 128)]
        middle = mm(split(constant), split(mine))
        pb[...] = constant
        left = jnp.concatenate([middle.T, pb[pl.ds(r * 64, 64), :]], 0)
        out = mm(split(left), full)
        cov[p] += out[:128]
        off[p] = out[128:]

        @pl.when(h == 0)
        def _():
            link = mm(split(el[2]), l_in)
            pb[...] = link.T
            gg[p] = mm(split(link), full)
            kk[p * 192 : p * 192 + 128, :] = gg[p, :, pl.ds(pl.multiple_of(r * 128, 128), 128)].T
            kk[p * 192 + 128 : p * 192 + 192, :] = pb[pl.ds(r * 64, 64), :]

    @pl.when(both(h == 0, edge))
    def _():
        for j in (0, 1):
            zh(j, 0).wait_recv()
            zh(j, 1).start()
            zh(j, 2).start()

    @pl.when(both(h == 0, jnp.logical_not(edge)))
    def _():
        for j in (0, 1):
            zh(j, 1).wait_recv()
            zh(j, 2).start()

    @pl.when(h == 0)
    def _():
        for j in (0, 1):
            zh(j, 2).wait_recv()
        left = split(mm(split(kk[...]), split(whole(ph[...]))))
        for p in (0, 1):
            at = slice(p * 192, p * 192 + 192)
            out = mm((left[0][at], left[1][at]), split(gg[p]))
            cov[p] += out[:128]
            off[p] += out[128:]

    for p in (0, 1):
        off[p] = off[p] * (-mask[p, r].astype(F32))

    for sends, one in started:
        if sends is None:
            one.wait_send()
        else:

            @pl.when(sends)
            def _():
                one().wait_send()

    @pl.when(sends_half)
    def _():
        for j in (0, 1):
            zh(j, 0).wait_send()

    @pl.when(jnp.logical_and(h == 0, edge))
    def _():
        for j in (0, 1):
            zh(j, 1).wait_send()

    @pl.when(h == 0)
    def _():
        for j in (0, 1):
            zh(j, 2).wait_send()


def body(fill_blocks, fill_mask, inv_diag, factor_off):
    vmem = pl.BlockSpec(memory_space=pltpu.VMEM)

    def sq(n):
        return pltpu.VMEM((n, 256, 256), F32)

    return pl.pallas_call(
        kernel,
        name="chain",
        out_shape=(
            jax.ShapeDtypeStruct((2, 128, 512), F32),
            jax.ShapeDtypeStruct((2, 64, 512), F32),
        ),
        in_specs=[pl.BlockSpec(memory_space=pl.ANY)] * 4,
        out_specs=(vmem, vmem),
        scratch_shapes=[
            pltpu.SMEM((2, 4), jnp.int32),
            pltpu.SMEM((2, 4), jnp.int32),
            pltpu.VMEM((2, 512, 512), F32),
            pltpu.VMEM((2, 64, 512), F32),
            pltpu.SemaphoreType.DMA((5,)),
            pltpu.VMEM((8, 256), jnp.int32),
            pltpu.VMEM((8, 256), jnp.int32),
            pltpu.VMEM((2, 512, 512), BF16),
            pltpu.VMEM((2, 512, 512), BF16),
            sq(2),
            pltpu.VMEM((2, 256, 512), F32),
            sq(2),
            sq(2),
            sq(2),
            sq(4),
            sq(4),
            sq(4),
            sq(4),
            sq(3),
            sq(3),
            pltpu.VMEM((256, 256), F32),
            pltpu.VMEM((256, 256), F32),
            pltpu.VMEM((256, 256), F32),
            sq(4),
            pltpu.VMEM((2, 256, 512), F32),
            pltpu.VMEM((384, 256), F32),
            pltpu.SemaphoreType.DMA((N_IDS,)),
            pltpu.SemaphoreType.DMA((N_IDS,)),
        ],
        compiler_params=pltpu.CompilerParams(
            collective_id=0, has_side_effects=True
        ),
    )(fill_blocks, fill_mask, inv_diag, factor_off)


def solution(mesh):
    torus = Mesh(mesh.devices.reshape(2, 4, 4, 2, mesh.shape["row"]), (*SEG, "row"))
    placed = (P(SEG, None), P(SEG, None), P(SEG, None, None), P(SEG, "row", None))
    return jax.shard_map(
        body,
        mesh=torus,
        in_specs=placed,
        out_specs=(P(SEG, "row", None), P(SEG, "row", None)),
        check_vma=False,
    )
```

```python
import jax
import jax.numpy as jnp
from jax import lax
from jax.experimental import pallas as pl
from jax.experimental.pallas import tpu as pltpu
from jax.sharding import Mesh
from jax.sharding import PartitionSpec as P

BLOCK = 64
SEG = ("seg_0", "seg_1", "seg_2", "seg_3")
F32 = jnp.float32
BF16 = jnp.bfloat16
N_IDS = 100

ID_IDX = 0
ID_ZL = 1
ID_ZF = 13
ID_CL = 25
ID_CA = 26
ID_YL = 27
ID_YA = 39
ID_XL = 51
ID_XA = 63
ID_RELAY = 99
ID_ZH = 75


def split(v):
    hi = v.astype(BF16)
    return hi, (v - hi.astype(F32)).astype(BF16)


def dot(a, b):
    return lax.dot_general(a, b, (((1,), (0,)), ((), ())), preferred_element_type=F32)


def mm(a, b):
    (ah, al), (bh, bl) = a, b
    return dot(ah, bh) + (dot(ah, bl) + dot(al, bh))


def sandwich(link, inner, added):
    left = mm(split(link.T), split(inner))
    return added + mm(split(left), split(link))


def kernel(
    blocks_hbm, mask_hbm, inv_hbm, fac_hbm, cov, off,
    blocks, mask, inv, fac, local, idx_out, idx_in, inv_h, inv_l, lp, fg, base, cl, ca, yl, ya, xl, xa,
    el, ea, ph, th, pb, rb, gg, kk, ss, rs,
):
    h, x, y, c = (lax.axis_index(a) for a in SEG)
    r = lax.axis_index("row")
    z = 4 * h + r
    seg = ((h * 4 + x) * 4 + y) * 2 + c

    def z_at(d):
        zz = lax.rem(z + d + 8, 8)
        return {"seg_0": zz // 4, "row": lax.rem(zz, 4)}

    def seg_at(d):
        s = lax.rem(seg + d + 64, 64)
        return {
            "seg_0": s // 32,
            "seg_1": lax.rem(s // 8, 4),
            "seg_2": lax.rem(s // 2, 4),
            "seg_3": lax.rem(s, 2),
        }

    def y_at(d):
        return {"seg_2": lax.rem(y + d + 4, 4)}

    def x_at(d):
        return {"seg_1": lax.rem(x + d + 4, 4)}

    mate = {"seg_3": 1 - c}

    barrier = pltpu.get_barrier_semaphore()

    def greet(who):
        pl.semaphore_signal(barrier, 1, device_id=who, device_id_type=pl.DeviceIdType.MESH)

    for who in (mate, z_at(1), z_at(-1), y_at(1), y_at(-1), x_at(1), x_at(-1)):
        greet(who)

    both = jnp.logical_and
    later = h == 1
    edge = jnp.logical_or(r == 0, r == 3)
    tail = both(both(x == 3, y == 3), c == 1)
    head = both(both(x == 0, y == 0), c == 0)
    plain_out, plain_in = jnp.logical_not(tail), jnp.logical_not(head)
    far_out = both(both(tail, h == 0), edge)
    far_in = both(both(head, later), edge)
    relay_in = both(both(head, later), jnp.logical_not(edge))
    across_half = {
        "seg_0": 1 - h, "seg_1": lax.rem(x + 1 + 2 * h, 4), "seg_2": lax.rem(y + 1 + 2 * h, 4),
        "seg_3": 1 - c, "row": 3 - r,
    }
    for cond, who in (
        (plain_out, seg_at(1)), (plain_in, seg_at(-1)), (far_out, across_half), (far_in, across_half),
    ):

        @pl.when(cond)
        def _():
            greet(who)

    greetings = 7
    for cond in (plain_out, plain_in, far_out, far_in):
        greetings = greetings + jnp.where(cond, 1, 0)

    loads = [
        pltpu.make_async_copy(src, dst, local.at[i])
        for i, (src, dst) in enumerate((
            (blocks_hbm, blocks), (mask_hbm, mask), (fac_hbm, fac),
            (inv_hbm.at[1], inv.at[1]), (inv_hbm.at[0], inv.at[0]),
        ))
    ]
    for load in loads:
        load.start()

    started = []

    def copy(src, dst, number, who):
        return pltpu.make_async_remote_copy(
            src_ref=src, dst_ref=dst, send_sem=ss.at[number], recv_sem=rs.at[number],
            device_id=who, device_id_type=pl.DeviceIdType.MESH,
        )

    for load in loads[:3]:
        load.wait()

    lane = lax.broadcasted_iota(jnp.int32, (8, 256), 1)
    slot = lane // BLOCK

    def targets(panel):
        t = jnp.zeros((8, 256), jnp.int32)
        for s in range(4):
            t = jnp.where(slot == s, blocks[panel, s], t)
        return t * BLOCK + (lane - slot * BLOCK)

    idx_out[...] = targets(1)
    target_1 = targets(0)

    row_at = lax.broadcasted_iota(jnp.int32, (512, 256), 0)

    def chooser(t):
        return jnp.where(row_at == t[0:1, :], 1.0, 0.0).astype(BF16)

    def keep(panel):
        live = mask[panel, r].astype(F32)
        return jnp.where(seg * 2 + panel < 127, live, 0.0)

    frows = [None, None]
    for p in (1, 0):
        loads[4 - p].wait()
        ih, il = split(inv[p])
        inv_h[p] = ih
        inv_l[p] = il
        frows[p] = mm(split(fac[p] * keep(p)), (ih, il))
        fg[p, pl.ds(r * 64, 64), :] = frows[p]

    def local_link(p, choose):
        fh, fl = split(fg[p, pl.ds(r * 64, 64), :])
        lp[p, pl.ds(r * 64, 64), :] = dot(fh, choose) + dot(fl, choose)

    def local_base(p, choose):
        ch = dot(inv_h[p], choose)
        cl_ = dot(inv_l[p], choose)
        chh, cll = ch.astype(BF16), cl_.astype(BF16)
        cth, ctl = ch.T.astype(BF16), cl_.T.astype(BF16)
        base[p] = mm((cth, ctl), (chh, cll))

    choose_1 = chooser(target_1)
    local_link(1, choose_1)

    pl.semaphore_wait(barrier, greetings)

    def begin(cond, made):
        @pl.when(cond)
        def _():
            made().start()

        started.append((cond, made))

    begin(plain_out, lambda: copy(idx_out, idx_in, ID_IDX, seg_at(1)))
    begin(far_out, lambda: copy(idx_out, idx_in, ID_IDX, across_half))
    inward = z_at(jnp.where(r == 0, 1, -1))
    relay = lambda: copy(idx_in, idx_in, ID_RELAY, inward)

    def z_parts(buf, ids, p, k, up):
        block = (r - k) if up else (r + k)
        block_in = (r - 1 - k) if up else (r + 1 + k)
        sends = jnp.logical_and(r < 3, r - k >= 0) if up else jnp.logical_and(r > 0, r + k <= 3)
        takes = (r - 1 - k >= 0) if up else (r + 1 + k <= 3)
        number = ids + p * 6 + (0 if up else 3) + k
        who = z_at(1 if up else -1)

        def made(b):
            part = buf.at[p, pl.ds(b * 64, 64), :]
            return copy(part, part, number, who)

        return sends, takes, lambda: made(block), lambda: made(block_in)

    def z_send(buf, ids, p, k):
        for up in (True, False):
            sends, _, out, _ = z_parts(buf, ids, p, k, up)

            @pl.when(sends)
            def _():
                out().start()

            started.append((sends, out))

    def z_take(buf, ids, p, k):
        for up in (True, False):
            _, takes, _, into = z_parts(buf, ids, p, k, up)

            @pl.when(takes)
            def _():
                into().wait_recv()

    def z_next(buf, ids, p, k):
        z_take(buf, ids, p, k)
        if k < 2:
            z_send(buf, ids, p, k + 1)

    z_send(lp, ID_ZL, 1, 0)
    local_base(1, choose_1)
    z_next(lp, ID_ZL, 1, 0)

    @pl.when(jnp.logical_or(plain_in, far_in))
    def _():
        copy(idx_out, idx_in, ID_IDX, mate).wait_recv()

    begin(far_in, relay)

    @pl.when(relay_in)
    def _():
        relay().wait_recv()

    @pl.when(both(head, h == 0))
    def _():
        idx_in[...] = target_1

    choose_0 = chooser(idx_in[...])
    local_link(0, choose_0)
    z_send(lp, ID_ZL, 0, 0)
    local_base(0, choose_0)
    z_next(lp, ID_ZL, 1, 1)
    z_next(lp, ID_ZL, 0, 0)
    for p in (0, 1):
        mine = inv[p, :, pl.ds(pl.multiple_of(r * 128, 128), 128)]
        cov[p] = mm(split(mine.T), (inv_h[p], inv_l[p]))
    z_next(lp, ID_ZL, 0, 1)
    z_next(lp, ID_ZL, 1, 2)
    z_next(lp, ID_ZL, 0, 2)
    for p in (1, 0):
        z_send(fg, ID_ZF, p, 0)

    link_0 = split(lp[0])
    cl[c] = mm(split(lp[1]), link_0)
    cl_copy = copy(cl.at[c], cl.at[c], ID_CL, mate)
    cl_copy.start()
    ca[c] = sandwich(lp[0], base[1], base[0])
    ca_copy = copy(ca.at[c], ca.at[c], ID_CA, mate)
    ca_copy.start()
    started.append((None, cl_copy))
    started.append((None, ca_copy))

    turn = 1 - 2 * c

    def link_part(j):
        return pl.ds(c * 128 + j * 64, 64), slice(None)

    def constant_part(j):
        if j == 0:
            at = pl.ds(pl.multiple_of(c * 128, 128), 128)
            return at, at
        return pl.ds(c * 64, 64), pl.ds(128, 128)

    def ring_send(buf, ids, at, where, part):
        for way, j in ((0, 0), (1, 1), (0, 1), (1, 0)):
            piece = buf.at[at, *part(j)]
            one = copy(piece, piece, ids + way * 2 + j, where(turn if way == 0 else -turn))
            one.start()
            started.append((None, one))

    def places(at):
        return tuple(lax.rem(at + d + 4, 4) for d in (-turn, turn, 2))

    def mated(buf, place, j, number, part):
        piece = buf.at[place, *part(j)]
        one = copy(piece, piece, number, mate)
        one.start()
        started.append((None, one))
        return one

    def direct(buf, ids, at, where, part):
        behind, ahead, _ = places(at)
        mates = []
        for way, j in ((0, 0), (1, 1), (0, 1), (1, 0)):
            place = behind if way == 0 else ahead
            piece = buf.at[place, *part(j)]
            copy(piece, piece, ids + way * 2 + j, mate).wait_recv()
            if way == j:
                onward = copy(piece, piece, ids + 4 + way, where(turn if way == 0 else -turn))
                onward.start()
                started.append((None, onward))
            mates.append(mated(buf, place, j, ids + 6 + way * 2 + j, part))
        return mates

    def opposite(buf, ids, at, part):
        across = places(at)[2]
        mates = []
        for way in (0, 1):
            piece = buf.at[across, *part(way)]
            copy(piece, piece, ids + 4 + way, mate).wait_recv()
            mates.append(mated(buf, across, way, ids + 10 + way, part))
        return mates

    def done(mates):
        for one in mates:
            one.wait_recv()

    def whole(v):
        return jnp.concatenate([v[:128], jnp.concatenate([v[:128, 128:].T, v[128:, 128:]], 1)], 0)

    rows_256 = lax.broadcasted_iota(jnp.int32, (256, 256), 0)
    eye = (rows_256 == lax.broadcasted_iota(jnp.int32, (256, 256), 1)).astype(F32)

    def near_products(buf):
        rb[0] = eye
        rb[1] = buf[0]
        low = mm(split(buf[1]), split(buf[0]))
        rb[2] = low
        rb[3] = mm(split(buf[2]), split(low))

    def term(buf, place, added):
        return sandwich(rb[place], whole(buf[place]), added)

    def exclusive_links(links, at, out):
        @pl.when(at == 3)
        def _():
            out[...] = eye

        @pl.when(at < 3)
        def _():
            out[...] = links[3]

        for i in (2, 1):

            @pl.when(at < i)
            def _():
                out[...] = mm(split(out[...]), split(links[i]))

    def exclusive_constants(links, consts, at, out):
        @pl.when(at == 3)
        def _():
            out[...] = jnp.zeros((256, 256), F32)

        @pl.when(at < 3)
        def _():
            out[...] = whole(consts[3])

        for i in (2, 1):

            @pl.when(at < i)
            def _():
                out[...] = sandwich(links[i], out[...], whole(consts[i]))

    cl_copy.wait_recv()
    yl[y] = mm(split(cl[1]), split(cl[0]))
    ring_send(yl, ID_YL, y, y_at, link_part)
    ca_copy.wait_recv()
    ya[y] = sandwich(cl[0], ca[1], ca[0])
    ring_send(ya, ID_YA, y, y_at, constant_part)

    yl_mates = direct(yl, ID_YL, y, y_at, link_part)
    z_next(fg, ID_ZF, 1, 0)
    z_next(fg, ID_ZF, 0, 0)
    ya_mates = direct(ya, ID_YA, y, y_at, constant_part)
    done(yl_mates + opposite(yl, ID_YL, y, link_part))
    high = mm(split(yl[3]), split(yl[2]))
    low = mm(split(yl[1]), split(yl[0]))
    xl[x] = mm(split(high), split(low))
    ring_send(xl, ID_XL, x, x_at, link_part)
    z_next(fg, ID_ZF, 1, 1)
    near_products(yl)
    done(ya_mates)
    behind, ahead, across = places(y)
    total = term(ya, ahead, term(ya, y, jnp.zeros((256, 256), F32)))
    ya_mates = opposite(ya, ID_YA, y, constant_part)
    total = term(ya, behind, total)
    done(ya_mates)
    xa[x] = term(ya, across, total)
    ring_send(xa, ID_XA, x, x_at, constant_part)

    z_next(fg, ID_ZF, 0, 1)
    exclusive_links(yl, y, el.at[1])
    exclusive_constants(yl, ya, y, ea.at[1])
    xl_mates = direct(xl, ID_XL, x, x_at, link_part)

    @pl.when(c == 0)
    def _():
        ea[1] = sandwich(cl[1], ea[1], ca[1])
        el[1] = mm(split(el[1]), split(cl[1]))

    ea[0] = sandwich(lp[1], ea[1], base[1])
    el[0] = mm(split(el[1]), split(lp[1]))

    xa_mates = direct(xa, ID_XA, x, x_at, constant_part)
    done(xl_mates + opposite(xl, ID_XL, x, link_part))
    sends_half = both(later, edge)
    behind, ahead, across = places(x)
    z_next(fg, ID_ZF, 1, 2)
    z_next(fg, ID_ZF, 0, 2)
    done(xa_mates)

    @pl.when(sends_half)
    def _():
        near_products(xl)
        zero = jnp.zeros((256, 256), F32)
        th[...] = term(xa, behind, term(xa, ahead, term(xa, x, zero)))

    @pl.when(h == 0)
    def _():
        exclusive_links(xl, x, el.at[2])
        entry = split(el[2])
        for p in (1, 0):
            link = mm(entry, split(el[p]))
            pb[...] = link.T
            gg[p] = mm(split(link), split(fg[p]))
            kk[p * 192 : p * 192 + 128, :] = gg[p, :, pl.ds(pl.multiple_of(r * 128, 128), 128)].T
            kk[p * 192 + 128 : p * 192 + 192, :] = pb[pl.ds(r * 64, 64), :]

    done(opposite(xa, ID_XA, x, constant_part))

    hop = z_at(jnp.where(r == 0, -1, 1))

    def zh(j, kind):
        piece = ph.at[*constant_part(j)]
        if kind == 0:
            return copy(th.at[*constant_part(j)], piece, ID_ZH + j, hop)
        if kind == 1:
            return copy(piece, piece, ID_ZH + 2 + j, inward)
        return copy(piece, piece, ID_ZH + 4 + j, mate)

    @pl.when(sends_half)
    def _():
        th[...] = term(xa, across, th[...])
        for j in (0, 1):
            zh(j, 0).start()

    exclusive_constants(xl, xa, x, ea.at[2])

    def outputs(p):
        constant = sandwich(el[p], ea[2], ea[p])
        mine = fg[p, :, pl.ds(pl.multiple_of(r * 128, 128), 128)]
        middle = mm(split(constant), split(mine))
        pb[...] = constant
        left = jnp.concatenate([middle.T, pb[pl.ds(r * 64, 64), :]], 0)
        out = mm(split(left), split(fg[p]))
        cov[p] += out[:128]
        off[p] = out[128:]

    outputs(1)

    @pl.when(both(h == 0, edge))
    def _():
        for j in (0, 1):
            zh(j, 0).wait_recv()
            zh(j, 1).start()
            zh(j, 2).start()

    outputs(0)

    @pl.when(both(h == 0, jnp.logical_not(edge)))
    def _():
        for j in (0, 1):
            zh(j, 1).wait_recv()
            zh(j, 2).start()

    @pl.when(h == 0)
    def _():
        for j in (0, 1):
            zh(j, 2).wait_recv()
        left = split(mm(split(kk[...]), split(whole(ph[...]))))
        for p in (0, 1):
            at = slice(p * 192, p * 192 + 192)
            out = mm((left[0][at], left[1][at]), split(gg[p]))
            cov[p] += out[:128]
            off[p] += out[128:]

    for p in (0, 1):
        off[p] = off[p] * (-mask[p, r].astype(F32))

    for sends, one in started:
        if sends is None:
            one.wait_send()
        else:

            @pl.when(sends)
            def _():
                one().wait_send()

    @pl.when(sends_half)
    def _():
        for j in (0, 1):
            zh(j, 0).wait_send()

    @pl.when(jnp.logical_and(h == 0, edge))
    def _():
        for j in (0, 1):
            zh(j, 1).wait_send()

    @pl.when(h == 0)
    def _():
        for j in (0, 1):
            zh(j, 2).wait_send()


def body(fill_blocks, fill_mask, inv_diag, factor_off):
    vmem = pl.BlockSpec(memory_space=pltpu.VMEM)

    def sq(n):
        return pltpu.VMEM((n, 256, 256), F32)

    return pl.pallas_call(
        kernel,
        name="chain",
        out_shape=(
            jax.ShapeDtypeStruct((2, 128, 512), F32),
            jax.ShapeDtypeStruct((2, 64, 512), F32),
        ),
        in_specs=[pl.BlockSpec(memory_space=pl.ANY)] * 4,
        out_specs=(vmem, vmem),
        scratch_shapes=[
            pltpu.SMEM((2, 4), jnp.int32),
            pltpu.SMEM((2, 4), jnp.int32),
            pltpu.VMEM((2, 512, 512), F32),
            pltpu.VMEM((2, 64, 512), F32),
            pltpu.SemaphoreType.DMA((5,)),
            pltpu.VMEM((8, 256), jnp.int32),
            pltpu.VMEM((8, 256), jnp.int32),
            pltpu.VMEM((2, 512, 512), BF16),
            pltpu.VMEM((2, 512, 512), BF16),
            sq(2),
            pltpu.VMEM((2, 256, 512), F32),
            sq(2),
            sq(2),
            sq(2),
            sq(4),
            sq(4),
            sq(4),
            sq(4),
            sq(3),
            sq(3),
            pltpu.VMEM((256, 256), F32),
            pltpu.VMEM((256, 256), F32),
            pltpu.VMEM((256, 256), F32),
            sq(4),
            pltpu.VMEM((2, 256, 512), F32),
            pltpu.VMEM((384, 256), F32),
            pltpu.SemaphoreType.DMA((N_IDS,)),
            pltpu.SemaphoreType.DMA((N_IDS,)),
        ],
        compiler_params=pltpu.CompilerParams(
            collective_id=0, has_side_effects=True
        ),
    )(fill_blocks, fill_mask, inv_diag, factor_off)


def solution(mesh):
    torus = Mesh(mesh.devices.reshape(2, 4, 4, 2, mesh.shape["row"]), (*SEG, "row"))
    placed = (P(SEG, None), P(SEG, None), P(SEG, None, None), P(SEG, "row", None))
    return jax.shard_map(
        body,
        mesh=torus,
        in_specs=placed,
        out_specs=(P(SEG, "row", None), P(SEG, "row", None)),
        check_vma=False,
    )
```

```python
import jax
import jax.numpy as jnp
from jax import lax
from jax.experimental import pallas as pl
from jax.experimental.pallas import tpu as pltpu
from jax.sharding import Mesh
from jax.sharding import PartitionSpec as P

BLOCK = 64
SEG = ("seg_0", "seg_1", "seg_2", "seg_3")
F32 = jnp.float32
BF16 = jnp.bfloat16
N_IDS = 100

ID_IDX = 0
ID_ZL = 1
ID_ZF = 13
ID_CL = 25
ID_CA = 26
ID_YL = 27
ID_YA = 39
ID_XL = 51
ID_XA = 63
ID_ZL_LATE = 84
ID_RELAY = 99
ID_ZH = 75


def split(v):
    hi = v.astype(BF16)
    return hi, (v - hi.astype(F32)).astype(BF16)


def dot(a, b):
    return lax.dot_general(a, b, (((1,), (0,)), ((), ())), preferred_element_type=F32)


def mm(a, b):
    (ah, al), (bh, bl) = a, b
    return dot(ah, bh) + (dot(ah, bl) + dot(al, bh))


def sandwich(link, inner, added):
    left = mm(split(link.T), split(inner))
    return added + mm(split(left), split(link))


def kernel(
    blocks_hbm, mask_hbm, inv_hbm, fac_hbm, cov, off,
    blocks, mask, inv, fac, local, idx_out, idx_in, inv_h, inv_l, lp, fg, base, cl, ca, yl, ya, xl, xa,
    el, ea, ph, th, pb, rb, sm, gg, kk, ss, rs,
):
    h, x, y, c = (lax.axis_index(a) for a in SEG)
    r = lax.axis_index("row")
    z = 4 * h + r
    seg = ((h * 4 + x) * 4 + y) * 2 + c

    both = jnp.logical_and

    def z_at(d):
        zz = lax.rem(z + d + 8, 8)
        return {"seg_0": zz // 4, "row": lax.rem(zz, 4)}

    def seg_at(d):
        s = lax.rem(seg + d + 64, 64)
        return {
            "seg_0": s // 32,
            "seg_1": lax.rem(s // 8, 4),
            "seg_2": lax.rem(s // 2, 4),
            "seg_3": lax.rem(s, 2),
        }

    def y_at(d):
        return {"seg_2": lax.rem(y + d + 4, 4)}

    def x_at(d):
        return {"seg_1": lax.rem(x + d + 4, 4)}

    mate = {"seg_3": 1 - c}

    barrier = pltpu.get_barrier_semaphore()

    def greet(who):
        pl.semaphore_signal(barrier, 1, device_id=who, device_id_type=pl.DeviceIdType.MESH)

    for who in (mate, z_at(1), z_at(-1), y_at(1), y_at(-1), x_at(1), x_at(-1)):
        greet(who)

    later = h == 1
    edge = jnp.logical_or(r == 0, r == 3)
    tail = both(both(x == 3, y == 3), c == 1)
    head = both(both(x == 0, y == 0), c == 0)
    plain_out, plain_in = jnp.logical_not(tail), jnp.logical_not(head)
    far_out = both(both(tail, h == 0), edge)
    far_in = both(both(head, later), edge)
    relay_in = both(both(head, later), jnp.logical_not(edge))
    across_half = {
        "seg_0": 1 - h, "seg_1": lax.rem(x + 1 + 2 * h, 4), "seg_2": lax.rem(y + 1 + 2 * h, 4),
        "seg_3": 1 - c, "row": 3 - r,
    }
    for cond, who in (
        (plain_in, seg_at(-1)), (far_in, across_half),
    ):

        @pl.when(cond)
        def _():
            greet(who)

    greetings = 7
    for cond in (plain_out, far_out):
        greetings = greetings + jnp.where(cond, 1, 0)

    loads = [
        pltpu.make_async_copy(src, dst, local.at[i])
        for i, (src, dst) in enumerate((
            (blocks_hbm, blocks), (mask_hbm, mask), (fac_hbm, fac),
            (inv_hbm.at[1], inv.at[1]), (inv_hbm.at[0], inv.at[0]),
        ))
    ]
    for load in loads:
        load.start()

    started = []

    def copy(src, dst, number, who):
        return pltpu.make_async_remote_copy(
            src_ref=src, dst_ref=dst, send_sem=ss.at[number], recv_sem=rs.at[number],
            device_id=who, device_id_type=pl.DeviceIdType.MESH,
        )

    for load in loads[:3]:
        load.wait()

    lane = lax.broadcasted_iota(jnp.int32, (8, 256), 1)
    slot = lane // BLOCK

    def targets(panel):
        t = jnp.zeros((8, 256), jnp.int32)
        for s in range(4):
            t = jnp.where(slot == s, blocks[panel, s], t)
        return t * BLOCK + (lane - slot * BLOCK)

    idx_out[...] = targets(1)
    target_1 = targets(0)

    row_at = lax.broadcasted_iota(jnp.int32, (512, 256), 0)

    def chooser(t):
        return jnp.where(row_at == t[0:1, :], 1.0, 0.0).astype(BF16)

    def keep(panel):
        live = mask[panel, r].astype(F32)
        return jnp.where(seg * 2 + panel < 127, live, 0.0)

    frows = [None, None]
    for p in (1, 0):
        loads[4 - p].wait()
        ih, il = split(inv[p])
        inv_h[p] = ih
        inv_l[p] = il
        frows[p] = mm(split(fac[p] * keep(p)), (ih, il))
        fg[p, pl.ds(r * 64, 64), :] = frows[p]

    def local_link(p, choose):
        fh, fl = split(fg[p, pl.ds(r * 64, 64), :])
        lp[p, pl.ds(r * 64, 64), :] = dot(fh, choose) + dot(fl, choose)

    def local_base(p, choose):
        ch = dot(inv_h[p], choose)
        cl_ = dot(inv_l[p], choose)
        chh, cll = ch.astype(BF16), cl_.astype(BF16)
        cth, ctl = ch.T.astype(BF16), cl_.T.astype(BF16)
        base[p] = mm((cth, ctl), (chh, cll))

    choose_1 = chooser(target_1)
    local_link(1, choose_1)

    pl.semaphore_wait(barrier, greetings)

    def begin(cond, made):
        @pl.when(cond)
        def _():
            made().start()

        started.append((cond, made))

    begin(plain_out, lambda: copy(idx_out, idx_in, ID_IDX, seg_at(1)))
    begin(far_out, lambda: copy(idx_out, idx_in, ID_IDX, across_half))
    inward = z_at(jnp.where(r == 0, 1, -1))
    relay = lambda: copy(idx_in, idx_in, ID_RELAY, inward)

    def z_parts(buf, ids, p, k, up, lo, n):
        block = (r - k) if up else (r + k)
        block_in = (r - 1 - k) if up else (r + 1 + k)
        sends = jnp.logical_and(r < 3, r - k >= 0) if up else jnp.logical_and(r > 0, r + k <= 3)
        takes = (r - 1 - k >= 0) if up else (r + 1 + k <= 3)
        number = ids + p * 6 + (0 if up else 3) + k
        who = z_at(1 if up else -1)

        def made(b):
            part = buf.at[p, pl.ds(b * 64 + lo, n), :]
            return copy(part, part, number, who)

        return sends, takes, lambda: made(block), lambda: made(block_in)

    def z_send(buf, ids, p, k, lo=0, n=64, cond=None):
        for up in (True, False):
            sends, _, out, _ = z_parts(buf, ids, p, k, up, lo, n)
            if cond is not None:
                sends = both(sends, cond)

            @pl.when(sends)
            def _():
                out().start()

            started.append((sends, out))

    def z_take(buf, ids, p, k, lo=0, n=64, cond=None):
        for up in (True, False):
            _, takes, _, into = z_parts(buf, ids, p, k, up, lo, n)
            if cond is not None:
                takes = both(takes, cond)

            @pl.when(takes)
            def _():
                into().wait_recv()

    def z_next(buf, ids, p, k, lo=0, n=64, cond=None):
        z_take(buf, ids, p, k, lo, n, cond)
        if k < 2:
            z_send(buf, ids, p, k + 1, lo, n, cond)

    halves = ((ID_ZL, 0), (ID_ZL_LATE, 32))
    waits_long = both(head, later)

    z_send(lp, ID_ZL, 1, 0)
    local_base(1, choose_1)
    z_next(lp, ID_ZL, 1, 0)
    z_next(lp, ID_ZL, 1, 1, cond=waits_long)

    @pl.when(jnp.logical_or(plain_in, far_in))
    def _():
        copy(idx_out, idx_in, ID_IDX, mate).wait_recv()

    begin(far_in, relay)

    @pl.when(relay_in)
    def _():
        relay().wait_recv()

    @pl.when(both(head, h == 0))
    def _():
        idx_in[...] = target_1

    choose_0 = chooser(idx_in[...])
    local_link(0, choose_0)
    for ids, lo in halves:
        z_send(lp, ids, 0, 0, lo, 32)
    local_base(0, choose_0)
    z_next(lp, ID_ZL, 1, 1, cond=jnp.logical_not(waits_long))
    for ids, lo in halves:
        z_next(lp, ids, 0, 0, lo, 32)
    for p in (0, 1):
        mine = inv[p, :, pl.ds(pl.multiple_of(r * 128, 128), 128)]
        cov[p] = mm(split(mine.T), (inv_h[p], inv_l[p]))
    for ids, lo in halves:
        z_next(lp, ids, 0, 1, lo, 32)
    z_next(lp, ID_ZL, 1, 2)
    for ids, lo in halves:
        z_next(lp, ids, 0, 2, lo, 32)
    for p in (1, 0):
        z_send(fg, ID_ZF, p, 0)

    link_0 = split(lp[0])
    cl[c] = mm(split(lp[1]), link_0)
    cl_copy = copy(cl.at[c], cl.at[c], ID_CL, mate)
    cl_copy.start()
    ca[c] = sandwich(lp[0], base[1], base[0])
    ca_copy = copy(ca.at[c], ca.at[c], ID_CA, mate)
    ca_copy.start()
    started.append((None, cl_copy))
    started.append((None, ca_copy))

    turn = 1 - 2 * c

    def link_part(j):
        return pl.ds(c * 128 + j * 64, 64), slice(None)

    def constant_part(j):
        if j == 0:
            at = pl.ds(pl.multiple_of(c * 128, 128), 128)
            return at, at
        return pl.ds(c * 64, 64), pl.ds(128, 128)

    def ring_send(buf, ids, at, where, part):
        for way, j in ((0, 0), (1, 1), (0, 1), (1, 0)):
            piece = buf.at[at, *part(j)]
            one = copy(piece, piece, ids + way * 2 + j, where(turn if way == 0 else -turn))
            one.start()
            started.append((None, one))

    def places(at):
        return tuple(lax.rem(at + d + 4, 4) for d in (-turn, turn, 2))

    def mated(buf, place, j, number, part):
        piece = buf.at[place, *part(j)]
        one = copy(piece, piece, number, mate)
        one.start()
        started.append((None, one))
        return one

    def direct(buf, ids, at, where, part):
        behind, ahead, _ = places(at)
        mates = []
        for way, j in ((0, 0), (1, 1), (0, 1), (1, 0)):
            place = behind if way == 0 else ahead
            piece = buf.at[place, *part(j)]
            copy(piece, piece, ids + way * 2 + j, mate).wait_recv()
            if way == j:
                onward = copy(piece, piece, ids + 4 + way, where(turn if way == 0 else -turn))
                onward.start()
                started.append((None, onward))
            mates.append(mated(buf, place, j, ids + 6 + way * 2 + j, part))
        return mates

    def opposite(buf, ids, at, part):
        across = places(at)[2]
        mates = []
        for way in (0, 1):
            piece = buf.at[across, *part(way)]
            copy(piece, piece, ids + 4 + way, mate).wait_recv()
            mates.append(mated(buf, across, way, ids + 10 + way, part))
        return mates

    def done(mates):
        for one in mates:
            one.wait_recv()

    def whole(v):
        return jnp.concatenate([v[:128], jnp.concatenate([v[:128, 128:].T, v[128:, 128:]], 1)], 0)

    rows_256 = lax.broadcasted_iota(jnp.int32, (256, 256), 0)
    eye = (rows_256 == lax.broadcasted_iota(jnp.int32, (256, 256), 1)).astype(F32)

    def near_products(buf):
        rb[0] = eye
        rb[1] = buf[0]
        low = mm(split(buf[1]), split(buf[0]))
        rb[2] = low
        rb[3] = mm(split(buf[2]), split(low))

    def term(buf, place, added):
        return sandwich(rb[place], whole(buf[place]), added)

    def exclusive_links(links, at, out):
        @pl.when(at == 3)
        def _():
            out[...] = eye

        @pl.when(at < 3)
        def _():
            out[...] = links[3]

        for i in (2, 1):

            @pl.when(at < i)
            def _():
                out[...] = mm(split(out[...]), split(links[i]))

    def exclusive_constants(links, consts, at, out):
        @pl.when(at == 3)
        def _():
            out[...] = jnp.zeros((256, 256), F32)

        @pl.when(at < 3)
        def _():
            out[...] = whole(consts[3])

        for i in (2, 1):

            @pl.when(at < i)
            def _():
                out[...] = sandwich(links[i], out[...], whole(consts[i]))

    cl_copy.wait_recv()
    yl[y] = mm(split(cl[1]), split(cl[0]))
    ring_send(yl, ID_YL, y, y_at, link_part)
    ca_copy.wait_recv()
    ya[y] = sandwich(cl[0], ca[1], ca[0])
    ring_send(ya, ID_YA, y, y_at, constant_part)

    yl_mates = direct(yl, ID_YL, y, y_at, link_part)
    z_next(fg, ID_ZF, 1, 0)
    z_next(fg, ID_ZF, 0, 0)
    ya_mates = direct(ya, ID_YA, y, y_at, constant_part)
    done(yl_mates)
    done(ya_mates)

    @pl.when(y == 0)
    def _():
        rb[2] = mm(split(yl[1]), split(yl[0]))
        sm[...] = sandwich(yl[0], whole(ya[1]), whole(ya[0]))

    @pl.when(y == 1)
    def _():
        low = mm(split(yl[1]), split(yl[0]))
        near = sandwich(yl[0], whole(ya[1]), whole(ya[0]))
        rb[3] = mm(split(yl[2]), split(low))
        sm[...] = sandwich(low, whole(ya[2]), near)

    @pl.when(y == 2)
    def _():
        rb[0] = eye
        sm[...] = sandwich(yl[1], sandwich(yl[2], whole(ya[3]), whole(ya[2])), whole(ya[1]))

    @pl.when(y == 3)
    def _():
        rb[1] = yl[0]
        sm[...] = sandwich(yl[2], whole(ya[3]), whole(ya[2]))

    done(opposite(yl, ID_YL, y, link_part))
    high = mm(split(yl[3]), split(yl[2]))
    low = mm(split(yl[1]), split(yl[0]))
    xl[x] = mm(split(high), split(low))
    ring_send(xl, ID_XL, x, x_at, link_part)
    z_next(fg, ID_ZF, 1, 1)

    @pl.when(y == 0)
    def _():
        sm[...] = sandwich(mm(split(yl[2]), split(rb[2])), whole(ya[3]), sm[...])

    @pl.when(y == 2)
    def _():
        sm[...] = sandwich(yl[0], sm[...], jnp.zeros((256, 256), F32))

    @pl.when(y == 3)
    def _():
        sm[...] = sandwich(mm(split(yl[1]), split(yl[0])), sm[...], whole(ya[0]))

    across = places(y)[2]
    done(opposite(ya, ID_YA, y, constant_part))
    xa[x] = term(ya, across, sm[...])
    ring_send(xa, ID_XA, x, x_at, constant_part)

    z_next(fg, ID_ZF, 0, 1)
    exclusive_links(yl, y, el.at[1])
    exclusive_constants(yl, ya, y, ea.at[1])
    xl_mates = direct(xl, ID_XL, x, x_at, link_part)

    @pl.when(c == 0)
    def _():
        ea[1] = sandwich(cl[1], ea[1], ca[1])
        el[1] = mm(split(el[1]), split(cl[1]))

    ea[0] = sandwich(lp[1], ea[1], base[1])
    el[0] = mm(split(el[1]), split(lp[1]))

    xa_mates = direct(xa, ID_XA, x, x_at, constant_part)
    done(xl_mates + opposite(xl, ID_XL, x, link_part))
    sends_half = both(later, edge)
    behind, ahead, across = places(x)
    z_next(fg, ID_ZF, 1, 2)
    z_next(fg, ID_ZF, 0, 2)
    done(xa_mates)

    @pl.when(sends_half)
    def _():
        near_products(xl)
        zero = jnp.zeros((256, 256), F32)
        th[...] = term(xa, behind, term(xa, ahead, term(xa, x, zero)))

    @pl.when(h == 0)
    def _():
        exclusive_links(xl, x, el.at[2])
        entry = split(el[2])
        for p in (1, 0):
            link = mm(entry, split(el[p]))
            pb[...] = link.T
            gg[p] = mm(split(link), split(fg[p]))
            kk[p * 192 : p * 192 + 128, :] = gg[p, :, pl.ds(pl.multiple_of(r * 128, 128), 128)].T
            kk[p * 192 + 128 : p * 192 + 192, :] = pb[pl.ds(r * 64, 64), :]

    done(opposite(xa, ID_XA, x, constant_part))

    hop = z_at(jnp.where(r == 0, -1, 1))

    def zh(j, kind):
        if j < 2:
            part = pl.ds(c * 128 + j * 64, 64), pl.ds(pl.multiple_of(c * 128, 128), 128)
        else:
            part = pl.ds(c * 64, 64), pl.ds(128, 128)
        piece = ph.at[*part]
        if kind == 0:
            return copy(th.at[*part], piece, ID_ZH + j, hop)
        return copy(piece, piece, ID_ZH + 3 * kind + j, inward if kind == 1 else mate)

    @pl.when(sends_half)
    def _():
        th[...] = term(xa, across, th[...])
        for j in (0, 1, 2):
            zh(j, 0).start()

    exclusive_constants(xl, xa, x, ea.at[2])

    def outputs(p):
        constant = sandwich(el[p], ea[2], ea[p])
        mine = fg[p, :, pl.ds(pl.multiple_of(r * 128, 128), 128)]
        middle = mm(split(constant), split(mine))
        pb[...] = constant
        left = jnp.concatenate([middle.T, pb[pl.ds(r * 64, 64), :]], 0)
        out = mm(split(left), split(fg[p]))
        cov[p] += out[:128]
        off[p] = out[128:]

    outputs(1)

    @pl.when(both(h == 0, edge))
    def _():
        for j in (0, 1, 2):
            zh(j, 0).wait_recv()
            zh(j, 1).start()
            zh(j, 2).start()

    outputs(0)

    @pl.when(both(h == 0, jnp.logical_not(edge)))
    def _():
        for j in (0, 1, 2):
            zh(j, 1).wait_recv()
            zh(j, 2).start()

    @pl.when(h == 0)
    def _():
        for j in (0, 1, 2):
            zh(j, 2).wait_recv()
        left = split(mm(split(kk[...]), split(whole(ph[...]))))
        for p in (0, 1):
            at = slice(p * 192, p * 192 + 192)
            out = mm((left[0][at], left[1][at]), split(gg[p]))
            cov[p] += out[:128]
            off[p] += out[128:]

    for p in (0, 1):
        off[p] = off[p] * (-mask[p, r].astype(F32))

    for sends, one in started:
        if sends is None:
            one.wait_send()
        else:

            @pl.when(sends)
            def _():
                one().wait_send()

    @pl.when(sends_half)
    def _():
        for j in (0, 1, 2):
            zh(j, 0).wait_send()

    @pl.when(jnp.logical_and(h == 0, edge))
    def _():
        for j in (0, 1, 2):
            zh(j, 1).wait_send()

    @pl.when(h == 0)
    def _():
        for j in (0, 1, 2):
            zh(j, 2).wait_send()


def body(fill_blocks, fill_mask, inv_diag, factor_off):
    vmem = pl.BlockSpec(memory_space=pltpu.VMEM)

    def sq(n):
        return pltpu.VMEM((n, 256, 256), F32)

    return pl.pallas_call(
        kernel,
        name="chain",
        out_shape=(
            jax.ShapeDtypeStruct((2, 128, 512), F32),
            jax.ShapeDtypeStruct((2, 64, 512), F32),
        ),
        in_specs=[pl.BlockSpec(memory_space=pl.ANY)] * 4,
        out_specs=(vmem, vmem),
        scratch_shapes=[
            pltpu.SMEM((2, 4), jnp.int32),
            pltpu.SMEM((2, 4), jnp.int32),
            pltpu.VMEM((2, 512, 512), F32),
            pltpu.VMEM((2, 64, 512), F32),
            pltpu.SemaphoreType.DMA((5,)),
            pltpu.VMEM((8, 256), jnp.int32),
            pltpu.VMEM((8, 256), jnp.int32),
            pltpu.VMEM((2, 512, 512), BF16),
            pltpu.VMEM((2, 512, 512), BF16),
            sq(2),
            pltpu.VMEM((2, 256, 512), F32),
            sq(2),
            sq(2),
            sq(2),
            sq(4),
            sq(4),
            sq(4),
            sq(4),
            sq(3),
            sq(3),
            pltpu.VMEM((256, 256), F32),
            pltpu.VMEM((256, 256), F32),
            pltpu.VMEM((256, 256), F32),
            sq(4),
            pltpu.VMEM((256, 256), F32),
            pltpu.VMEM((2, 256, 512), F32),
            pltpu.VMEM((384, 256), F32),
            pltpu.SemaphoreType.DMA((N_IDS,)),
            pltpu.SemaphoreType.DMA((N_IDS,)),
        ],
        compiler_params=pltpu.CompilerParams(
            collective_id=0, has_side_effects=True
        ),
    )(fill_blocks, fill_mask, inv_diag, factor_off)


def solution(mesh):
    torus = Mesh(mesh.devices.reshape(2, 4, 4, 2, mesh.shape["row"]), (*SEG, "row"))
    placed = (P(SEG, None), P(SEG, None), P(SEG, None, None), P(SEG, "row", None))
    return jax.shard_map(
        body,
        mesh=torus,
        in_specs=placed,
        out_specs=(P(SEG, "row", None), P(SEG, "row", None)),
        check_vma=False,
    )
```

```python
import jax
import jax.numpy as jnp
from jax import lax
from jax.experimental import pallas as pl
from jax.experimental.pallas import tpu as pltpu
from jax.sharding import Mesh
from jax.sharding import PartitionSpec as P

BLOCK = 64
SEG = ("seg_0", "seg_1", "seg_2", "seg_3")
F32 = jnp.float32
BF16 = jnp.bfloat16
N_IDS = 100

ID_IDX = 0
ID_ZL = 1
ID_ZF = 13
ID_CL = 25
ID_CA = 26
ID_YL = 27
ID_YA = 39
ID_XL = 51
ID_XA = 63
ID_ZL_LATE = 84
ID_ZF_LATE = 90
ID_RELAY = 99
ID_ZH = 75


def split(v):
    hi = v.astype(BF16)
    return hi, (v - hi.astype(F32)).astype(BF16)


def dot(a, b):
    return lax.dot_general(a, b, (((1,), (0,)), ((), ())), preferred_element_type=F32)


def mm(a, b):
    (ah, al), (bh, bl) = a, b
    return dot(ah, bh) + (dot(ah, bl) + dot(al, bh))


def sandwich(link, inner, added):
    left = mm(split(link.T), split(inner))
    return added + mm(split(left), split(link))


def kernel(
    blocks_hbm, mask_hbm, inv_hbm, fac_hbm, cov, off,
    blocks, mask, inv, fac, local, idx_out, idx_in, inv_h, inv_l, lp, fg, base, cl, ca, yl, ya, xl, xa,
    el, ea, ph, th, pb, rb, sm, gg, kk, ss, rs,
):
    h, x, y, c = (lax.axis_index(a) for a in SEG)
    r = lax.axis_index("row")
    z = 4 * h + r
    seg = ((h * 4 + x) * 4 + y) * 2 + c

    both = jnp.logical_and

    def z_at(d):
        zz = lax.rem(z + d + 8, 8)
        return {"seg_0": zz // 4, "row": lax.rem(zz, 4)}

    def seg_at(d):
        s = lax.rem(seg + d + 64, 64)
        return {
            "seg_0": s // 32,
            "seg_1": lax.rem(s // 8, 4),
            "seg_2": lax.rem(s // 2, 4),
            "seg_3": lax.rem(s, 2),
        }

    def y_at(d):
        return {"seg_2": lax.rem(y + d + 4, 4)}

    def x_at(d):
        return {"seg_1": lax.rem(x + d + 4, 4)}

    mate = {"seg_3": 1 - c}

    barrier = pltpu.get_barrier_semaphore()

    def greet(who):
        pl.semaphore_signal(barrier, 1, device_id=who, device_id_type=pl.DeviceIdType.MESH)

    for who in (mate, z_at(1), z_at(-1), y_at(1), y_at(-1), x_at(1), x_at(-1)):
        greet(who)

    later = h == 1
    edge = jnp.logical_or(r == 0, r == 3)
    tail = both(both(x == 3, y == 3), c == 1)
    head = both(both(x == 0, y == 0), c == 0)
    plain_out, plain_in = jnp.logical_not(tail), jnp.logical_not(head)
    far_out = both(both(tail, h == 0), edge)
    far_in = both(both(head, later), edge)
    relay_in = both(both(head, later), jnp.logical_not(edge))
    across_half = {
        "seg_0": 1 - h, "seg_1": lax.rem(x + 1 + 2 * h, 4), "seg_2": lax.rem(y + 1 + 2 * h, 4),
        "seg_3": 1 - c, "row": 3 - r,
    }
    for cond, who in (
        (plain_in, seg_at(-1)), (far_in, across_half),
    ):

        @pl.when(cond)
        def _():
            greet(who)

    greetings = 7
    for cond in (plain_out, far_out):
        greetings = greetings + jnp.where(cond, 1, 0)

    loads = [
        pltpu.make_async_copy(src, dst, local.at[i])
        for i, (src, dst) in enumerate((
            (blocks_hbm, blocks), (mask_hbm, mask), (fac_hbm, fac),
            (inv_hbm.at[c], inv.at[c]), (inv_hbm.at[1 - c], inv.at[1 - c]),
        ))
    ]
    for load in loads:
        load.start()

    started = []

    def copy(src, dst, number, who):
        return pltpu.make_async_remote_copy(
            src_ref=src, dst_ref=dst, send_sem=ss.at[number], recv_sem=rs.at[number],
            device_id=who, device_id_type=pl.DeviceIdType.MESH,
        )

    for load in loads[:3]:
        load.wait()

    lane = lax.broadcasted_iota(jnp.int32, (8, 256), 1)
    slot = lane // BLOCK

    def targets(panel):
        t = jnp.zeros((8, 256), jnp.int32)
        for s in range(4):
            t = jnp.where(slot == s, blocks[panel, s], t)
        return t * BLOCK + (lane - slot * BLOCK)

    idx_out[...] = targets(1)
    target_1 = targets(0)

    row_at = lax.broadcasted_iota(jnp.int32, (512, 256), 0)

    def chooser(t):
        return jnp.where(row_at == t[0:1, :], 1.0, 0.0).astype(BF16)

    def keep(panel):
        live = mask[panel, r].astype(F32)
        return jnp.where(seg * 2 + panel < 127, live, 0.0)

    def factor_rows(p):
        ih, il = split(inv[p])
        inv_h[p] = ih
        inv_l[p] = il
        fg[p, pl.ds(r * 64, 64), :] = mm(split(fac[p] * keep(p)), (ih, il))

    def local_link(p, choose):
        fh, fl = split(fg[p, pl.ds(r * 64, 64), :])
        lp[p, pl.ds(r * 64, 64), :] = dot(fh, choose) + dot(fl, choose)

    def local_base(p, choose):
        ch = dot(inv_h[p], choose)
        cl_ = dot(inv_l[p], choose)
        chh, cll = ch.astype(BF16), cl_.astype(BF16)
        cth, ctl = ch.T.astype(BF16), cl_.T.astype(BF16)
        base[p] = mm((cth, ctl), (chh, cll))

    is_a, is_b = c == 0, c == 1
    loads[3].wait()
    factor_rows(c)

    @pl.when(is_b)
    def _():
        local_link(1, chooser(target_1))

    pl.semaphore_wait(barrier, greetings)

    def begin(cond, made):
        @pl.when(cond)
        def _():
            made().start()

        started.append((cond, made))

    begin(plain_out, lambda: copy(idx_out, idx_in, ID_IDX, seg_at(1)))
    begin(far_out, lambda: copy(idx_out, idx_in, ID_IDX, across_half))
    inward = z_at(jnp.where(r == 0, 1, -1))

    @pl.when(both(head, h == 0))
    def _():
        idx_in[...] = target_1

    relay = lambda: copy(idx_in, idx_in, ID_RELAY, inward)

    def z_parts(buf, ids, p, k, up, lo, n):
        block = (r - k) if up else (r + k)
        block_in = (r - 1 - k) if up else (r + 1 + k)
        sends = jnp.logical_and(r < 3, r - k >= 0) if up else jnp.logical_and(r > 0, r + k <= 3)
        takes = (r - 1 - k >= 0) if up else (r + 1 + k <= 3)
        number = ids + p * 6 + (0 if up else 3) + k
        who = z_at(1 if up else -1)

        def made(b):
            part = buf.at[p, pl.ds(b * 64 + lo, n), :]
            return copy(part, part, number, who)

        return sends, takes, lambda: made(block), lambda: made(block_in)

    def z_send(buf, ids, p, k, lo=0, n=64, cond=None):
        for up in (True, False):
            sends, _, out, _ = z_parts(buf, ids, p, k, up, lo, n)
            if cond is not None:
                sends = both(sends, cond)

            @pl.when(sends)
            def _():
                out().start()

            started.append((sends, out))

    def z_take(buf, ids, p, k, lo=0, n=64, cond=None):
        for up in (True, False):
            _, takes, _, into = z_parts(buf, ids, p, k, up, lo, n)
            if cond is not None:
                takes = both(takes, cond)

            @pl.when(takes)
            def _():
                into().wait_recv()

    def z_next(buf, ids, p, k, lo=0, n=64, cond=None):
        z_take(buf, ids, p, k, lo, n, cond)
        if k < 2:
            z_send(buf, ids, p, k + 1, lo, n, cond)

    waits_long = both(head, later)
    units = (
        (fg, ID_ZF, 0, 0, 32, is_a), (fg, ID_ZF_LATE, 0, 32, 32, is_a),
        (lp, ID_ZL, 1, 0, 64, None),
        (lp, ID_ZL, 0, 0, 32, is_b), (lp, ID_ZL_LATE, 0, 32, 32, is_b),
    )

    def every(k):
        for buf, ids, p, lo, n, cond in units:
            z_next(buf, ids, p, k, lo, n, cond)

    for buf, ids, p, lo, n, cond in units[:2]:
        z_send(buf, ids, p, 0, lo, n, cond)
    z_send(lp, ID_ZL, 1, 0, cond=is_b)
    loads[4].wait()
    factor_rows(1 - c)

    @pl.when(is_a)
    def _():
        local_link(1, chooser(target_1))

    z_send(lp, ID_ZL, 1, 0, cond=is_a)

    @pl.when(is_b)
    def _():
        copy(idx_out, idx_in, ID_IDX, mate).wait_recv()
        local_link(0, chooser(idx_in[...]))

    for buf, ids, p, lo, n, cond in units[3:]:
        z_send(buf, ids, p, 0, lo, n, cond)
    local_base(1, chooser(target_1))
    every(0)

    @pl.when(both(is_a, plain_in))
    def _():
        copy(idx_out, idx_in, ID_IDX, mate).wait_recv()

    @pl.when(jnp.logical_not(waits_long))
    def _():
        local_base(0, chooser(idx_in[...]))

    every(1)

    @pl.when(far_in)
    def _():
        copy(idx_out, idx_in, ID_IDX, mate).wait_recv()

    begin(far_in, relay)
    for p in (0, 1):
        mine = inv[p, :, pl.ds(pl.multiple_of(r * 128, 128), 128)]
        cov[p] = mm(split(mine.T), (inv_h[p], inv_l[p]))
    every(2)

    @pl.when(relay_in)
    def _():
        relay().wait_recv()

    @pl.when(waits_long)
    def _():
        local_base(0, chooser(idx_in[...]))

    @pl.when(is_a)
    def _():
        fh, fl = split(fg[0])
        choose = chooser(idx_in[...])
        lp[0] = dot(fh, choose) + dot(fl, choose)

    z_send(fg, ID_ZF, 1, 0)
    z_send(fg, ID_ZF, 0, 0, cond=is_b)

    link_0 = split(lp[0])
    cl[c] = mm(split(lp[1]), link_0)
    cl_copy = copy(cl.at[c], cl.at[c], ID_CL, mate)
    cl_copy.start()
    ca[c] = sandwich(lp[0], base[1], base[0])
    ca_copy = copy(ca.at[c], ca.at[c], ID_CA, mate)
    ca_copy.start()
    started.append((None, cl_copy))
    started.append((None, ca_copy))

    turn = 1 - 2 * c

    def link_part(j):
        return pl.ds(c * 128 + j * 64, 64), slice(None)

    def constant_part(j):
        if j == 0:
            at = pl.ds(pl.multiple_of(c * 128, 128), 128)
            return at, at
        return pl.ds(c * 64, 64), pl.ds(128, 128)

    def ring_send(buf, ids, at, where, part):
        for way, j in ((0, 0), (1, 1), (0, 1), (1, 0)):
            piece = buf.at[at, *part(j)]
            one = copy(piece, piece, ids + way * 2 + j, where(turn if way == 0 else -turn))
            one.start()
            started.append((None, one))

    def places(at):
        return tuple(lax.rem(at + d + 4, 4) for d in (-turn, turn, 2))

    def mated(buf, place, j, number, part):
        piece = buf.at[place, *part(j)]
        one = copy(piece, piece, number, mate)
        one.start()
        started.append((None, one))
        return one

    def direct(buf, ids, at, where, part):
        behind, ahead, _ = places(at)
        mates = []
        for way, j in ((0, 0), (1, 1), (0, 1), (1, 0)):
            place = behind if way == 0 else ahead
            piece = buf.at[place, *part(j)]
            copy(piece, piece, ids + way * 2 + j, mate).wait_recv()
            if way == j:
                onward = copy(piece, piece, ids + 4 + way, where(turn if way == 0 else -turn))
                onward.start()
                started.append((None, onward))
            mates.append(mated(buf, place, j, ids + 6 + way * 2 + j, part))
        return mates

    def opposite(buf, ids, at, part):
        across = places(at)[2]
        mates = []
        for way in (0, 1):
            piece = buf.at[across, *part(way)]
            copy(piece, piece, ids + 4 + way, mate).wait_recv()
            mates.append(mated(buf, across, way, ids + 10 + way, part))
        return mates

    def done(mates):
        for one in mates:
            one.wait_recv()

    def whole(v):
        return jnp.concatenate([v[:128], jnp.concatenate([v[:128, 128:].T, v[128:, 128:]], 1)], 0)

    rows_256 = lax.broadcasted_iota(jnp.int32, (256, 256), 0)
    eye = (rows_256 == lax.broadcasted_iota(jnp.int32, (256, 256), 1)).astype(F32)

    def near_products(buf):
        rb[0] = eye
        rb[1] = buf[0]
        low = mm(split(buf[1]), split(buf[0]))
        rb[2] = low
        rb[3] = mm(split(buf[2]), split(low))

    def term(buf, place, added):
        return sandwich(rb[place], whole(buf[place]), added)

    def exclusive_links(links, at, out):
        @pl.when(at == 3)
        def _():
            out[...] = eye

        @pl.when(at < 3)
        def _():
            out[...] = links[3]

        for i in (2, 1):

            @pl.when(at < i)
            def _():
                out[...] = mm(split(out[...]), split(links[i]))

    def exclusive_constants(links, consts, at, out):
        @pl.when(at == 3)
        def _():
            out[...] = jnp.zeros((256, 256), F32)

        @pl.when(at < 3)
        def _():
            out[...] = whole(consts[3])

        for i in (2, 1):

            @pl.when(at < i)
            def _():
                out[...] = sandwich(links[i], out[...], whole(consts[i]))

    cl_copy.wait_recv()
    yl[y] = mm(split(cl[1]), split(cl[0]))
    ring_send(yl, ID_YL, y, y_at, link_part)
    ca_copy.wait_recv()
    ya[y] = sandwich(cl[0], ca[1], ca[0])
    ring_send(ya, ID_YA, y, y_at, constant_part)

    yl_mates = direct(yl, ID_YL, y, y_at, link_part)
    z_next(fg, ID_ZF, 1, 0)
    z_next(fg, ID_ZF, 0, 0, cond=is_b)
    ya_mates = direct(ya, ID_YA, y, y_at, constant_part)
    done(yl_mates)
    done(ya_mates)

    @pl.when(y == 0)
    def _():
        rb[2] = mm(split(yl[1]), split(yl[0]))
        sm[...] = sandwich(yl[0], whole(ya[1]), whole(ya[0]))

    @pl.when(y == 1)
    def _():
        low = mm(split(yl[1]), split(yl[0]))
        near = sandwich(yl[0], whole(ya[1]), whole(ya[0]))
        rb[3] = mm(split(yl[2]), split(low))
        sm[...] = sandwich(low, whole(ya[2]), near)

    @pl.when(y == 2)
    def _():
        rb[0] = eye
        sm[...] = sandwich(yl[1], sandwich(yl[2], whole(ya[3]), whole(ya[2])), whole(ya[1]))

    @pl.when(y == 3)
    def _():
        rb[1] = yl[0]
        sm[...] = sandwich(yl[2], whole(ya[3]), whole(ya[2]))

    done(opposite(yl, ID_YL, y, link_part))
    high = mm(split(yl[3]), split(yl[2]))
    low = mm(split(yl[1]), split(yl[0]))
    xl[x] = mm(split(high), split(low))
    ring_send(xl, ID_XL, x, x_at, link_part)
    z_next(fg, ID_ZF, 1, 1)

    @pl.when(y == 0)
    def _():
        sm[...] = sandwich(mm(split(yl[2]), split(rb[2])), whole(ya[3]), sm[...])

    @pl.when(y == 2)
    def _():
        sm[...] = sandwich(yl[0], sm[...], jnp.zeros((256, 256), F32))

    @pl.when(y == 3)
    def _():
        sm[...] = sandwich(mm(split(yl[1]), split(yl[0])), sm[...], whole(ya[0]))

    across = places(y)[2]
    done(opposite(ya, ID_YA, y, constant_part))
    xa[x] = term(ya, across, sm[...])
    ring_send(xa, ID_XA, x, x_at, constant_part)

    z_next(fg, ID_ZF, 0, 1, cond=is_b)
    exclusive_links(yl, y, el.at[1])
    exclusive_constants(yl, ya, y, ea.at[1])
    xl_mates = direct(xl, ID_XL, x, x_at, link_part)

    @pl.when(c == 0)
    def _():
        ea[1] = sandwich(cl[1], ea[1], ca[1])
        el[1] = mm(split(el[1]), split(cl[1]))

    ea[0] = sandwich(lp[1], ea[1], base[1])
    el[0] = mm(split(el[1]), split(lp[1]))

    xa_mates = direct(xa, ID_XA, x, x_at, constant_part)
    done(xl_mates + opposite(xl, ID_XL, x, link_part))
    sends_half = both(later, edge)
    behind, ahead, across = places(x)
    z_next(fg, ID_ZF, 1, 2)
    z_next(fg, ID_ZF, 0, 2, cond=is_b)
    done(xa_mates)

    @pl.when(sends_half)
    def _():
        near_products(xl)
        zero = jnp.zeros((256, 256), F32)
        th[...] = term(xa, behind, term(xa, ahead, term(xa, x, zero)))

    @pl.when(h == 0)
    def _():
        exclusive_links(xl, x, el.at[2])
        entry = split(el[2])
        for p in (1, 0):
            link = mm(entry, split(el[p]))
            pb[...] = link.T
            gg[p] = mm(split(link), split(fg[p]))
            kk[p * 192 : p * 192 + 128, :] = gg[p, :, pl.ds(pl.multiple_of(r * 128, 128), 128)].T
            kk[p * 192 + 128 : p * 192 + 192, :] = pb[pl.ds(r * 64, 64), :]

    done(opposite(xa, ID_XA, x, constant_part))

    hop = z_at(jnp.where(r == 0, -1, 1))

    def zh(j, kind):
        if j < 2:
            part = pl.ds(c * 128 + j * 64, 64), pl.ds(pl.multiple_of(c * 128, 128), 128)
        else:
            part = pl.ds(c * 64, 64), pl.ds(128, 128)
        piece = ph.at[*part]
        if kind == 0:
            return copy(th.at[*part], piece, ID_ZH + j, hop)
        return copy(piece, piece, ID_ZH + 3 * kind + j, inward if kind == 1 else mate)

    @pl.when(sends_half)
    def _():
        th[...] = term(xa, across, th[...])
        for j in (0, 1, 2):
            zh(j, 0).start()

    exclusive_constants(xl, xa, x, ea.at[2])

    def outputs(p):
        constant = sandwich(el[p], ea[2], ea[p])
        mine = fg[p, :, pl.ds(pl.multiple_of(r * 128, 128), 128)]
        middle = mm(split(constant), split(mine))
        pb[...] = constant
        left = jnp.concatenate([middle.T, pb[pl.ds(r * 64, 64), :]], 0)
        out = mm(split(left), split(fg[p]))
        cov[p] += out[:128]
        off[p] = out[128:]

    outputs(1)

    @pl.when(both(h == 0, edge))
    def _():
        for j in (0, 1, 2):
            zh(j, 0).wait_recv()
            zh(j, 1).start()
            zh(j, 2).start()

    outputs(0)

    @pl.when(both(h == 0, jnp.logical_not(edge)))
    def _():
        for j in (0, 1, 2):
            zh(j, 1).wait_recv()
            zh(j, 2).start()

    @pl.when(h == 0)
    def _():
        for j in (0, 1, 2):
            zh(j, 2).wait_recv()
        left = split(mm(split(kk[...]), split(whole(ph[...]))))
        for p in (0, 1):
            at = slice(p * 192, p * 192 + 192)
            out = mm((left[0][at], left[1][at]), split(gg[p]))
            cov[p] += out[:128]
            off[p] += out[128:]

    for p in (0, 1):
        off[p] = off[p] * (-mask[p, r].astype(F32))

    for sends, one in started:
        if sends is None:
            one.wait_send()
        else:

            @pl.when(sends)
            def _():
                one().wait_send()

    @pl.when(sends_half)
    def _():
        for j in (0, 1, 2):
            zh(j, 0).wait_send()

    @pl.when(jnp.logical_and(h == 0, edge))
    def _():
        for j in (0, 1, 2):
            zh(j, 1).wait_send()

    @pl.when(h == 0)
    def _():
        for j in (0, 1, 2):
            zh(j, 2).wait_send()


def body(fill_blocks, fill_mask, inv_diag, factor_off):
    vmem = pl.BlockSpec(memory_space=pltpu.VMEM)

    def sq(n):
        return pltpu.VMEM((n, 256, 256), F32)

    return pl.pallas_call(
        kernel,
        name="chain",
        out_shape=(
            jax.ShapeDtypeStruct((2, 128, 512), F32),
            jax.ShapeDtypeStruct((2, 64, 512), F32),
        ),
        in_specs=[pl.BlockSpec(memory_space=pl.ANY)] * 4,
        out_specs=(vmem, vmem),
        scratch_shapes=[
            pltpu.SMEM((2, 4), jnp.int32),
            pltpu.SMEM((2, 4), jnp.int32),
            pltpu.VMEM((2, 512, 512), F32),
            pltpu.VMEM((2, 64, 512), F32),
            pltpu.SemaphoreType.DMA((5,)),
            pltpu.VMEM((8, 256), jnp.int32),
            pltpu.VMEM((8, 256), jnp.int32),
            pltpu.VMEM((2, 512, 512), BF16),
            pltpu.VMEM((2, 512, 512), BF16),
            sq(2),
            pltpu.VMEM((2, 256, 512), F32),
            sq(2),
            sq(2),
            sq(2),
            sq(4),
            sq(4),
            sq(4),
            sq(4),
            sq(3),
            sq(3),
            pltpu.VMEM((256, 256), F32),
            pltpu.VMEM((256, 256), F32),
            pltpu.VMEM((256, 256), F32),
            sq(4),
            pltpu.VMEM((256, 256), F32),
            pltpu.VMEM((2, 256, 512), F32),
            pltpu.VMEM((384, 256), F32),
            pltpu.SemaphoreType.DMA((N_IDS,)),
            pltpu.SemaphoreType.DMA((N_IDS,)),
        ],
        compiler_params=pltpu.CompilerParams(
            collective_id=0, has_side_effects=True
        ),
    )(fill_blocks, fill_mask, inv_diag, factor_off)


def solution(mesh):
    torus = Mesh(mesh.devices.reshape(2, 4, 4, 2, mesh.shape["row"]), (*SEG, "row"))
    placed = (P(SEG, None), P(SEG, None), P(SEG, None, None), P(SEG, "row", None))
    return jax.shard_map(
        body,
        mesh=torus,
        in_specs=placed,
        out_specs=(P(SEG, "row", None), P(SEG, "row", None)),
        check_vma=False,
    )
```

```python
import jax
import jax.numpy as jnp
from jax import lax
from jax.experimental import pallas as pl
from jax.experimental.pallas import tpu as pltpu
from jax.sharding import Mesh
from jax.sharding import PartitionSpec as P

BLOCK = 64
SEG = ("seg_0", "seg_1", "seg_2", "seg_3")
F32 = jnp.float32
BF16 = jnp.bfloat16
N_IDS = 100

ID_IDX = 0
ID_ZL = 1
ID_ZF = 13
ID_CL = 25
ID_CA = 26
ID_YL = 27
ID_YA = 39
ID_XL = 51
ID_XA = 63
ID_ZL_LATE = 84
ID_ZF_LATE = 90
ID_RELAY = 99
ID_ZH = 75


def split(v):
    hi = v.astype(BF16)
    return hi, (v - hi.astype(F32)).astype(BF16)


def dot(a, b):
    return lax.dot_general(a, b, (((1,), (0,)), ((), ())), preferred_element_type=F32)


def mm(a, b):
    (ah, al), (bh, bl) = a, b
    return dot(ah, bh) + (dot(ah, bl) + dot(al, bh))


def sandwich(link, inner, added):
    left = mm(split(link.T), split(inner))
    return added + mm(split(left), split(link))


def kernel(
    blocks_hbm, mask_hbm, inv_hbm, fac_hbm, cov, off,
    blocks, mask, inv, fac, local, idx_out, idx_in, inv_h, inv_l, lp, fg, base, cl, ca, yl, ya, xl, xa,
    el, ea, ph, th, pb, rb, sm, gg, kk, ss, rs,
):
    h, x, y, c = (lax.axis_index(a) for a in SEG)
    r = lax.axis_index("row")
    z = 4 * h + r
    seg = ((h * 4 + x) * 4 + y) * 2 + c

    both = jnp.logical_and

    def z_at(d):
        zz = lax.rem(z + d + 8, 8)
        return {"seg_0": zz // 4, "row": lax.rem(zz, 4)}

    def seg_at(d):
        s = lax.rem(seg + d + 64, 64)
        return {
            "seg_0": s // 32,
            "seg_1": lax.rem(s // 8, 4),
            "seg_2": lax.rem(s // 2, 4),
            "seg_3": lax.rem(s, 2),
        }

    def y_at(d):
        return {"seg_2": lax.rem(y + d + 4, 4)}

    def x_at(d):
        return {"seg_1": lax.rem(x + d + 4, 4)}

    mate = {"seg_3": 1 - c}

    barrier = pltpu.get_barrier_semaphore()

    def greet(who):
        pl.semaphore_signal(barrier, 1, device_id=who, device_id_type=pl.DeviceIdType.MESH)

    for who in (mate, z_at(1), z_at(-1), y_at(1), y_at(-1), x_at(1), x_at(-1)):
        greet(who)

    later = h == 1
    edge = jnp.logical_or(r == 0, r == 3)
    tail = both(both(x == 3, y == 3), c == 1)
    head = both(both(x == 0, y == 0), c == 0)
    plain_out, plain_in = jnp.logical_not(tail), jnp.logical_not(head)
    far_out = both(both(tail, h == 0), edge)
    far_in = both(both(head, later), edge)
    relay_in = both(both(head, later), jnp.logical_not(edge))
    across_half = {
        "seg_0": 1 - h, "seg_1": lax.rem(x + 1 + 2 * h, 4), "seg_2": lax.rem(y + 1 + 2 * h, 4),
        "seg_3": 1 - c, "row": 3 - r,
    }
    for cond, who in (
        (plain_in, seg_at(-1)), (far_in, across_half),
    ):

        @pl.when(cond)
        def _():
            greet(who)

    greetings = 7
    for cond in (plain_out, far_out):
        greetings = greetings + jnp.where(cond, 1, 0)

    loads = [
        pltpu.make_async_copy(src, dst, local.at[i])
        for i, (src, dst) in enumerate((
            (blocks_hbm, blocks), (mask_hbm, mask), (fac_hbm, fac),
            (inv_hbm.at[c], inv.at[c]), (inv_hbm.at[1 - c], inv.at[1 - c]),
        ))
    ]
    for load in loads:
        load.start()

    started = []

    def copy(src, dst, number, who):
        return pltpu.make_async_remote_copy(
            src_ref=src, dst_ref=dst, send_sem=ss.at[number], recv_sem=rs.at[number],
            device_id=who, device_id_type=pl.DeviceIdType.MESH,
        )

    for load in loads[:3]:
        load.wait()

    lane = lax.broadcasted_iota(jnp.int32, (8, 256), 1)
    slot = lane // BLOCK

    def targets(panel):
        t = jnp.zeros((8, 256), jnp.int32)
        for s in range(4):
            t = jnp.where(slot == s, blocks[panel, s], t)
        return t * BLOCK + (lane - slot * BLOCK)

    idx_out[...] = targets(1)
    target_1 = targets(0)

    row_at = lax.broadcasted_iota(jnp.int32, (512, 256), 0)

    def chooser(t):
        return jnp.where(row_at == t[0:1, :], 1.0, 0.0).astype(BF16)

    def keep(panel):
        live = mask[panel, r].astype(F32)
        return jnp.where(seg * 2 + panel < 127, live, 0.0)

    def factor_rows(p):
        ih, il = split(inv[p])
        inv_h[p] = ih
        inv_l[p] = il
        fg[p, pl.ds(r * 64, 64), :] = mm(split(fac[p] * keep(p)), (ih, il))

    def local_link(p, choose):
        fh, fl = split(fg[p, pl.ds(r * 64, 64), :])
        lp[p, pl.ds(r * 64, 64), :] = dot(fh, choose) + dot(fl, choose)

    def local_base(p, choose):
        ch = dot(inv_h[p], choose)
        cl_ = dot(inv_l[p], choose)
        chh, cll = ch.astype(BF16), cl_.astype(BF16)
        cth, ctl = ch.T.astype(BF16), cl_.T.astype(BF16)
        base[p] = mm((cth, ctl), (chh, cll))

    is_a, is_b = c == 0, c == 1
    loads[3].wait()
    factor_rows(c)

    @pl.when(is_b)
    def _():
        local_link(1, chooser(target_1))

    pl.semaphore_wait(barrier, greetings)

    def begin(cond, made):
        @pl.when(cond)
        def _():
            made().start()

        started.append((cond, made))

    begin(plain_out, lambda: copy(idx_out, idx_in, ID_IDX, seg_at(1)))
    begin(far_out, lambda: copy(idx_out, idx_in, ID_IDX, across_half))
    inward = z_at(jnp.where(r == 0, 1, -1))

    @pl.when(both(head, h == 0))
    def _():
        idx_in[...] = target_1

    relay = lambda: copy(idx_in, idx_in, ID_RELAY, inward)

    def z_parts(buf, ids, p, k, up, lo, n):
        block = (r - k) if up else (r + k)
        block_in = (r - 1 - k) if up else (r + 1 + k)
        sends = jnp.logical_and(r < 3, r - k >= 0) if up else jnp.logical_and(r > 0, r + k <= 3)
        takes = (r - 1 - k >= 0) if up else (r + 1 + k <= 3)
        number = ids + p * 6 + (0 if up else 3) + k
        who = z_at(1 if up else -1)

        def made(b):
            part = buf.at[p, pl.ds(b * 64 + lo, n), :]
            return copy(part, part, number, who)

        return sends, takes, lambda: made(block), lambda: made(block_in)

    def z_send(buf, ids, p, k, lo=0, n=64, cond=None):
        for up in (True, False):
            sends, _, out, _ = z_parts(buf, ids, p, k, up, lo, n)
            if cond is not None:
                sends = both(sends, cond)

            @pl.when(sends)
            def _():
                out().start()

            started.append((sends, out))

    def z_take(buf, ids, p, k, lo=0, n=64, cond=None):
        for up in (True, False):
            _, takes, _, into = z_parts(buf, ids, p, k, up, lo, n)
            if cond is not None:
                takes = both(takes, cond)

            @pl.when(takes)
            def _():
                into().wait_recv()

    def z_next(buf, ids, p, k, lo=0, n=64, cond=None):
        z_take(buf, ids, p, k, lo, n, cond)
        if k < 2:
            z_send(buf, ids, p, k + 1, lo, n, cond)

    waits_long = both(head, later)
    units = (
        (fg, ID_ZF, 0, 0, 32, is_a), (fg, ID_ZF_LATE, 0, 32, 32, is_a),
        (lp, ID_ZL, 1, 0, 64, None),
        (lp, ID_ZL, 0, 0, 32, is_b), (lp, ID_ZL_LATE, 0, 32, 32, is_b),
    )

    def every(k):
        for buf, ids, p, lo, n, cond in units:
            z_next(buf, ids, p, k, lo, n, cond)

    for buf, ids, p, lo, n, cond in units[:2]:
        z_send(buf, ids, p, 0, lo, n, cond)
    z_send(lp, ID_ZL, 1, 0, cond=is_b)
    loads[4].wait()
    factor_rows(1 - c)

    @pl.when(is_a)
    def _():
        local_link(1, chooser(target_1))

    z_send(lp, ID_ZL, 1, 0, cond=is_a)

    @pl.when(is_b)
    def _():
        copy(idx_out, idx_in, ID_IDX, mate).wait_recv()
        local_link(0, chooser(idx_in[...]))

    for buf, ids, p, lo, n, cond in units[3:]:
        z_send(buf, ids, p, 0, lo, n, cond)
    local_base(1, chooser(target_1))
    every(0)

    @pl.when(both(is_a, plain_in))
    def _():
        copy(idx_out, idx_in, ID_IDX, mate).wait_recv()

    @pl.when(jnp.logical_not(waits_long))
    def _():
        local_base(0, chooser(idx_in[...]))

    every(1)

    @pl.when(far_in)
    def _():
        copy(idx_out, idx_in, ID_IDX, mate).wait_recv()

    begin(far_in, relay)
    for p in (0, 1):
        mine = inv[p, :, pl.ds(pl.multiple_of(r * 128, 128), 128)]
        cov[p] = mm(split(mine.T), (inv_h[p], inv_l[p]))
    every(2)

    @pl.when(relay_in)
    def _():
        relay().wait_recv()

    @pl.when(waits_long)
    def _():
        local_base(0, chooser(idx_in[...]))

    @pl.when(is_a)
    def _():
        fh, fl = split(fg[0])
        choose = chooser(idx_in[...])
        lp[0] = dot(fh, choose) + dot(fl, choose)

    z_send(fg, ID_ZF, 1, 0)
    z_send(fg, ID_ZF, 0, 0, cond=is_b)

    link_0 = split(lp[0])
    cl[c] = mm(split(lp[1]), link_0)
    cl_copy = copy(cl.at[c], cl.at[c], ID_CL, mate)
    cl_copy.start()
    ca[c] = sandwich(lp[0], base[1], base[0])
    ca_copy = copy(ca.at[c], ca.at[c], ID_CA, mate)
    ca_copy.start()
    started.append((None, cl_copy))
    started.append((None, ca_copy))

    turn = 1 - 2 * c

    def link_part(j):
        return pl.ds(c * 128 + j * 64, 64), slice(None)

    def constant_part(j):
        if j == 0:
            at = pl.ds(pl.multiple_of(c * 128, 128), 128)
            return at, at
        return pl.ds(c * 64, 64), pl.ds(128, 128)

    def ring_send(buf, ids, at, where, part):
        for way, j in ((0, 0), (1, 1), (0, 1), (1, 0)):
            piece = buf.at[at, *part(j)]
            one = copy(piece, piece, ids + way * 2 + j, where(turn if way == 0 else -turn))
            one.start()
            started.append((None, one))

    def places(at):
        return tuple(lax.rem(at + d + 4, 4) for d in (-turn, turn, 2))

    def mated(buf, place, j, number, part):
        piece = buf.at[place, *part(j)]
        one = copy(piece, piece, number, mate)
        one.start()
        started.append((None, one))
        return one

    def direct(buf, ids, at, where, part):
        behind, ahead, _ = places(at)
        mates = []
        for way, j in ((0, 0), (1, 1), (0, 1), (1, 0)):
            place = behind if way == 0 else ahead
            piece = buf.at[place, *part(j)]
            copy(piece, piece, ids + way * 2 + j, mate).wait_recv()
            if way == j:
                onward = copy(piece, piece, ids + 4 + way, where(turn if way == 0 else -turn))
                onward.start()
                started.append((None, onward))
            mates.append(mated(buf, place, j, ids + 6 + way * 2 + j, part))
        return mates

    def opposite(buf, ids, at, part):
        across = places(at)[2]
        mates = []
        for way in (0, 1):
            piece = buf.at[across, *part(way)]
            copy(piece, piece, ids + 4 + way, mate).wait_recv()
            mates.append(mated(buf, across, way, ids + 10 + way, part))
        return mates

    def done(mates):
        for one in mates:
            one.wait_recv()

    def whole(v):
        return jnp.concatenate([v[:128], jnp.concatenate([v[:128, 128:].T, v[128:, 128:]], 1)], 0)

    rows_256 = lax.broadcasted_iota(jnp.int32, (256, 256), 0)
    eye = (rows_256 == lax.broadcasted_iota(jnp.int32, (256, 256), 1)).astype(F32)

    def near_products(buf):
        rb[0] = eye
        rb[1] = buf[0]
        low = mm(split(buf[1]), split(buf[0]))
        rb[2] = low
        rb[3] = mm(split(buf[2]), split(low))

    def term(buf, place, added):
        return sandwich(rb[place], whole(buf[place]), added)

    def exclusive_links(links, at, out):
        @pl.when(at == 3)
        def _():
            out[...] = eye

        @pl.when(at < 3)
        def _():
            out[...] = links[3]

        for i in (2, 1):

            @pl.when(at < i)
            def _():
                out[...] = mm(split(out[...]), split(links[i]))

    def exclusive_constants(links, consts, at, out):
        @pl.when(at == 3)
        def _():
            out[...] = jnp.zeros((256, 256), F32)

        @pl.when(at < 3)
        def _():
            out[...] = whole(consts[3])

        for i in (2, 1):

            @pl.when(at < i)
            def _():
                out[...] = sandwich(links[i], out[...], whole(consts[i]))

    cl_copy.wait_recv()
    yl[y] = mm(split(cl[1]), split(cl[0]))
    ring_send(yl, ID_YL, y, y_at, link_part)
    ca_copy.wait_recv()
    ya[y] = sandwich(cl[0], ca[1], ca[0])
    ring_send(ya, ID_YA, y, y_at, constant_part)

    yl_mates = direct(yl, ID_YL, y, y_at, link_part)
    z_next(fg, ID_ZF, 1, 0)
    z_next(fg, ID_ZF, 0, 0, cond=is_b)
    ya_mates = direct(ya, ID_YA, y, y_at, constant_part)
    done(yl_mates)
    done(ya_mates)

    @pl.when(y == 0)
    def _():
        rb[2] = mm(split(yl[1]), split(yl[0]))
        sm[...] = sandwich(yl[0], whole(ya[1]), whole(ya[0]))

    @pl.when(y == 1)
    def _():
        low = mm(split(yl[1]), split(yl[0]))
        near = sandwich(yl[0], whole(ya[1]), whole(ya[0]))
        rb[3] = mm(split(yl[2]), split(low))
        sm[...] = sandwich(low, whole(ya[2]), near)

    @pl.when(y == 2)
    def _():
        rb[0] = eye
        sm[...] = sandwich(yl[1], sandwich(yl[2], whole(ya[3]), whole(ya[2])), whole(ya[1]))

    @pl.when(y == 3)
    def _():
        rb[1] = yl[0]
        sm[...] = sandwich(yl[2], whole(ya[3]), whole(ya[2]))

    done(opposite(yl, ID_YL, y, link_part))
    high = mm(split(yl[3]), split(yl[2]))
    low = mm(split(yl[1]), split(yl[0]))
    xl[x] = mm(split(high), split(low))
    ring_send(xl, ID_XL, x, x_at, link_part)
    z_next(fg, ID_ZF, 1, 1)

    @pl.when(y == 0)
    def _():
        sm[...] = sandwich(mm(split(yl[2]), split(rb[2])), whole(ya[3]), sm[...])

    @pl.when(y == 2)
    def _():
        sm[...] = sandwich(yl[0], sm[...], jnp.zeros((256, 256), F32))

    @pl.when(y == 3)
    def _():
        sm[...] = sandwich(mm(split(yl[1]), split(yl[0])), sm[...], whole(ya[0]))

    across = places(y)[2]
    done(opposite(ya, ID_YA, y, constant_part))
    xa[x] = term(ya, across, sm[...])
    ring_send(xa, ID_XA, x, x_at, constant_part)

    z_next(fg, ID_ZF, 0, 1, cond=is_b)

    def group_map():
        exclusive_links(yl, y, el.at[1])
        exclusive_constants(yl, ya, y, ea.at[1])

    def panel_maps():
        @pl.when(c == 0)
        def _():
            ea[1] = sandwich(cl[1], ea[1], ca[1])
            el[1] = mm(split(el[1]), split(cl[1]))

        ea[0] = sandwich(lp[1], ea[1], base[1])
        el[0] = mm(split(el[1]), split(lp[1]))

    pl.when(h == 0)(group_map)
    xl_mates = direct(xl, ID_XL, x, x_at, link_part)
    pl.when(h == 0)(panel_maps)
    xa_mates = direct(xa, ID_XA, x, x_at, constant_part)
    done(xl_mates + opposite(xl, ID_XL, x, link_part))
    sends_half = both(later, edge)
    behind, ahead, across = places(x)
    z_next(fg, ID_ZF, 1, 2, cond=h == 0)
    z_next(fg, ID_ZF, 0, 2, cond=both(is_b, h == 0))
    done(xa_mates)

    @pl.when(sends_half)
    def _():
        near_products(xl)
        zero = jnp.zeros((256, 256), F32)
        th[...] = term(xa, behind, term(xa, ahead, term(xa, x, zero)))

    @pl.when(h == 0)
    def _():
        exclusive_links(xl, x, el.at[2])
        entry = split(el[2])
        for p in (1, 0):
            link = mm(entry, split(el[p]))
            pb[...] = link.T
            gg[p] = mm(split(link), split(fg[p]))
            kk[p * 192 : p * 192 + 128, :] = gg[p, :, pl.ds(pl.multiple_of(r * 128, 128), 128)].T
            kk[p * 192 + 128 : p * 192 + 192, :] = pb[pl.ds(r * 64, 64), :]

    done(opposite(xa, ID_XA, x, constant_part))

    hop = z_at(jnp.where(r == 0, -1, 1))

    def zh(j, kind):
        if j < 2:
            part = pl.ds(c * 128 + j * 64, 64), pl.ds(pl.multiple_of(c * 128, 128), 128)
        else:
            part = pl.ds(c * 64, 64), pl.ds(128, 128)
        piece = ph.at[*part]
        if kind == 0:
            return copy(th.at[*part], piece, ID_ZH + j, hop)
        return copy(piece, piece, ID_ZH + 3 * kind + j, inward if kind == 1 else mate)

    @pl.when(sends_half)
    def _():
        th[...] = term(xa, across, th[...])
        for j in (0, 1, 2):
            zh(j, 0).start()

    z_next(fg, ID_ZF, 1, 2, cond=later)
    z_next(fg, ID_ZF, 0, 2, cond=both(is_b, later))

    @pl.when(later)
    def _():
        group_map()
        panel_maps()

    exclusive_constants(xl, xa, x, ea.at[2])

    def outputs(p):
        constant = sandwich(el[p], ea[2], ea[p])
        mine = fg[p, :, pl.ds(pl.multiple_of(r * 128, 128), 128)]
        middle = mm(split(constant), split(mine))
        pb[...] = constant
        left = jnp.concatenate([middle.T, pb[pl.ds(r * 64, 64), :]], 0)
        out = mm(split(left), split(fg[p]))
        cov[p] += out[:128]
        off[p] = out[128:]

    outputs(1)

    @pl.when(both(h == 0, edge))
    def _():
        for j in (0, 1, 2):
            zh(j, 0).wait_recv()
            zh(j, 1).start()
            zh(j, 2).start()

    outputs(0)

    @pl.when(both(h == 0, jnp.logical_not(edge)))
    def _():
        for j in (0, 1, 2):
            zh(j, 1).wait_recv()
            zh(j, 2).start()

    @pl.when(h == 0)
    def _():
        for j in (0, 1, 2):
            zh(j, 2).wait_recv()
        left = split(mm(split(kk[...]), split(whole(ph[...]))))
        for p in (0, 1):
            at = slice(p * 192, p * 192 + 192)
            out = mm((left[0][at], left[1][at]), split(gg[p]))
            cov[p] += out[:128]
            off[p] += out[128:]

    for p in (0, 1):
        off[p] = off[p] * (-mask[p, r].astype(F32))

    for sends, one in started:
        if sends is None:
            one.wait_send()
        else:

            @pl.when(sends)
            def _():
                one().wait_send()

    @pl.when(sends_half)
    def _():
        for j in (0, 1, 2):
            zh(j, 0).wait_send()

    @pl.when(jnp.logical_and(h == 0, edge))
    def _():
        for j in (0, 1, 2):
            zh(j, 1).wait_send()

    @pl.when(h == 0)
    def _():
        for j in (0, 1, 2):
            zh(j, 2).wait_send()


def body(fill_blocks, fill_mask, inv_diag, factor_off):
    vmem = pl.BlockSpec(memory_space=pltpu.VMEM)

    def sq(n):
        return pltpu.VMEM((n, 256, 256), F32)

    return pl.pallas_call(
        kernel,
        name="chain",
        out_shape=(
            jax.ShapeDtypeStruct((2, 128, 512), F32),
            jax.ShapeDtypeStruct((2, 64, 512), F32),
        ),
        in_specs=[pl.BlockSpec(memory_space=pl.ANY)] * 4,
        out_specs=(vmem, vmem),
        scratch_shapes=[
            pltpu.SMEM((2, 4), jnp.int32),
            pltpu.SMEM((2, 4), jnp.int32),
            pltpu.VMEM((2, 512, 512), F32),
            pltpu.VMEM((2, 64, 512), F32),
            pltpu.SemaphoreType.DMA((5,)),
            pltpu.VMEM((8, 256), jnp.int32),
            pltpu.VMEM((8, 256), jnp.int32),
            pltpu.VMEM((2, 512, 512), BF16),
            pltpu.VMEM((2, 512, 512), BF16),
            sq(2),
            pltpu.VMEM((2, 256, 512), F32),
            sq(2),
            sq(2),
            sq(2),
            sq(4),
            sq(4),
            sq(4),
            sq(4),
            sq(3),
            sq(3),
            pltpu.VMEM((256, 256), F32),
            pltpu.VMEM((256, 256), F32),
            pltpu.VMEM((256, 256), F32),
            sq(4),
            pltpu.VMEM((256, 256), F32),
            pltpu.VMEM((2, 256, 512), F32),
            pltpu.VMEM((384, 256), F32),
            pltpu.SemaphoreType.DMA((N_IDS,)),
            pltpu.SemaphoreType.DMA((N_IDS,)),
        ],
        compiler_params=pltpu.CompilerParams(
            collective_id=0, has_side_effects=True
        ),
    )(fill_blocks, fill_mask, inv_diag, factor_off)


def solution(mesh):
    torus = Mesh(mesh.devices.reshape(2, 4, 4, 2, mesh.shape["row"]), (*SEG, "row"))
    placed = (P(SEG, None), P(SEG, None), P(SEG, None, None), P(SEG, "row", None))
    return jax.shard_map(
        body,
        mesh=torus,
        in_specs=placed,
        out_specs=(P(SEG, "row", None), P(SEG, "row", None)),
        check_vma=False,
    )
```

```python
import jax
import jax.numpy as jnp
from jax import lax
from jax.experimental import pallas as pl
from jax.experimental.pallas import tpu as pltpu
from jax.sharding import Mesh
from jax.sharding import PartitionSpec as P

BLOCK = 64
SEG = ("seg_0", "seg_1", "seg_2", "seg_3")
F32 = jnp.float32
BF16 = jnp.bfloat16
N_IDS = 100

ID_IDX = 0
ID_ZL = 1
ID_ZF = 13
ID_CL = 25
ID_CA = 26
ID_YL = 27
ID_YA = 39
ID_XL = 51
ID_XA = 63
ID_ZL_LATE = 84
ID_ZF_LATE = 90
ID_RELAY = 99
ID_ZH = 75


def split(v):
    hi = v.astype(BF16)
    return hi, (v - hi.astype(F32)).astype(BF16)


def dot(a, b):
    return lax.dot_general(a, b, (((1,), (0,)), ((), ())), preferred_element_type=F32)


def mm(a, b):
    (ah, al), (bh, bl) = a, b
    return dot(ah, bh) + (dot(ah, bl) + dot(al, bh))


def sandwich(link, inner, added):
    left = mm(split(link.T), split(inner))
    return added + mm(split(left), split(link))


def kernel(
    blocks_hbm, mask_hbm, inv_hbm, fac_hbm, cov, off,
    blocks, mask, inv, fac, local, idx_out, idx_in, inv_h, inv_l, lp, fg, base, cl, ca, yl, ya, xl, xa,
    el, ea, ph, th, pb, rb, sm, gg, kk, ss, rs,
):
    h, x, y, c = (lax.axis_index(a) for a in SEG)
    r = lax.axis_index("row")
    z = 4 * h + r
    seg = ((h * 4 + x) * 4 + y) * 2 + c

    both = jnp.logical_and

    def z_at(d):
        zz = lax.rem(z + d + 8, 8)
        return {"seg_0": zz // 4, "row": lax.rem(zz, 4)}

    def seg_at(d):
        s = lax.rem(seg + d + 64, 64)
        return {
            "seg_0": s // 32,
            "seg_1": lax.rem(s // 8, 4),
            "seg_2": lax.rem(s // 2, 4),
            "seg_3": lax.rem(s, 2),
        }

    def y_at(d):
        return {"seg_2": lax.rem(y + d + 4, 4)}

    def x_at(d):
        return {"seg_1": lax.rem(x + d + 4, 4)}

    mate = {"seg_3": 1 - c}

    loads = [
        pltpu.make_async_copy(src, dst, local.at[i])
        for i, (src, dst) in enumerate((
            (blocks_hbm, blocks), (mask_hbm, mask), (fac_hbm, fac),
            (inv_hbm.at[c], inv.at[c]), (inv_hbm.at[1 - c], inv.at[1 - c]),
        ))
    ]
    for load in loads:
        load.start()

    barrier = pltpu.get_barrier_semaphore()

    def greet(who):
        pl.semaphore_signal(barrier, 1, device_id=who, device_id_type=pl.DeviceIdType.MESH)

    for who in (mate, z_at(1), z_at(-1), y_at(1), y_at(-1), x_at(1), x_at(-1)):
        greet(who)

    later = h == 1
    edge = jnp.logical_or(r == 0, r == 3)
    tail = both(both(x == 3, y == 3), c == 1)
    head = both(both(x == 0, y == 0), c == 0)
    plain_out, plain_in = jnp.logical_not(tail), jnp.logical_not(head)
    far_out = both(both(tail, h == 0), edge)
    far_in = both(both(head, later), edge)
    relay_in = both(both(head, later), jnp.logical_not(edge))
    across_half = {
        "seg_0": 1 - h, "seg_1": lax.rem(x + 1 + 2 * h, 4), "seg_2": lax.rem(y + 1 + 2 * h, 4),
        "seg_3": 1 - c, "row": 3 - r,
    }
    for cond, who in (
        (plain_in, seg_at(-1)), (far_in, across_half),
    ):

        @pl.when(cond)
        def _():
            greet(who)

    greetings = 7
    for cond in (plain_out, far_out):
        greetings = greetings + jnp.where(cond, 1, 0)

    started = []

    def copy(src, dst, number, who):
        return pltpu.make_async_remote_copy(
            src_ref=src, dst_ref=dst, send_sem=ss.at[number], recv_sem=rs.at[number],
            device_id=who, device_id_type=pl.DeviceIdType.MESH,
        )

    for load in loads[:3]:
        load.wait()

    lane = lax.broadcasted_iota(jnp.int32, (8, 256), 1)
    slot = lane // BLOCK

    def targets(panel):
        t = jnp.zeros((8, 256), jnp.int32)
        for s in range(4):
            t = jnp.where(slot == s, blocks[panel, s], t)
        return t * BLOCK + (lane - slot * BLOCK)

    idx_out[...] = targets(1)
    target_1 = targets(0)

    row_at = lax.broadcasted_iota(jnp.int32, (512, 256), 0)

    def chooser(t):
        return jnp.where(row_at == t[0:1, :], 1.0, 0.0).astype(BF16)

    def keep(panel):
        live = mask[panel, r].astype(F32)
        return jnp.where(seg * 2 + panel < 127, live, 0.0)

    def factor_rows(p):
        ih, il = split(inv[p])
        inv_h[p] = ih
        inv_l[p] = il
        fg[p, pl.ds(r * 64, 64), :] = mm(split(fac[p] * keep(p)), (ih, il))

    def local_link(p, choose):
        fh, fl = split(fg[p, pl.ds(r * 64, 64), :])
        lp[p, pl.ds(r * 64, 64), :] = dot(fh, choose) + dot(fl, choose)

    def local_base(p, choose):
        ch = dot(inv_h[p], choose)
        cl_ = dot(inv_l[p], choose)
        chh, cll = ch.astype(BF16), cl_.astype(BF16)
        cth, ctl = ch.T.astype(BF16), cl_.T.astype(BF16)
        base[p] = mm((cth, ctl), (chh, cll))

    is_a, is_b = c == 0, c == 1
    loads[3].wait()
    factor_rows(c)

    @pl.when(is_b)
    def _():
        local_link(1, chooser(target_1))

    pl.semaphore_wait(barrier, greetings)

    def begin(cond, made):
        @pl.when(cond)
        def _():
            made().start()

        started.append((cond, made))

    begin(plain_out, lambda: copy(idx_out, idx_in, ID_IDX, seg_at(1)))
    begin(far_out, lambda: copy(idx_out, idx_in, ID_IDX, across_half))
    inward = z_at(jnp.where(r == 0, 1, -1))

    @pl.when(both(head, h == 0))
    def _():
        idx_in[...] = target_1

    relay = lambda: copy(idx_in, idx_in, ID_RELAY, inward)

    def z_parts(buf, ids, p, k, up, lo, n):
        block = (r - k) if up else (r + k)
        block_in = (r - 1 - k) if up else (r + 1 + k)
        sends = jnp.logical_and(r < 3, r - k >= 0) if up else jnp.logical_and(r > 0, r + k <= 3)
        takes = (r - 1 - k >= 0) if up else (r + 1 + k <= 3)
        number = ids + p * 6 + (0 if up else 3) + k
        who = z_at(1 if up else -1)

        def made(b):
            part = buf.at[p, pl.ds(b * 64 + lo, n), :]
            return copy(part, part, number, who)

        return sends, takes, lambda: made(block), lambda: made(block_in)

    def z_send(buf, ids, p, k, lo=0, n=64, cond=None):
        for up in (True, False):
            sends, _, out, _ = z_parts(buf, ids, p, k, up, lo, n)
            if cond is not None:
                sends = both(sends, cond)

            @pl.when(sends)
            def _():
                out().start()

            started.append((sends, out))

    def z_take(buf, ids, p, k, lo=0, n=64, cond=None):
        for up in (True, False):
            _, takes, _, into = z_parts(buf, ids, p, k, up, lo, n)
            if cond is not None:
                takes = both(takes, cond)

            @pl.when(takes)
            def _():
                into().wait_recv()

    def z_next(buf, ids, p, k, lo=0, n=64, cond=None):
        z_take(buf, ids, p, k, lo, n, cond)
        if k < 2:
            z_send(buf, ids, p, k + 1, lo, n, cond)

    waits_long = both(head, later)
    units = (
        (fg, ID_ZF, 0, 0, 32, is_a), (fg, ID_ZF_LATE, 0, 32, 32, is_a),
        (lp, ID_ZL, 1, 0, 64, None),
        (lp, ID_ZL, 0, 0, 32, is_b), (lp, ID_ZL_LATE, 0, 32, 32, is_b),
    )

    def every(k):
        for buf, ids, p, lo, n, cond in units:
            z_next(buf, ids, p, k, lo, n, cond)

    for buf, ids, p, lo, n, cond in units[:2]:
        z_send(buf, ids, p, 0, lo, n, cond)
    z_send(lp, ID_ZL, 1, 0, cond=is_b)
    loads[4].wait()
    factor_rows(1 - c)

    @pl.when(is_a)
    def _():
        local_link(1, chooser(target_1))

    z_send(lp, ID_ZL, 1, 0, cond=is_a)

    @pl.when(is_b)
    def _():
        copy(idx_out, idx_in, ID_IDX, mate).wait_recv()
        local_link(0, chooser(idx_in[...]))

    for buf, ids, p, lo, n, cond in units[3:]:
        z_send(buf, ids, p, 0, lo, n, cond)
    local_base(1, chooser(target_1))
    every(0)

    @pl.when(both(is_a, plain_in))
    def _():
        copy(idx_out, idx_in, ID_IDX, mate).wait_recv()

    @pl.when(jnp.logical_not(waits_long))
    def _():
        local_base(0, chooser(idx_in[...]))

    every(1)

    @pl.when(far_in)
    def _():
        copy(idx_out, idx_in, ID_IDX, mate).wait_recv()

    begin(far_in, relay)
    for p in (0, 1):
        mine = inv[p, :, pl.ds(pl.multiple_of(r * 128, 128), 128)]
        cov[p] = mm(split(mine.T), (inv_h[p], inv_l[p]))
    every(2)

    @pl.when(relay_in)
    def _():
        relay().wait_recv()

    @pl.when(waits_long)
    def _():
        local_base(0, chooser(idx_in[...]))

    @pl.when(is_a)
    def _():
        fh, fl = split(fg[0])
        choose = chooser(idx_in[...])
        lp[0] = dot(fh, choose) + dot(fl, choose)

    z_send(fg, ID_ZF, 1, 0)
    z_send(fg, ID_ZF, 0, 0, cond=is_b)

    link_0 = split(lp[0])
    cl[c] = mm(split(lp[1]), link_0)
    cl_copy = copy(cl.at[c], cl.at[c], ID_CL, mate)
    cl_copy.start()
    ca[c] = sandwich(lp[0], base[1], base[0])
    ca_copy = copy(ca.at[c], ca.at[c], ID_CA, mate)
    ca_copy.start()
    started.append((None, cl_copy))
    started.append((None, ca_copy))

    turn = 1 - 2 * c

    def link_part(j):
        return pl.ds(c * 128 + j * 64, 64), slice(None)

    def constant_part(j):
        if j == 0:
            at = pl.ds(pl.multiple_of(c * 128, 128), 128)
            return at, at
        return pl.ds(c * 64, 64), pl.ds(128, 128)

    def ring_send(buf, ids, at, where, part):
        for way, j in ((0, 0), (1, 1), (0, 1), (1, 0)):
            piece = buf.at[at, *part(j)]
            one = copy(piece, piece, ids + way * 2 + j, where(turn if way == 0 else -turn))
            one.start()
            started.append((None, one))

    def places(at):
        return tuple(lax.rem(at + d + 4, 4) for d in (-turn, turn, 2))

    def mated(buf, place, j, number, part):
        piece = buf.at[place, *part(j)]
        one = copy(piece, piece, number, mate)
        one.start()
        started.append((None, one))
        return one

    def direct(buf, ids, at, where, part):
        behind, ahead, _ = places(at)
        mates = []
        for way, j in ((0, 0), (1, 1), (0, 1), (1, 0)):
            place = behind if way == 0 else ahead
            piece = buf.at[place, *part(j)]
            copy(piece, piece, ids + way * 2 + j, mate).wait_recv()
            if way == j:
                onward = copy(piece, piece, ids + 4 + way, where(turn if way == 0 else -turn))
                onward.start()
                started.append((None, onward))
            mates.append(mated(buf, place, j, ids + 6 + way * 2 + j, part))
        return mates

    def opposite(buf, ids, at, part):
        across = places(at)[2]
        mates = []
        for way in (0, 1):
            piece = buf.at[across, *part(way)]
            copy(piece, piece, ids + 4 + way, mate).wait_recv()
            mates.append(mated(buf, across, way, ids + 10 + way, part))
        return mates

    def done(mates):
        for one in mates:
            one.wait_recv()

    def whole(v):
        return jnp.concatenate([v[:128], jnp.concatenate([v[:128, 128:].T, v[128:, 128:]], 1)], 0)

    rows_256 = lax.broadcasted_iota(jnp.int32, (256, 256), 0)
    eye = (rows_256 == lax.broadcasted_iota(jnp.int32, (256, 256), 1)).astype(F32)

    def near_products(buf):
        rb[0] = eye
        rb[1] = buf[0]
        low = mm(split(buf[1]), split(buf[0]))
        rb[2] = low
        rb[3] = mm(split(buf[2]), split(low))

    def term(buf, place, added):
        return sandwich(rb[place], whole(buf[place]), added)

    def exclusive_links(links, at, out):
        @pl.when(at == 3)
        def _():
            out[...] = eye

        @pl.when(at < 3)
        def _():
            out[...] = links[3]

        for i in (2, 1):

            @pl.when(at < i)
            def _():
                out[...] = mm(split(out[...]), split(links[i]))

    def exclusive_constants(links, consts, at, out):
        @pl.when(at == 3)
        def _():
            out[...] = jnp.zeros((256, 256), F32)

        @pl.when(at < 3)
        def _():
            out[...] = whole(consts[3])

        for i in (2, 1):

            @pl.when(at < i)
            def _():
                out[...] = sandwich(links[i], out[...], whole(consts[i]))

    cl_copy.wait_recv()
    yl[y] = mm(split(cl[1]), split(cl[0]))
    ring_send(yl, ID_YL, y, y_at, link_part)
    ca_copy.wait_recv()
    ya[y] = sandwich(cl[0], ca[1], ca[0])
    ring_send(ya, ID_YA, y, y_at, constant_part)

    yl_mates = direct(yl, ID_YL, y, y_at, link_part)
    z_next(fg, ID_ZF, 1, 0)
    z_next(fg, ID_ZF, 0, 0, cond=is_b)
    ya_mates = direct(ya, ID_YA, y, y_at, constant_part)
    done(yl_mates)
    done(ya_mates)

    @pl.when(y == 0)
    def _():
        rb[2] = mm(split(yl[1]), split(yl[0]))
        sm[...] = sandwich(yl[0], whole(ya[1]), whole(ya[0]))

    @pl.when(y == 1)
    def _():
        low = mm(split(yl[1]), split(yl[0]))
        near = sandwich(yl[0], whole(ya[1]), whole(ya[0]))
        rb[3] = mm(split(yl[2]), split(low))
        sm[...] = sandwich(low, whole(ya[2]), near)

    @pl.when(y == 2)
    def _():
        rb[0] = eye
        sm[...] = sandwich(yl[1], sandwich(yl[2], whole(ya[3]), whole(ya[2])), whole(ya[1]))

    @pl.when(y == 3)
    def _():
        rb[1] = yl[0]
        sm[...] = sandwich(yl[2], whole(ya[3]), whole(ya[2]))

    done(opposite(yl, ID_YL, y, link_part))
    high = mm(split(yl[3]), split(yl[2]))
    low = mm(split(yl[1]), split(yl[0]))
    xl[x] = mm(split(high), split(low))
    ring_send(xl, ID_XL, x, x_at, link_part)
    z_next(fg, ID_ZF, 1, 1)

    @pl.when(y == 0)
    def _():
        sm[...] = sandwich(mm(split(yl[2]), split(rb[2])), whole(ya[3]), sm[...])

    @pl.when(y == 2)
    def _():
        sm[...] = sandwich(yl[0], sm[...], jnp.zeros((256, 256), F32))

    @pl.when(y == 3)
    def _():
        sm[...] = sandwich(mm(split(yl[1]), split(yl[0])), sm[...], whole(ya[0]))

    across = places(y)[2]
    done(opposite(ya, ID_YA, y, constant_part))
    xa[x] = term(ya, across, sm[...])
    ring_send(xa, ID_XA, x, x_at, constant_part)

    z_next(fg, ID_ZF, 0, 1, cond=is_b)
    exclusive_links(yl, y, el.at[1])
    exclusive_constants(yl, ya, y, ea.at[1])
    xl_mates = direct(xl, ID_XL, x, x_at, link_part)

    @pl.when(c == 0)
    def _():
        ea[1] = sandwich(cl[1], ea[1], ca[1])
        el[1] = mm(split(el[1]), split(cl[1]))

    ea[0] = sandwich(lp[1], ea[1], base[1])
    el[0] = mm(split(el[1]), split(lp[1]))

    xa_mates = direct(xa, ID_XA, x, x_at, constant_part)
    done(xl_mates + opposite(xl, ID_XL, x, link_part))
    sends_half = both(later, edge)
    behind, ahead, across = places(x)
    z_next(fg, ID_ZF, 1, 2)
    z_next(fg, ID_ZF, 0, 2, cond=is_b)
    done(xa_mates)

    @pl.when(sends_half)
    def _():
        near_products(xl)
        zero = jnp.zeros((256, 256), F32)
        th[...] = term(xa, behind, term(xa, ahead, term(xa, x, zero)))

    @pl.when(h == 0)
    def _():
        exclusive_links(xl, x, el.at[2])
        entry = split(el[2])
        for p in (1, 0):
            link = mm(entry, split(el[p]))
            pb[...] = link.T
            gg[p] = mm(split(link), split(fg[p]))
            kk[p * 192 : p * 192 + 128, :] = gg[p, :, pl.ds(pl.multiple_of(r * 128, 128), 128)].T
            kk[p * 192 + 128 : p * 192 + 192, :] = pb[pl.ds(r * 64, 64), :]

    done(opposite(xa, ID_XA, x, constant_part))

    hop = z_at(jnp.where(r == 0, -1, 1))

    def zh(j, kind):
        if j < 2:
            part = pl.ds(c * 128 + j * 64, 64), pl.ds(pl.multiple_of(c * 128, 128), 128)
        else:
            part = pl.ds(c * 64, 64), pl.ds(128, 128)
        piece = ph.at[*part]
        if kind == 0:
            return copy(th.at[*part], piece, ID_ZH + j, hop)
        return copy(piece, piece, ID_ZH + 3 * kind + j, inward if kind == 1 else mate)

    @pl.when(sends_half)
    def _():
        th[...] = term(xa, across, th[...])
        for j in (0, 1, 2):
            zh(j, 0).start()

    exclusive_constants(xl, xa, x, ea.at[2])

    def outputs(p):
        constant = sandwich(el[p], ea[2], ea[p])
        mine = fg[p, :, pl.ds(pl.multiple_of(r * 128, 128), 128)]
        middle = mm(split(constant), split(mine))
        pb[...] = constant
        left = jnp.concatenate([middle.T, pb[pl.ds(r * 64, 64), :]], 0)
        out = mm(split(left), split(fg[p]))
        cov[p] += out[:128]
        off[p] = out[128:]

    outputs(1)

    @pl.when(both(h == 0, edge))
    def _():
        for j in (0, 1, 2):
            zh(j, 0).wait_recv()
            zh(j, 1).start()
            zh(j, 2).start()

    outputs(0)

    @pl.when(both(h == 0, jnp.logical_not(edge)))
    def _():
        for j in (0, 1, 2):
            zh(j, 1).wait_recv()
            zh(j, 2).start()

    @pl.when(h == 0)
    def _():
        for j in (0, 1, 2):
            zh(j, 2).wait_recv()
        left = split(mm(split(kk[...]), split(whole(ph[...]))))
        for p in (0, 1):
            at = slice(p * 192, p * 192 + 192)
            out = mm((left[0][at], left[1][at]), split(gg[p]))
            cov[p] += out[:128]
            off[p] += out[128:]

    for p in (0, 1):
        off[p] = off[p] * (-mask[p, r].astype(F32))

    for sends, one in started:
        if sends is None:
            one.wait_send()
        else:

            @pl.when(sends)
            def _():
                one().wait_send()

    @pl.when(sends_half)
    def _():
        for j in (0, 1, 2):
            zh(j, 0).wait_send()

    @pl.when(jnp.logical_and(h == 0, edge))
    def _():
        for j in (0, 1, 2):
            zh(j, 1).wait_send()

    @pl.when(h == 0)
    def _():
        for j in (0, 1, 2):
            zh(j, 2).wait_send()


def body(fill_blocks, fill_mask, inv_diag, factor_off):
    vmem = pl.BlockSpec(memory_space=pltpu.VMEM)

    def sq(n):
        return pltpu.VMEM((n, 256, 256), F32)

    return pl.pallas_call(
        kernel,
        name="chain",
        out_shape=(pltpu.VMEM((2, 128, 512), F32), pltpu.VMEM((2, 64, 512), F32)),
        in_specs=[pl.BlockSpec(memory_space=pltpu.HBM)] * 4,
        out_specs=(vmem, vmem),
        scratch_shapes=[
            pltpu.SMEM((2, 4), jnp.int32),
            pltpu.SMEM((2, 4), jnp.int32),
            pltpu.VMEM((2, 512, 512), F32),
            pltpu.VMEM((2, 64, 512), F32),
            pltpu.SemaphoreType.DMA((5,)),
            pltpu.VMEM((8, 256), jnp.int32),
            pltpu.VMEM((8, 256), jnp.int32),
            pltpu.VMEM((2, 512, 512), BF16),
            pltpu.VMEM((2, 512, 512), BF16),
            sq(2),
            pltpu.VMEM((2, 256, 512), F32),
            sq(2),
            sq(2),
            sq(2),
            sq(4),
            sq(4),
            sq(4),
            sq(4),
            sq(3),
            sq(3),
            pltpu.VMEM((256, 256), F32),
            pltpu.VMEM((256, 256), F32),
            pltpu.VMEM((256, 256), F32),
            sq(4),
            pltpu.VMEM((256, 256), F32),
            pltpu.VMEM((2, 256, 512), F32),
            pltpu.VMEM((384, 256), F32),
            pltpu.SemaphoreType.DMA((N_IDS,)),
            pltpu.SemaphoreType.DMA((N_IDS,)),
        ],
        compiler_params=pltpu.CompilerParams(
            collective_id=0, has_side_effects=True
        ),
    )(fill_blocks, fill_mask, inv_diag, factor_off)


def solution(mesh):
    torus = Mesh(mesh.devices.reshape(2, 4, 4, 2, mesh.shape["row"]), (*SEG, "row"))
    placed = (P(SEG, None), P(SEG, None), P(SEG, None, None), P(SEG, "row", None))
    return jax.shard_map(
        body,
        mesh=torus,
        in_specs=placed,
        out_specs=(P(SEG, "row", None), P(SEG, "row", None)),
        check_vma=False,
    )
```

```python
import jax
import jax.numpy as jnp
from jax import lax
from jax.experimental import pallas as pl
from jax.experimental.pallas import tpu as pltpu
from jax.sharding import Mesh
from jax.sharding import PartitionSpec as P

BLOCK = 64
SEG = ("seg_0", "seg_1", "seg_2", "seg_3")
F32 = jnp.float32
BF16 = jnp.bfloat16
N_IDS = 100

ID_IDX = 0
ID_ZL = 1
ID_ZF = 13
ID_CL = 25
ID_CA = 26
ID_YL = 27
ID_YA = 39
ID_XL = 51
ID_XA = 63
ID_ZL_LATE = 84
ID_ZF_LATE = 90
ID_RELAY = 99
ID_ZH = 75


def split(v):
    hi = v.astype(BF16)
    return hi, (v - hi.astype(F32)).astype(BF16)


def dot(a, b):
    return lax.dot_general(a, b, (((1,), (0,)), ((), ())), preferred_element_type=F32)


def mm(a, b):
    (ah, al), (bh, bl) = a, b
    return dot(ah, bh) + (dot(ah, bl) + dot(al, bh))


def sandwich(link, inner, added):
    left = mm(split(link.T), split(inner))
    return added + mm(split(left), split(link))


def kernel(
    blocks_hbm, mask_hbm, inv_hbm, fac_hbm, cov, off,
    blocks, mask, inv, fac, local, idx_out, idx_in, inv_h, inv_l, lp, fg, base, cl, ca, yl, ya, xl, xa,
    el, ea, ph, th, pb, rb, sm, gg, kk, ss, rs,
):
    h, x, y, c = (lax.axis_index(a) for a in SEG)
    r = lax.axis_index("row")
    z = 4 * h + r
    seg = ((h * 4 + x) * 4 + y) * 2 + c

    both = jnp.logical_and

    def z_at(d):
        zz = lax.rem(z + d + 8, 8)
        return {"seg_0": zz // 4, "row": lax.rem(zz, 4)}

    def seg_at(d):
        s = lax.rem(seg + d + 64, 64)
        return {
            "seg_0": s // 32,
            "seg_1": lax.rem(s // 8, 4),
            "seg_2": lax.rem(s // 2, 4),
            "seg_3": lax.rem(s, 2),
        }

    def y_at(d):
        return {"seg_2": lax.rem(y + d + 4, 4)}

    def x_at(d):
        return {"seg_1": lax.rem(x + d + 4, 4)}

    mate = {"seg_3": 1 - c}

    loads = [
        pltpu.make_async_copy(src, dst, local.at[i])
        for i, (src, dst) in enumerate((
            (blocks_hbm, blocks), (mask_hbm, mask), (fac_hbm, fac),
            (inv_hbm.at[c], inv.at[c]), (inv_hbm.at[1 - c], inv.at[1 - c]),
        ))
    ]
    for load in loads:
        load.start()

    barrier = pltpu.get_barrier_semaphore()

    def greet(who):
        pl.semaphore_signal(barrier, 1, device_id=who, device_id_type=pl.DeviceIdType.MESH)

    for who in (mate, z_at(1), z_at(-1), y_at(1), y_at(-1), x_at(1), x_at(-1)):
        greet(who)

    later = h == 1
    edge = jnp.logical_or(r == 0, r == 3)
    tail = both(both(x == 3, y == 3), c == 1)
    head = both(both(x == 0, y == 0), c == 0)
    plain_out, plain_in = jnp.logical_not(tail), jnp.logical_not(head)
    far_out = both(both(tail, h == 0), edge)
    far_in = both(both(head, later), edge)
    relay_in = both(both(head, later), jnp.logical_not(edge))
    across_half = {
        "seg_0": 1 - h, "seg_1": lax.rem(x + 1 + 2 * h, 4), "seg_2": lax.rem(y + 1 + 2 * h, 4),
        "seg_3": 1 - c, "row": 3 - r,
    }
    for cond, who in (
        (plain_in, seg_at(-1)), (far_in, across_half),
    ):

        @pl.when(cond)
        def _():
            greet(who)

    greetings = 7
    for cond in (plain_out, far_out):
        greetings = greetings + jnp.where(cond, 1, 0)

    started = []

    def copy(src, dst, number, who):
        return pltpu.make_async_remote_copy(
            src_ref=src, dst_ref=dst, send_sem=ss.at[number], recv_sem=rs.at[number],
            device_id=who, device_id_type=pl.DeviceIdType.MESH,
        )

    for load in loads[:3]:
        load.wait()

    lane = lax.broadcasted_iota(jnp.int32, (8, 256), 1)
    slot = lane // BLOCK

    def targets(panel):
        t = jnp.zeros((8, 256), jnp.int32)
        for s in range(4):
            t = jnp.where(slot == s, blocks[panel, s], t)
        return t * BLOCK + (lane - slot * BLOCK)

    idx_out[...] = targets(1)
    target_1 = targets(0)

    row_at = lax.broadcasted_iota(jnp.int32, (512, 256), 0)

    def chooser(t):
        return jnp.where(row_at == t[0:1, :], 1.0, 0.0).astype(BF16)

    def keep(panel):
        live = mask[panel, r].astype(F32)
        return jnp.where(seg * 2 + panel < 127, live, 0.0)

    def factor_rows(p):
        ih, il = split(inv[p])
        inv_h[p] = ih
        inv_l[p] = il
        fg[p, pl.ds(r * 64, 64), :] = mm(split(fac[p] * keep(p)), (ih, il))

    def local_link(p, choose):
        fh, fl = split(fg[p, pl.ds(r * 64, 64), :])
        lp[p, pl.ds(r * 64, 64), :] = dot(fh, choose) + dot(fl, choose)

    def local_base(p, choose):
        ch = dot(inv_h[p], choose)
        cl_ = dot(inv_l[p], choose)
        chh, cll = ch.astype(BF16), cl_.astype(BF16)
        cth, ctl = ch.T.astype(BF16), cl_.T.astype(BF16)
        base[p] = mm((cth, ctl), (chh, cll))

    is_a, is_b = c == 0, c == 1
    loads[3].wait()
    factor_rows(c)

    @pl.when(is_b)
    def _():
        local_link(1, chooser(target_1))

    pl.semaphore_wait(barrier, greetings)

    def begin(cond, made):
        @pl.when(cond)
        def _():
            made().start()

        started.append((cond, made))

    begin(plain_out, lambda: copy(idx_out, idx_in, ID_IDX, seg_at(1)))
    begin(far_out, lambda: copy(idx_out, idx_in, ID_IDX, across_half))
    inward = z_at(jnp.where(r == 0, 1, -1))

    @pl.when(both(head, h == 0))
    def _():
        idx_in[...] = target_1

    relay = lambda: copy(idx_in, idx_in, ID_RELAY, inward)

    def z_parts(buf, ids, p, k, up, lo, n):
        block = (r - k) if up else (r + k)
        block_in = (r - 1 - k) if up else (r + 1 + k)
        sends = jnp.logical_and(r < 3, r - k >= 0) if up else jnp.logical_and(r > 0, r + k <= 3)
        takes = (r - 1 - k >= 0) if up else (r + 1 + k <= 3)
        number = ids + p * 6 + (0 if up else 3) + k
        who = z_at(1 if up else -1)

        def made(b):
            part = buf.at[p, pl.ds(b * 64 + lo, n), :]
            return copy(part, part, number, who)

        return sends, takes, lambda: made(block), lambda: made(block_in)

    def z_send(buf, ids, p, k, lo=0, n=64, cond=None):
        for up in (True, False):
            sends, _, out, _ = z_parts(buf, ids, p, k, up, lo, n)
            if cond is not None:
                sends = both(sends, cond)

            @pl.when(sends)
            def _():
                out().start()

            started.append((sends, out))

    def z_take(buf, ids, p, k, lo=0, n=64, cond=None):
        for up in (True, False):
            _, takes, _, into = z_parts(buf, ids, p, k, up, lo, n)
            if cond is not None:
                takes = both(takes, cond)

            @pl.when(takes)
            def _():
                into().wait_recv()

    def z_next(buf, ids, p, k, lo=0, n=64, cond=None):
        z_take(buf, ids, p, k, lo, n, cond)
        if k < 2:
            z_send(buf, ids, p, k + 1, lo, n, cond)

    waits_long = both(head, later)
    units = (
        (fg, ID_ZF, 0, 0, 32, is_a), (fg, ID_ZF_LATE, 0, 32, 32, is_a),
        (lp, ID_ZL, 1, 0, 64, None),
        (lp, ID_ZL, 0, 0, 32, is_b), (lp, ID_ZL_LATE, 0, 32, 32, is_b),
    )

    def every(k):
        for buf, ids, p, lo, n, cond in units:
            z_next(buf, ids, p, k, lo, n, cond)

    for buf, ids, p, lo, n, cond in units[:2]:
        z_send(buf, ids, p, 0, lo, n, cond)
    z_send(lp, ID_ZL, 1, 0, cond=is_b)
    loads[4].wait()
    factor_rows(1 - c)

    @pl.when(is_a)
    def _():
        local_link(1, chooser(target_1))

    z_send(lp, ID_ZL, 1, 0, cond=is_a)

    @pl.when(is_b)
    def _():
        copy(idx_out, idx_in, ID_IDX, mate).wait_recv()
        local_link(0, chooser(idx_in[...]))

    for buf, ids, p, lo, n, cond in units[3:]:
        z_send(buf, ids, p, 0, lo, n, cond)
    local_base(1, chooser(target_1))
    every(0)

    @pl.when(both(is_a, plain_in))
    def _():
        copy(idx_out, idx_in, ID_IDX, mate).wait_recv()

    @pl.when(jnp.logical_not(waits_long))
    def _():
        local_base(0, chooser(idx_in[...]))

    every(1)

    @pl.when(far_in)
    def _():
        copy(idx_out, idx_in, ID_IDX, mate).wait_recv()

    begin(far_in, relay)
    for p in (0, 1):
        mine = inv[p, :, pl.ds(pl.multiple_of(r * 128, 128), 128)]
        cov[p] = mm(split(mine.T), (inv_h[p], inv_l[p]))
    every(2)

    @pl.when(relay_in)
    def _():
        relay().wait_recv()

    @pl.when(waits_long)
    def _():
        local_base(0, chooser(idx_in[...]))

    @pl.when(is_a)
    def _():
        fh, fl = split(fg[0])
        choose = chooser(idx_in[...])
        lp[0] = dot(fh, choose) + dot(fl, choose)

    z_send(fg, ID_ZF, 1, 0)
    z_send(fg, ID_ZF, 0, 0, cond=is_b)

    link_0 = split(lp[0])
    cl[c] = mm(split(lp[1]), link_0)
    cl_copy = copy(cl.at[c], cl.at[c], ID_CL, mate)
    cl_copy.start()
    ca[c] = sandwich(lp[0], base[1], base[0])
    ca_copy = copy(ca.at[c], ca.at[c], ID_CA, mate)
    ca_copy.start()
    started.append((None, cl_copy))
    started.append((None, ca_copy))

    turn = 1 - 2 * c

    def link_part(j):
        return pl.ds(c * 128 + j * 64, 64), slice(None)

    def constant_part(j):
        if j == 0:
            at = pl.ds(pl.multiple_of(c * 128, 128), 128)
            return at, at
        return pl.ds(c * 64, 64), pl.ds(128, 128)

    def ring_send(buf, ids, at, where, part):
        for way, j in ((0, 0), (1, 1), (0, 1), (1, 0)):
            piece = buf.at[at, *part(j)]
            one = copy(piece, piece, ids + way * 2 + j, where(turn if way == 0 else -turn))
            one.start()
            started.append((None, one))

    def places(at):
        return tuple(lax.rem(at + d + 4, 4) for d in (-turn, turn, 2))

    def mated(buf, place, j, number, part):
        piece = buf.at[place, *part(j)]
        one = copy(piece, piece, number, mate)
        one.start()
        started.append((None, one))
        return one

    def direct(buf, ids, at, where, part):
        behind, ahead, _ = places(at)
        mates = []
        for way, j in ((0, 0), (1, 1), (0, 1), (1, 0)):
            place = behind if way == 0 else ahead
            piece = buf.at[place, *part(j)]
            copy(piece, piece, ids + way * 2 + j, mate).wait_recv()
            if way == j:
                onward = copy(piece, piece, ids + 4 + way, where(turn if way == 0 else -turn))
                onward.start()
                started.append((None, onward))
            mates.append(mated(buf, place, j, ids + 6 + way * 2 + j, part))
        return mates

    def opposite(buf, ids, at, part):
        across = places(at)[2]
        mates = []
        for way in (0, 1):
            piece = buf.at[across, *part(way)]
            copy(piece, piece, ids + 4 + way, mate).wait_recv()
            mates.append(mated(buf, across, way, ids + 10 + way, part))
        return mates

    def done(mates):
        for one in mates:
            one.wait_recv()

    def whole(v):
        return jnp.concatenate([v[:128], jnp.concatenate([v[:128, 128:].T, v[128:, 128:]], 1)], 0)

    rows_256 = lax.broadcasted_iota(jnp.int32, (256, 256), 0)
    eye = (rows_256 == lax.broadcasted_iota(jnp.int32, (256, 256), 1)).astype(F32)

    def near_products(buf):
        rb[0] = eye
        rb[1] = buf[0]
        low = mm(split(buf[1]), split(buf[0]))
        rb[2] = low
        rb[3] = mm(split(buf[2]), split(low))

    def term(buf, place, added):
        return sandwich(rb[place], whole(buf[place]), added)

    def exclusive_links(links, at, out):
        @pl.when(at == 3)
        def _():
            out[...] = eye

        @pl.when(at < 3)
        def _():
            out[...] = links[3]

        for i in (2, 1):

            @pl.when(at < i)
            def _():
                out[...] = mm(split(out[...]), split(links[i]))

    def exclusive_constants(links, consts, at, out):
        @pl.when(at == 3)
        def _():
            out[...] = jnp.zeros((256, 256), F32)

        @pl.when(at < 3)
        def _():
            out[...] = whole(consts[3])

        for i in (2, 1):

            @pl.when(at < i)
            def _():
                out[...] = sandwich(links[i], out[...], whole(consts[i]))

    cl_copy.wait_recv()
    yl[y] = mm(split(cl[1]), split(cl[0]))
    ring_send(yl, ID_YL, y, y_at, link_part)
    ca_copy.wait_recv()
    ya[y] = sandwich(cl[0], ca[1], ca[0])
    ring_send(ya, ID_YA, y, y_at, constant_part)

    yl_mates = direct(yl, ID_YL, y, y_at, link_part)
    z_next(fg, ID_ZF, 1, 0)
    z_next(fg, ID_ZF, 0, 0, cond=is_b)
    ya_mates = direct(ya, ID_YA, y, y_at, constant_part)
    done(yl_mates)
    done(ya_mates)

    @pl.when(y == 0)
    def _():
        rb[2] = mm(split(yl[1]), split(yl[0]))
        sm[...] = sandwich(yl[0], whole(ya[1]), whole(ya[0]))

    @pl.when(y == 1)
    def _():
        low = mm(split(yl[1]), split(yl[0]))
        near = sandwich(yl[0], whole(ya[1]), whole(ya[0]))
        rb[3] = mm(split(yl[2]), split(low))
        sm[...] = sandwich(low, whole(ya[2]), near)

    @pl.when(y == 2)
    def _():
        rb[0] = eye
        sm[...] = sandwich(yl[1], sandwich(yl[2], whole(ya[3]), whole(ya[2])), whole(ya[1]))

    @pl.when(y == 3)
    def _():
        rb[1] = yl[0]
        sm[...] = sandwich(yl[2], whole(ya[3]), whole(ya[2]))

    done(opposite(yl, ID_YL, y, link_part))
    high = mm(split(yl[3]), split(yl[2]))
    low = mm(split(yl[1]), split(yl[0]))
    xl[x] = mm(split(high), split(low))
    ring_send(xl, ID_XL, x, x_at, link_part)
    z_next(fg, ID_ZF, 1, 1)

    @pl.when(y == 0)
    def _():
        sm[...] = sandwich(mm(split(yl[2]), split(rb[2])), whole(ya[3]), sm[...])

    @pl.when(y == 2)
    def _():
        sm[...] = sandwich(yl[0], sm[...], jnp.zeros((256, 256), F32))

    @pl.when(y == 3)
    def _():
        sm[...] = sandwich(mm(split(yl[1]), split(yl[0])), sm[...], whole(ya[0]))

    across = places(y)[2]
    done(opposite(ya, ID_YA, y, constant_part))
    xa[x] = term(ya, across, sm[...])
    ring_send(xa, ID_XA, x, x_at, constant_part)

    z_next(fg, ID_ZF, 0, 1, cond=is_b)
    exclusive_links(yl, y, el.at[1])
    exclusive_constants(yl, ya, y, ea.at[1])
    xl_mates = direct(xl, ID_XL, x, x_at, link_part)

    @pl.when(c == 0)
    def _():
        ea[1] = sandwich(cl[1], ea[1], ca[1])
        el[1] = mm(split(el[1]), split(cl[1]))

    ea[0] = sandwich(lp[1], ea[1], base[1])
    el[0] = mm(split(el[1]), split(lp[1]))

    xa_mates = direct(xa, ID_XA, x, x_at, constant_part)
    done(xl_mates + opposite(xl, ID_XL, x, link_part))
    sends_half = both(later, edge)
    behind, ahead, across = places(x)
    z_next(fg, ID_ZF, 1, 2)
    z_next(fg, ID_ZF, 0, 2, cond=is_b)
    done(xa_mates)

    @pl.when(sends_half)
    def _():
        near_products(xl)
        zero = jnp.zeros((256, 256), F32)
        th[...] = term(xa, behind, term(xa, ahead, term(xa, x, zero)))

    @pl.when(h == 0)
    def _():
        exclusive_links(xl, x, el.at[2])
        entry = split(el[2])
        for p in (1, 0):
            link = mm(entry, split(el[p]))
            pb[...] = link.T
            gg[p] = mm(split(link), split(fg[p]))
            kk[p * 192 : p * 192 + 128, :] = gg[p, :, pl.ds(pl.multiple_of(r * 128, 128), 128)].T
            kk[p * 192 + 128 : p * 192 + 192, :] = pb[pl.ds(r * 64, 64), :]

    done(opposite(xa, ID_XA, x, constant_part))

    hop = z_at(jnp.where(r == 0, -1, 1))

    def zh(j, kind):
        if j < 2:
            part = pl.ds(c * 128 + j * 64, 64), pl.ds(pl.multiple_of(c * 128, 128), 128)
        else:
            part = pl.ds(c * 64, 64), pl.ds(128, 128)
        piece = ph.at[*part]
        if kind == 0:
            return copy(th.at[*part], piece, ID_ZH + j, hop)
        return copy(piece, piece, ID_ZH + 3 * kind + j, inward if kind == 1 else mate)

    @pl.when(sends_half)
    def _():
        th[...] = term(xa, across, th[...])
        for j in (0, 1, 2):
            zh(j, 0).start()

    exclusive_constants(xl, xa, x, ea.at[2])

    def outputs(p):
        constant = sandwich(el[p], ea[2], ea[p])
        mine = fg[p, :, pl.ds(pl.multiple_of(r * 128, 128), 128)]
        middle = mm(split(constant), split(mine))
        pb[...] = constant
        left = jnp.concatenate([middle.T, pb[pl.ds(r * 64, 64), :]], 0)
        out = mm(split(left), split(fg[p]))
        cov[p] += out[:128]
        off[p] = out[128:]

    outputs(1)

    @pl.when(both(h == 0, edge))
    def _():
        for j in (0, 1, 2):
            zh(j, 0).wait_recv()
            zh(j, 1).start()
            zh(j, 2).start()

    outputs(0)

    @pl.when(both(h == 0, jnp.logical_not(edge)))
    def _():
        for j in (0, 1, 2):
            zh(j, 1).wait_recv()
            zh(j, 2).start()

    @pl.when(h == 0)
    def _():
        for j in (0, 1, 2):
            zh(j, 2).wait_recv()
        left = split(mm(split(kk[...]), split(whole(ph[...]))))
        for p in (0, 1):
            at = slice(p * 192, p * 192 + 192)
            out = mm((left[0][at], left[1][at]), split(gg[p]))
            cov[p] += out[:128]
            off[p] += out[128:]

    for p in (0, 1):
        off[p] = off[p] * (-mask[p, r].astype(F32))

    for sends, one in started:
        if sends is None:
            one.wait_send()
        else:

            @pl.when(sends)
            def _():
                one().wait_send()

    @pl.when(sends_half)
    def _():
        for j in (0, 1, 2):
            zh(j, 0).wait_send()

    @pl.when(jnp.logical_and(h == 0, edge))
    def _():
        for j in (0, 1, 2):
            zh(j, 1).wait_send()

    @pl.when(h == 0)
    def _():
        for j in (0, 1, 2):
            zh(j, 2).wait_send()


def put_out(cov, off, cov_out, off_out, sems):
    copies = (
        pltpu.make_async_copy(cov, cov_out, sems.at[0]),
        pltpu.make_async_copy(off, off_out, sems.at[1]),
    )
    for one in copies:
        one.start()
    for one in copies:
        one.wait()


def body(fill_blocks, fill_mask, inv_diag, factor_off):
    vmem = pl.BlockSpec(memory_space=pltpu.VMEM)

    def sq(n):
        return pltpu.VMEM((n, 256, 256), F32)

    results = pl.pallas_call(
        kernel,
        name="chain",
        out_shape=(pltpu.VMEM((2, 128, 512), F32), pltpu.VMEM((2, 64, 512), F32)),
        in_specs=[pl.BlockSpec(memory_space=pltpu.HBM)] * 4,
        out_specs=(vmem, vmem),
        scratch_shapes=[
            pltpu.SMEM((2, 4), jnp.int32),
            pltpu.SMEM((2, 4), jnp.int32),
            pltpu.VMEM((2, 512, 512), F32),
            pltpu.VMEM((2, 64, 512), F32),
            pltpu.SemaphoreType.DMA((5,)),
            pltpu.VMEM((8, 256), jnp.int32),
            pltpu.VMEM((8, 256), jnp.int32),
            pltpu.VMEM((2, 512, 512), BF16),
            pltpu.VMEM((2, 512, 512), BF16),
            sq(2),
            pltpu.VMEM((2, 256, 512), F32),
            sq(2),
            sq(2),
            sq(2),
            sq(4),
            sq(4),
            sq(4),
            sq(4),
            sq(3),
            sq(3),
            pltpu.VMEM((256, 256), F32),
            pltpu.VMEM((256, 256), F32),
            pltpu.VMEM((256, 256), F32),
            sq(4),
            pltpu.VMEM((256, 256), F32),
            pltpu.VMEM((2, 256, 512), F32),
            pltpu.VMEM((384, 256), F32),
            pltpu.SemaphoreType.DMA((N_IDS,)),
            pltpu.SemaphoreType.DMA((N_IDS,)),
        ],
        compiler_params=pltpu.CompilerParams(
            collective_id=0, has_side_effects=True
        ),
    )(fill_blocks, fill_mask, inv_diag, factor_off)
    hbm = pl.BlockSpec(memory_space=pltpu.HBM)
    return pl.pallas_call(
        put_out,
        name="put_out",
        out_shape=(
            jax.ShapeDtypeStruct((2, 128, 512), F32),
            jax.ShapeDtypeStruct((2, 64, 512), F32),
        ),
        in_specs=[vmem, vmem],
        out_specs=(hbm, hbm),
        scratch_shapes=[pltpu.SemaphoreType.DMA((2,))],
        compiler_params=pltpu.CompilerParams(vmem_limit_bytes=4 << 20),
    )(*results)


def solution(mesh):
    torus = Mesh(mesh.devices.reshape(2, 4, 4, 2, mesh.shape["row"]), (*SEG, "row"))
    placed = (P(SEG, None), P(SEG, None), P(SEG, None, None), P(SEG, "row", None))
    return jax.shard_map(
        body,
        mesh=torus,
        in_specs=placed,
        out_specs=(P(SEG, "row", None), P(SEG, "row", None)),
        check_vma=False,
    )
```

```python
import jax
import jax.numpy as jnp
from jax import lax
from jax.experimental import pallas as pl
from jax.experimental.pallas import tpu as pltpu
from jax.sharding import Mesh
from jax.sharding import PartitionSpec as P

BLOCK = 64
SEG = ("seg_0", "seg_1", "seg_2", "seg_3")
F32 = jnp.float32
BF16 = jnp.bfloat16
N_IDS = 100

ID_IDX = 0
ID_ZL = 1
ID_ZF = 13
ID_CL = 25
ID_CA = 26
ID_YL = 27
ID_YA = 39
ID_XL = 51
ID_XA = 63
ID_ZL_LATE = 84
ID_ZF_LATE = 90
ID_RELAY = 99
ID_ZH = 75


def split(v):
    hi = v.astype(BF16)
    return hi, (v - hi.astype(F32)).astype(BF16)


def dot(a, b):
    return lax.dot_general(a, b, (((1,), (0,)), ((), ())), preferred_element_type=F32)


def mm(a, b):
    (ah, al), (bh, bl) = a, b
    return dot(ah, bh) + (dot(ah, bl) + dot(al, bh))


def sandwich(link, inner, added):
    left = mm(split(link.T), split(inner))
    return added + mm(split(left), split(link))


def kernel(
    blocks_hbm, mask_hbm, inv_hbm, fac_hbm, cov, off,
    blocks, mask, inv, fac, local, idx_out, idx_in, inv_h, inv_l, lp, fg, base, cl, ca, yl, ya, xl, xa,
    el, ea, ph, th, pb, rb, sm, gg, kk, ss, rs,
):
    h, x, y, c = (lax.axis_index(a) for a in SEG)
    r = lax.axis_index("row")
    z = 4 * h + r
    seg = ((h * 4 + x) * 4 + y) * 2 + c

    both = jnp.logical_and

    def z_at(d):
        zz = lax.rem(z + d + 8, 8)
        return {"seg_0": zz // 4, "row": lax.rem(zz, 4)}

    def seg_at(d):
        s = lax.rem(seg + d + 64, 64)
        return {
            "seg_0": s // 32,
            "seg_1": lax.rem(s // 8, 4),
            "seg_2": lax.rem(s // 2, 4),
            "seg_3": lax.rem(s, 2),
        }

    def y_at(d):
        return {"seg_2": lax.rem(y + d + 4, 4)}

    def x_at(d):
        return {"seg_1": lax.rem(x + d + 4, 4)}

    mate = {"seg_3": 1 - c}

    loads = [
        pltpu.make_async_copy(src, dst, local.at[i])
        for i, (src, dst) in enumerate((
            (blocks_hbm, blocks), (mask_hbm, mask), (fac_hbm, fac),
            (inv_hbm.at[c], inv.at[c]), (inv_hbm.at[1 - c], inv.at[1 - c]),
        ))
    ]
    for load in loads:
        load.start()

    barrier = pltpu.get_barrier_semaphore()

    def greet(who):
        pl.semaphore_signal(barrier, 1, device_id=who, device_id_type=pl.DeviceIdType.MESH)

    for who in (mate, z_at(1), z_at(-1), y_at(1), y_at(-1), x_at(1), x_at(-1)):
        greet(who)

    later = h == 1
    edge = jnp.logical_or(r == 0, r == 3)
    tail = both(both(x == 3, y == 3), c == 1)
    head = both(both(x == 0, y == 0), c == 0)
    plain_out, plain_in = jnp.logical_not(tail), jnp.logical_not(head)
    far_out = both(both(tail, h == 0), edge)
    far_in = both(both(head, later), edge)
    relay_in = both(both(head, later), jnp.logical_not(edge))
    across_half = {
        "seg_0": 1 - h, "seg_1": lax.rem(x + 1 + 2 * h, 4), "seg_2": lax.rem(y + 1 + 2 * h, 4),
        "seg_3": 1 - c, "row": 3 - r,
    }
    for cond, who in (
        (plain_in, seg_at(-1)), (far_in, across_half),
    ):

        @pl.when(cond)
        def _():
            greet(who)

    greetings = 7
    for cond in (plain_out, far_out):
        greetings = greetings + jnp.where(cond, 1, 0)

    started = []

    def copy(src, dst, number, who):
        return pltpu.make_async_remote_copy(
            src_ref=src, dst_ref=dst, send_sem=ss.at[number], recv_sem=rs.at[number],
            device_id=who, device_id_type=pl.DeviceIdType.MESH,
        )

    for load in loads[:3]:
        load.wait()

    lane = lax.broadcasted_iota(jnp.int32, (8, 256), 1)
    slot = lane // BLOCK

    def targets(panel):
        t = jnp.zeros((8, 256), jnp.int32)
        for s in range(4):
            t = jnp.where(slot == s, blocks[panel, s], t)
        return t * BLOCK + (lane - slot * BLOCK)

    idx_out[...] = targets(1)
    target_1 = targets(0)

    row_at = lax.broadcasted_iota(jnp.int32, (512, 256), 0)

    def chooser(t):
        return jnp.where(row_at == t[0:1, :], 1.0, 0.0).astype(BF16)

    def keep(panel):
        live = mask[panel, r].astype(F32)
        return jnp.where(seg * 2 + panel < 127, live, 0.0)

    def factor_rows(p):
        ih, il = split(inv[p])
        inv_h[p] = ih
        inv_l[p] = il
        fg[p, pl.ds(r * 64, 64), :] = mm(split(fac[p] * keep(p)), (ih, il))

    def local_link(p, choose):
        fh, fl = split(fg[p, pl.ds(r * 64, 64), :])
        lp[p, pl.ds(r * 64, 64), :] = dot(fh, choose) + dot(fl, choose)

    def local_base(p, choose):
        ch = dot(inv_h[p], choose)
        cl_ = dot(inv_l[p], choose)
        chh, cll = ch.astype(BF16), cl_.astype(BF16)
        cth, ctl = ch.T.astype(BF16), cl_.T.astype(BF16)
        base[p] = mm((cth, ctl), (chh, cll))

    is_a, is_b = c == 0, c == 1
    loads[3].wait()
    factor_rows(c)

    @pl.when(is_b)
    def _():
        local_link(1, chooser(target_1))

    pl.semaphore_wait(barrier, greetings)

    def begin(cond, made):
        @pl.when(cond)
        def _():
            made().start()

        started.append((cond, made))

    begin(plain_out, lambda: copy(idx_out, idx_in, ID_IDX, seg_at(1)))
    begin(far_out, lambda: copy(idx_out, idx_in, ID_IDX, across_half))
    inward = z_at(jnp.where(r == 0, 1, -1))

    @pl.when(both(head, h == 0))
    def _():
        idx_in[...] = target_1

    relay = lambda: copy(idx_in, idx_in, ID_RELAY, inward)

    def z_parts(buf, ids, p, k, up, lo, n):
        block = (r - k) if up else (r + k)
        block_in = (r - 1 - k) if up else (r + 1 + k)
        sends = jnp.logical_and(r < 3, r - k >= 0) if up else jnp.logical_and(r > 0, r + k <= 3)
        takes = (r - 1 - k >= 0) if up else (r + 1 + k <= 3)
        number = ids + p * 6 + (0 if up else 3) + k
        who = z_at(1 if up else -1)

        def made(b):
            part = buf.at[p, pl.ds(b * 64 + lo, n), :]
            return copy(part, part, number, who)

        return sends, takes, lambda: made(block), lambda: made(block_in)

    def z_send(buf, ids, p, k, lo=0, n=64, cond=None):
        for up in (True, False):
            sends, _, out, _ = z_parts(buf, ids, p, k, up, lo, n)
            if cond is not None:
                sends = both(sends, cond)

            @pl.when(sends)
            def _():
                out().start()

            started.append((sends, out))

    def z_take(buf, ids, p, k, lo=0, n=64, cond=None):
        for up in (True, False):
            _, takes, _, into = z_parts(buf, ids, p, k, up, lo, n)
            if cond is not None:
                takes = both(takes, cond)

            @pl.when(takes)
            def _():
                into().wait_recv()

    def z_next(buf, ids, p, k, lo=0, n=64, cond=None):
        z_take(buf, ids, p, k, lo, n, cond)
        if k < 2:
            z_send(buf, ids, p, k + 1, lo, n, cond)

    waits_long = both(head, later)
    units = (
        (fg, ID_ZF, 0, 0, 32, is_a), (fg, ID_ZF_LATE, 0, 32, 32, is_a),
        (lp, ID_ZL, 1, 0, 64, None),
        (lp, ID_ZL, 0, 0, 32, is_b), (lp, ID_ZL_LATE, 0, 32, 32, is_b),
    )

    def every(k):
        for buf, ids, p, lo, n, cond in units:
            z_next(buf, ids, p, k, lo, n, cond)

    for buf, ids, p, lo, n, cond in units[:2]:
        z_send(buf, ids, p, 0, lo, n, cond)
    z_send(lp, ID_ZL, 1, 0, cond=is_b)
    loads[4].wait()
    factor_rows(1 - c)

    @pl.when(is_a)
    def _():
        local_link(1, chooser(target_1))

    z_send(lp, ID_ZL, 1, 0, cond=is_a)

    @pl.when(is_b)
    def _():
        copy(idx_out, idx_in, ID_IDX, mate).wait_recv()
        local_link(0, chooser(idx_in[...]))

    for buf, ids, p, lo, n, cond in units[3:]:
        z_send(buf, ids, p, 0, lo, n, cond)
    local_base(1, chooser(target_1))
    every(0)

    @pl.when(both(is_a, plain_in))
    def _():
        copy(idx_out, idx_in, ID_IDX, mate).wait_recv()

    @pl.when(jnp.logical_not(waits_long))
    def _():
        local_base(0, chooser(idx_in[...]))

    every(1)

    @pl.when(far_in)
    def _():
        copy(idx_out, idx_in, ID_IDX, mate).wait_recv()

    begin(far_in, relay)
    for p in (0, 1):
        mine = inv[p, :, pl.ds(pl.multiple_of(r * 128, 128), 128)]
        cov[p] = mm(split(mine.T), (inv_h[p], inv_l[p]))
    every(2)

    @pl.when(relay_in)
    def _():
        relay().wait_recv()

    @pl.when(waits_long)
    def _():
        local_base(0, chooser(idx_in[...]))

    @pl.when(is_a)
    def _():
        fh, fl = split(fg[0])
        choose = chooser(idx_in[...])
        lp[0] = dot(fh, choose) + dot(fl, choose)

    z_send(fg, ID_ZF, 1, 0)
    z_send(fg, ID_ZF, 0, 0, cond=is_b)

    link_0 = split(lp[0])
    cl[c] = mm(split(lp[1]), link_0)
    cl_copy = copy(cl.at[c], cl.at[c], ID_CL, mate)
    cl_copy.start()
    ca[c] = sandwich(lp[0], base[1], base[0])
    ca_copy = copy(ca.at[c], ca.at[c], ID_CA, mate)
    ca_copy.start()
    started.append((None, cl_copy))
    started.append((None, ca_copy))

    turn = 1 - 2 * c

    def link_part(j):
        return pl.ds(c * 128 + j * 64, 64), slice(None)

    def constant_part(j):
        if j == 0:
            at = pl.ds(pl.multiple_of(c * 128, 128), 128)
            return at, at
        return pl.ds(c * 64, 64), pl.ds(128, 128)

    def ring_send(buf, ids, at, where, part):
        for way, j in ((0, 0), (1, 1), (0, 1), (1, 0)):
            piece = buf.at[at, *part(j)]
            one = copy(piece, piece, ids + way * 2 + j, where(turn if way == 0 else -turn))
            one.start()
            started.append((None, one))

    def places(at):
        return tuple(lax.rem(at + d + 4, 4) for d in (-turn, turn, 2))

    def mated(buf, place, j, number, part):
        piece = buf.at[place, *part(j)]
        one = copy(piece, piece, number, mate)
        one.start()
        started.append((None, one))
        return one

    def direct(buf, ids, at, where, part):
        behind, ahead, _ = places(at)
        mates = []
        for way, j in ((0, 0), (1, 1), (0, 1), (1, 0)):
            place = behind if way == 0 else ahead
            piece = buf.at[place, *part(j)]
            copy(piece, piece, ids + way * 2 + j, mate).wait_recv()
            if way == j:
                onward = copy(piece, piece, ids + 4 + way, where(turn if way == 0 else -turn))
                onward.start()
                started.append((None, onward))
            mates.append(mated(buf, place, j, ids + 6 + way * 2 + j, part))
        return mates

    def opposite(buf, ids, at, part):
        across = places(at)[2]
        mates = []
        for way in (0, 1):
            piece = buf.at[across, *part(way)]
            copy(piece, piece, ids + 4 + way, mate).wait_recv()
            mates.append(mated(buf, across, way, ids + 10 + way, part))
        return mates

    def done(mates):
        for one in mates:
            one.wait_recv()

    def whole(v):
        return jnp.concatenate([v[:128], jnp.concatenate([v[:128, 128:].T, v[128:, 128:]], 1)], 0)

    rows_256 = lax.broadcasted_iota(jnp.int32, (256, 256), 0)
    eye = (rows_256 == lax.broadcasted_iota(jnp.int32, (256, 256), 1)).astype(F32)

    def near_products(buf):
        rb[0] = eye
        rb[1] = buf[0]
        low = mm(split(buf[1]), split(buf[0]))
        rb[2] = low
        rb[3] = mm(split(buf[2]), split(low))

    def term(buf, place, added):
        return sandwich(rb[place], whole(buf[place]), added)

    def exclusive_links(links, at, out):
        @pl.when(at == 3)
        def _():
            out[...] = eye

        @pl.when(at < 3)
        def _():
            out[...] = links[3]

        for i in (2, 1):

            @pl.when(at < i)
            def _():
                out[...] = mm(split(out[...]), split(links[i]))

    def exclusive_constants(links, consts, at, out):
        @pl.when(at == 3)
        def _():
            out[...] = jnp.zeros((256, 256), F32)

        @pl.when(at < 3)
        def _():
            out[...] = whole(consts[3])

        for i in (2, 1):

            @pl.when(at < i)
            def _():
                out[...] = sandwich(links[i], out[...], whole(consts[i]))

    cl_copy.wait_recv()
    yl[y] = mm(split(cl[1]), split(cl[0]))
    ring_send(yl, ID_YL, y, y_at, link_part)
    ca_copy.wait_recv()
    ya[y] = sandwich(cl[0], ca[1], ca[0])
    ring_send(ya, ID_YA, y, y_at, constant_part)

    yl_mates = direct(yl, ID_YL, y, y_at, link_part)
    ya_mates = direct(ya, ID_YA, y, y_at, constant_part)
    done(yl_mates)
    done(ya_mates)

    @pl.when(y == 0)
    def _():
        rb[2] = mm(split(yl[1]), split(yl[0]))
        sm[...] = sandwich(yl[0], whole(ya[1]), whole(ya[0]))

    @pl.when(y == 1)
    def _():
        low = mm(split(yl[1]), split(yl[0]))
        near = sandwich(yl[0], whole(ya[1]), whole(ya[0]))
        rb[3] = mm(split(yl[2]), split(low))
        sm[...] = sandwich(low, whole(ya[2]), near)

    @pl.when(y == 2)
    def _():
        rb[0] = eye
        sm[...] = sandwich(yl[1], sandwich(yl[2], whole(ya[3]), whole(ya[2])), whole(ya[1]))

    @pl.when(y == 3)
    def _():
        rb[1] = yl[0]
        sm[...] = sandwich(yl[2], whole(ya[3]), whole(ya[2]))

    done(opposite(yl, ID_YL, y, link_part))
    high = mm(split(yl[3]), split(yl[2]))
    low = mm(split(yl[1]), split(yl[0]))
    xl[x] = mm(split(high), split(low))
    ring_send(xl, ID_XL, x, x_at, link_part)
    z_next(fg, ID_ZF, 1, 0)
    z_next(fg, ID_ZF, 0, 0, cond=is_b)

    @pl.when(y == 0)
    def _():
        sm[...] = sandwich(mm(split(yl[2]), split(rb[2])), whole(ya[3]), sm[...])

    @pl.when(y == 2)
    def _():
        sm[...] = sandwich(yl[0], sm[...], jnp.zeros((256, 256), F32))

    @pl.when(y == 3)
    def _():
        sm[...] = sandwich(mm(split(yl[1]), split(yl[0])), sm[...], whole(ya[0]))

    across = places(y)[2]
    done(opposite(ya, ID_YA, y, constant_part))
    xa[x] = term(ya, across, sm[...])
    ring_send(xa, ID_XA, x, x_at, constant_part)

    exclusive_links(yl, y, el.at[1])
    exclusive_constants(yl, ya, y, ea.at[1])
    xl_mates = direct(xl, ID_XL, x, x_at, link_part)

    @pl.when(c == 0)
    def _():
        ea[1] = sandwich(cl[1], ea[1], ca[1])
        el[1] = mm(split(el[1]), split(cl[1]))

    ea[0] = sandwich(lp[1], ea[1], base[1])
    el[0] = mm(split(el[1]), split(lp[1]))

    z_next(fg, ID_ZF, 1, 1)
    z_next(fg, ID_ZF, 0, 1, cond=is_b)
    xa_mates = direct(xa, ID_XA, x, x_at, constant_part)
    done(xl_mates + opposite(xl, ID_XL, x, link_part))
    sends_half = both(later, edge)
    behind, ahead, across = places(x)
    z_next(fg, ID_ZF, 1, 2)
    z_next(fg, ID_ZF, 0, 2, cond=is_b)
    done(xa_mates)

    @pl.when(sends_half)
    def _():
        near_products(xl)
        zero = jnp.zeros((256, 256), F32)
        th[...] = term(xa, behind, term(xa, ahead, term(xa, x, zero)))

    @pl.when(h == 0)
    def _():
        exclusive_links(xl, x, el.at[2])
        entry = split(el[2])
        for p in (1, 0):
            link = mm(entry, split(el[p]))
            pb[...] = link.T
            gg[p] = mm(split(link), split(fg[p]))
            kk[p * 192 : p * 192 + 128, :] = gg[p, :, pl.ds(pl.multiple_of(r * 128, 128), 128)].T
            kk[p * 192 + 128 : p * 192 + 192, :] = pb[pl.ds(r * 64, 64), :]

    done(opposite(xa, ID_XA, x, constant_part))

    hop = z_at(jnp.where(r == 0, -1, 1))

    def zh(j, kind):
        if j < 2:
            part = pl.ds(c * 128 + j * 64, 64), pl.ds(pl.multiple_of(c * 128, 128), 128)
        else:
            part = pl.ds(c * 64, 64), pl.ds(128, 128)
        piece = ph.at[*part]
        if kind == 0:
            return copy(th.at[*part], piece, ID_ZH + j, hop)
        return copy(piece, piece, ID_ZH + 3 * kind + j, inward if kind == 1 else mate)

    @pl.when(sends_half)
    def _():
        th[...] = term(xa, across, th[...])
        for j in (0, 1, 2):
            zh(j, 0).start()

    exclusive_constants(xl, xa, x, ea.at[2])

    def outputs(p):
        constant = sandwich(el[p], ea[2], ea[p])
        mine = fg[p, :, pl.ds(pl.multiple_of(r * 128, 128), 128)]
        middle = mm(split(constant), split(mine))
        pb[...] = constant
        left = jnp.concatenate([middle.T, pb[pl.ds(r * 64, 64), :]], 0)
        out = mm(split(left), split(fg[p]))
        cov[p] += out[:128]
        off[p] = out[128:]

    outputs(1)

    @pl.when(both(h == 0, edge))
    def _():
        for j in (0, 1, 2):
            zh(j, 0).wait_recv()
            zh(j, 1).start()
            zh(j, 2).start()

    outputs(0)
    for sends, one in started:
        if sends is None:
            one.wait_send()
        else:

            @pl.when(sends)
            def _():
                one().wait_send()

    @pl.when(both(h == 0, jnp.logical_not(edge)))
    def _():
        for j in (0, 1, 2):
            zh(j, 1).wait_recv()
            zh(j, 2).start()

    @pl.when(h == 0)
    def _():
        for j in (0, 1, 2):
            zh(j, 2).wait_recv()
        left = split(mm(split(kk[...]), split(whole(ph[...]))))
        for p in (0, 1):
            at = slice(p * 192, p * 192 + 192)
            out = mm((left[0][at], left[1][at]), split(gg[p]))
            cov[p] += out[:128]
            off[p] += out[128:]

    for p in (0, 1):
        off[p] = off[p] * (-mask[p, r].astype(F32))

    @pl.when(sends_half)
    def _():
        for j in (0, 1, 2):
            zh(j, 0).wait_send()

    @pl.when(jnp.logical_and(h == 0, edge))
    def _():
        for j in (0, 1, 2):
            zh(j, 1).wait_send()

    @pl.when(h == 0)
    def _():
        for j in (0, 1, 2):
            zh(j, 2).wait_send()


def put_out(cov, off, cov_out, off_out, sems):
    copies = (
        pltpu.make_async_copy(cov, cov_out, sems.at[0]),
        pltpu.make_async_copy(off, off_out, sems.at[1]),
    )
    for one in copies:
        one.start()
    for one in copies:
        one.wait()


def body(fill_blocks, fill_mask, inv_diag, factor_off):
    vmem = pl.BlockSpec(memory_space=pltpu.VMEM)

    def sq(n):
        return pltpu.VMEM((n, 256, 256), F32)

    results = pl.pallas_call(
        kernel,
        name="chain",
        out_shape=(pltpu.VMEM((2, 128, 512), F32), pltpu.VMEM((2, 64, 512), F32)),
        in_specs=[pl.BlockSpec(memory_space=pltpu.HBM)] * 4,
        out_specs=(vmem, vmem),
        scratch_shapes=[
            pltpu.SMEM((2, 4), jnp.int32),
            pltpu.SMEM((2, 4), jnp.int32),
            pltpu.VMEM((2, 512, 512), F32),
            pltpu.VMEM((2, 64, 512), F32),
            pltpu.SemaphoreType.DMA((5,)),
            pltpu.VMEM((8, 256), jnp.int32),
            pltpu.VMEM((8, 256), jnp.int32),
            pltpu.VMEM((2, 512, 512), BF16),
            pltpu.VMEM((2, 512, 512), BF16),
            sq(2),
            pltpu.VMEM((2, 256, 512), F32),
            sq(2),
            sq(2),
            sq(2),
            sq(4),
            sq(4),
            sq(4),
            sq(4),
            sq(3),
            sq(3),
            pltpu.VMEM((256, 256), F32),
            pltpu.VMEM((256, 256), F32),
            pltpu.VMEM((256, 256), F32),
            sq(4),
            pltpu.VMEM((256, 256), F32),
            pltpu.VMEM((2, 256, 512), F32),
            pltpu.VMEM((384, 256), F32),
            pltpu.SemaphoreType.DMA((N_IDS,)),
            pltpu.SemaphoreType.DMA((N_IDS,)),
        ],
        compiler_params=pltpu.CompilerParams(
            collective_id=0, has_side_effects=True
        ),
    )(fill_blocks, fill_mask, inv_diag, factor_off)
    hbm = pl.BlockSpec(memory_space=pltpu.HBM)
    return pl.pallas_call(
        put_out,
        name="put_out",
        out_shape=(
            jax.ShapeDtypeStruct((2, 128, 512), F32),
            jax.ShapeDtypeStruct((2, 64, 512), F32),
        ),
        in_specs=[vmem, vmem],
        out_specs=(hbm, hbm),
        scratch_shapes=[pltpu.SemaphoreType.DMA((2,))],
        compiler_params=pltpu.CompilerParams(vmem_limit_bytes=4 << 20),
    )(*results)


def solution(mesh):
    torus = Mesh(mesh.devices.reshape(2, 4, 4, 2, mesh.shape["row"]), (*SEG, "row"))
    placed = (P(SEG, None), P(SEG, None), P(SEG, None, None), P(SEG, "row", None))
    return jax.shard_map(
        body,
        mesh=torus,
        in_specs=placed,
        out_specs=(P(SEG, "row", None), P(SEG, "row", None)),
        check_vma=False,
    )
```

```python
import jax
import jax.numpy as jnp
from jax import lax
from jax.experimental import pallas as pl
from jax.experimental.pallas import tpu as pltpu
from jax.sharding import Mesh
from jax.sharding import PartitionSpec as P

BLOCK = 64
SEG = ("seg_0", "seg_1", "seg_2", "seg_3")
F32 = jnp.float32
BF16 = jnp.bfloat16
N_IDS = 100

ID_IDX = 0
ID_ZL = 1
ID_ZF = 13
ID_CL = 25
ID_CA = 26
ID_YL = 27
ID_YA = 39
ID_XL = 51
ID_XA = 63
ID_ZL_LATE = 84
ID_ZF_LATE = 90
ID_RELAY = 99
ID_ZH = 75


def split(v):
    hi = v.astype(BF16)
    return hi, (v - hi.astype(F32)).astype(BF16)


def dot(a, b):
    return lax.dot_general(a, b, (((1,), (0,)), ((), ())), preferred_element_type=F32)


def mm(a, b):
    (ah, al), (bh, bl) = a, b
    return dot(ah, bh) + (dot(ah, bl) + dot(al, bh))


def sandwich(link, inner, added):
    left = mm(split(link.T), split(inner))
    return added + mm(split(left), split(link))


def kernel(
    blocks_hbm, mask_hbm, inv_hbm, fac_hbm, cov, off,
    blocks, mask, inv, fac, local, idx_out, idx_in, inv_h, inv_l, lp, fg, base, cl, ca, yl, ya, xl, xa,
    el, ea, ph, th, pb, rb, sm, gg, kk, ss, rs,
):
    h, x, y, c = (lax.axis_index(a) for a in SEG)
    r = lax.axis_index("row")
    z = 4 * h + r
    seg = ((h * 4 + x) * 4 + y) * 2 + c

    both = jnp.logical_and

    def z_at(d):
        zz = lax.rem(z + d + 8, 8)
        return {"seg_0": zz // 4, "row": lax.rem(zz, 4)}

    def seg_at(d):
        s = lax.rem(seg + d + 64, 64)
        return {
            "seg_0": s // 32,
            "seg_1": lax.rem(s // 8, 4),
            "seg_2": lax.rem(s // 2, 4),
            "seg_3": lax.rem(s, 2),
        }

    def y_at(d):
        return {"seg_2": lax.rem(y + d + 4, 4)}

    def x_at(d):
        return {"seg_1": lax.rem(x + d + 4, 4)}

    mate = {"seg_3": 1 - c}

    loads = [
        pltpu.make_async_copy(src, dst, local.at[i])
        for i, (src, dst) in enumerate((
            (blocks_hbm, blocks), (mask_hbm, mask), (fac_hbm, fac),
            (inv_hbm.at[c], inv.at[c]), (inv_hbm.at[1 - c], inv.at[1 - c]),
        ))
    ]
    for load in loads:
        load.start()

    barrier = pltpu.get_barrier_semaphore()

    def greet(who):
        pl.semaphore_signal(barrier, 1, device_id=who, device_id_type=pl.DeviceIdType.MESH)

    for who in (mate, z_at(1), z_at(-1), y_at(1), y_at(-1), x_at(1), x_at(-1)):
        greet(who)

    later = h == 1
    edge = jnp.logical_or(r == 0, r == 3)
    tail = both(both(x == 3, y == 3), c == 1)
    head = both(both(x == 0, y == 0), c == 0)
    plain_out, plain_in = jnp.logical_not(tail), jnp.logical_not(head)
    far_out = both(both(tail, h == 0), edge)
    far_in = both(both(head, later), edge)
    relay_in = both(both(head, later), jnp.logical_not(edge))
    across_half = {
        "seg_0": 1 - h, "seg_1": lax.rem(x + 1 + 2 * h, 4), "seg_2": lax.rem(y + 1 + 2 * h, 4),
        "seg_3": 1 - c, "row": 3 - r,
    }
    for cond, who in (
        (plain_in, seg_at(-1)), (far_in, across_half),
    ):

        @pl.when(cond)
        def _():
            greet(who)

    greetings = 7
    for cond in (plain_out, far_out):
        greetings = greetings + jnp.where(cond, 1, 0)

    started = []

    def copy(src, dst, number, who):
        return pltpu.make_async_remote_copy(
            src_ref=src, dst_ref=dst, send_sem=ss.at[number], recv_sem=rs.at[number],
            device_id=who, device_id_type=pl.DeviceIdType.MESH,
        )

    for load in loads[:3]:
        load.wait()

    lane = lax.broadcasted_iota(jnp.int32, (8, 256), 1)
    slot = lane // BLOCK

    def targets(panel):
        t = jnp.zeros((8, 256), jnp.int32)
        for s in range(4):
            t = jnp.where(slot == s, blocks[panel, s], t)
        return t * BLOCK + (lane - slot * BLOCK)

    idx_out[...] = targets(1)
    target_1 = targets(0)

    row_at = lax.broadcasted_iota(jnp.int32, (512, 256), 0)

    def chooser(t):
        return jnp.where(row_at == t[0:1, :], 1.0, 0.0).astype(BF16)

    def keep(panel):
        live = mask[panel, r].astype(F32)
        return jnp.where(seg * 2 + panel < 127, live, 0.0)

    def factor_rows(p):
        ih, il = split(inv[p])
        inv_h[p] = ih
        inv_l[p] = il
        fh, fl = split(fac[p] * keep(p))
        fg[p, pl.ds(r * 64, 64), :256] = mm((fh, fl), (ih[:, :256], il[:, :256]))
        fg[p, pl.ds(r * 64, 64), 256:] = mm((fh[:, 256:], fl[:, 256:]), (ih[256:, 256:], il[256:, 256:]))

    def local_link(p, choose):
        fh, fl = split(fg[p, pl.ds(r * 64, 64), :])
        lp[p, pl.ds(r * 64, 64), :] = dot(fh, choose) + dot(fl, choose)

    def local_base(p, choose):
        ch = dot(inv_h[p], choose)
        cl_ = dot(inv_l[p], choose)
        chh, cll = ch.astype(BF16), cl_.astype(BF16)
        cth, ctl = ch.T.astype(BF16), cl_.T.astype(BF16)
        base[p] = mm((cth, ctl), (chh, cll))

    is_a, is_b = c == 0, c == 1
    loads[3].wait()
    factor_rows(c)

    @pl.when(is_b)
    def _():
        local_link(1, chooser(target_1))

    pl.semaphore_wait(barrier, greetings)

    def begin(cond, made):
        @pl.when(cond)
        def _():
            made().start()

        started.append((cond, made))

    begin(plain_out, lambda: copy(idx_out, idx_in, ID_IDX, seg_at(1)))
    begin(far_out, lambda: copy(idx_out, idx_in, ID_IDX, across_half))
    inward = z_at(jnp.where(r == 0, 1, -1))

    @pl.when(both(head, h == 0))
    def _():
        idx_in[...] = target_1

    relay = lambda: copy(idx_in, idx_in, ID_RELAY, inward)

    def z_parts(buf, ids, p, k, up, lo, n):
        block = (r - k) if up else (r + k)
        block_in = (r - 1 - k) if up else (r + 1 + k)
        sends = jnp.logical_and(r < 3, r - k >= 0) if up else jnp.logical_and(r > 0, r + k <= 3)
        takes = (r - 1 - k >= 0) if up else (r + 1 + k <= 3)
        number = ids + p * 6 + (0 if up else 3) + k
        who = z_at(1 if up else -1)

        def made(b):
            part = buf.at[p, pl.ds(b * 64 + lo, n), :]
            return copy(part, part, number, who)

        return sends, takes, lambda: made(block), lambda: made(block_in)

    def z_send(buf, ids, p, k, lo=0, n=64, cond=None):
        for up in (True, False):
            sends, _, out, _ = z_parts(buf, ids, p, k, up, lo, n)
            if cond is not None:
                sends = both(sends, cond)

            @pl.when(sends)
            def _():
                out().start()

            started.append((sends, out))

    def z_take(buf, ids, p, k, lo=0, n=64, cond=None):
        for up in (True, False):
            _, takes, _, into = z_parts(buf, ids, p, k, up, lo, n)
            if cond is not None:
                takes = both(takes, cond)

            @pl.when(takes)
            def _():
                into().wait_recv()

    def z_next(buf, ids, p, k, lo=0, n=64, cond=None):
        z_take(buf, ids, p, k, lo, n, cond)
        if k < 2:
            z_send(buf, ids, p, k + 1, lo, n, cond)

    waits_long = both(head, later)
    units = (
        (fg, ID_ZF, 0, 0, 32, is_a), (fg, ID_ZF_LATE, 0, 32, 32, is_a),
        (lp, ID_ZL, 1, 0, 64, None),
        (lp, ID_ZL, 0, 0, 32, is_b), (lp, ID_ZL_LATE, 0, 32, 32, is_b),
    )

    def every(k):
        for buf, ids, p, lo, n, cond in units:
            z_next(buf, ids, p, k, lo, n, cond)

    for buf, ids, p, lo, n, cond in units[:2]:
        z_send(buf, ids, p, 0, lo, n, cond)
    z_send(lp, ID_ZL, 1, 0, cond=is_b)
    loads[4].wait()
    factor_rows(1 - c)

    @pl.when(is_a)
    def _():
        local_link(1, chooser(target_1))

    z_send(lp, ID_ZL, 1, 0, cond=is_a)

    @pl.when(is_b)
    def _():
        copy(idx_out, idx_in, ID_IDX, mate).wait_recv()
        local_link(0, chooser(idx_in[...]))

    for buf, ids, p, lo, n, cond in units[3:]:
        z_send(buf, ids, p, 0, lo, n, cond)
    local_base(1, chooser(target_1))
    every(0)

    @pl.when(both(is_a, plain_in))
    def _():
        copy(idx_out, idx_in, ID_IDX, mate).wait_recv()

    @pl.when(jnp.logical_not(waits_long))
    def _():
        local_base(0, chooser(idx_in[...]))

    every(1)

    @pl.when(far_in)
    def _():
        copy(idx_out, idx_in, ID_IDX, mate).wait_recv()

    begin(far_in, relay)
    for p in (0, 1):
        mine = inv[p, :, pl.ds(pl.multiple_of(r * 128, 128), 128)]
        cov[p] = mm(split(mine.T), (inv_h[p], inv_l[p]))

    @pl.when(relay_in)
    def _():
        relay().wait_recv()

    @pl.when(waits_long)
    def _():
        local_base(0, chooser(idx_in[...]))

    every(2)

    @pl.when(is_a)
    def _():
        fh, fl = split(fg[0])
        choose = chooser(idx_in[...])
        lp[0] = dot(fh, choose) + dot(fl, choose)

    z_send(fg, ID_ZF, 1, 0)
    z_send(fg, ID_ZF, 0, 0, cond=is_b)

    link_0 = split(lp[0])
    cl[c] = mm(split(lp[1]), link_0)
    cl_copy = copy(cl.at[c], cl.at[c], ID_CL, mate)
    cl_copy.start()
    ca[c] = sandwich(lp[0], base[1], base[0])
    ca_copy = copy(ca.at[c], ca.at[c], ID_CA, mate)
    ca_copy.start()
    started.append((None, cl_copy))
    started.append((None, ca_copy))

    turn = 1 - 2 * c

    def link_part(j):
        return pl.ds(c * 128 + j * 64, 64), slice(None)

    def constant_part(j):
        if j == 0:
            at = pl.ds(pl.multiple_of(c * 128, 128), 128)
            return at, at
        return pl.ds(c * 64, 64), pl.ds(128, 128)

    def ring_send(buf, ids, at, where, part):
        for way, j in ((0, 0), (1, 1), (0, 1), (1, 0)):
            piece = buf.at[at, *part(j)]
            one = copy(piece, piece, ids + way * 2 + j, where(turn if way == 0 else -turn))
            one.start()
            started.append((None, one))

    def places(at):
        return tuple(lax.rem(at + d + 4, 4) for d in (-turn, turn, 2))

    def mated(buf, place, j, number, part):
        piece = buf.at[place, *part(j)]
        one = copy(piece, piece, number, mate)
        one.start()
        started.append((None, one))
        return one

    def direct(buf, ids, at, where, part):
        behind, ahead, _ = places(at)
        mates = []
        for way, j in ((0, 0), (1, 1), (0, 1), (1, 0)):
            place = behind if way == 0 else ahead
            piece = buf.at[place, *part(j)]
            copy(piece, piece, ids + way * 2 + j, mate).wait_recv()
            if way == j:
                onward = copy(piece, piece, ids + 4 + way, where(turn if way == 0 else -turn))
                onward.start()
                started.append((None, onward))
            mates.append(mated(buf, place, j, ids + 6 + way * 2 + j, part))
        return mates

    def opposite(buf, ids, at, part):
        across = places(at)[2]
        mates = []
        for way in (0, 1):
            piece = buf.at[across, *part(way)]
            copy(piece, piece, ids + 4 + way, mate).wait_recv()
            mates.append(mated(buf, across, way, ids + 10 + way, part))
        return mates

    def done(mates):
        for one in mates:
            one.wait_recv()

    def whole(v):
        return jnp.concatenate([v[:128], jnp.concatenate([v[:128, 128:].T, v[128:, 128:]], 1)], 0)

    rows_256 = lax.broadcasted_iota(jnp.int32, (256, 256), 0)
    eye = (rows_256 == lax.broadcasted_iota(jnp.int32, (256, 256), 1)).astype(F32)

    def near_products(buf):
        rb[0] = eye
        rb[1] = buf[0]
        low = mm(split(buf[1]), split(buf[0]))
        rb[2] = low
        rb[3] = mm(split(buf[2]), split(low))

    def term(buf, place, added):
        return sandwich(rb[place], whole(buf[place]), added)

    def exclusive_links(links, at, out):
        @pl.when(at == 3)
        def _():
            out[...] = eye

        @pl.when(at < 3)
        def _():
            out[...] = links[3]

        for i in (2, 1):

            @pl.when(at < i)
            def _():
                out[...] = mm(split(out[...]), split(links[i]))

    def exclusive_constants(links, consts, at, out):
        @pl.when(at == 3)
        def _():
            out[...] = jnp.zeros((256, 256), F32)

        @pl.when(at < 3)
        def _():
            out[...] = whole(consts[3])

        for i in (2, 1):

            @pl.when(at < i)
            def _():
                out[...] = sandwich(links[i], out[...], whole(consts[i]))

    cl_copy.wait_recv()
    yl[y] = mm(split(cl[1]), split(cl[0]))
    ring_send(yl, ID_YL, y, y_at, link_part)
    ca_copy.wait_recv()
    ya[y] = sandwich(cl[0], ca[1], ca[0])
    ring_send(ya, ID_YA, y, y_at, constant_part)

    yl_mates = direct(yl, ID_YL, y, y_at, link_part)
    ya_mates = direct(ya, ID_YA, y, y_at, constant_part)
    done(yl_mates)
    done(ya_mates)

    @pl.when(y == 0)
    def _():
        rb[2] = mm(split(yl[1]), split(yl[0]))
        sm[...] = sandwich(yl[0], whole(ya[1]), whole(ya[0]))

    @pl.when(y == 1)
    def _():
        low = mm(split(yl[1]), split(yl[0]))
        near = sandwich(yl[0], whole(ya[1]), whole(ya[0]))
        rb[3] = mm(split(yl[2]), split(low))
        sm[...] = sandwich(low, whole(ya[2]), near)

    @pl.when(y == 2)
    def _():
        rb[0] = eye
        sm[...] = sandwich(yl[1], sandwich(yl[2], whole(ya[3]), whole(ya[2])), whole(ya[1]))

    @pl.when(y == 3)
    def _():
        rb[1] = yl[0]
        sm[...] = sandwich(yl[2], whole(ya[3]), whole(ya[2]))

    done(opposite(yl, ID_YL, y, link_part))
    high = mm(split(yl[3]), split(yl[2]))
    low = mm(split(yl[1]), split(yl[0]))
    xl[x] = mm(split(high), split(low))
    ring_send(xl, ID_XL, x, x_at, link_part)
    z_next(fg, ID_ZF, 1, 0)
    z_next(fg, ID_ZF, 0, 0, cond=is_b)

    @pl.when(y == 0)
    def _():
        sm[...] = sandwich(mm(split(yl[2]), split(rb[2])), whole(ya[3]), sm[...])

    @pl.when(y == 2)
    def _():
        sm[...] = sandwich(yl[0], sm[...], jnp.zeros((256, 256), F32))

    @pl.when(y == 3)
    def _():
        sm[...] = sandwich(mm(split(yl[1]), split(yl[0])), sm[...], whole(ya[0]))

    across = places(y)[2]
    done(opposite(ya, ID_YA, y, constant_part))
    xa[x] = term(ya, across, sm[...])
    ring_send(xa, ID_XA, x, x_at, constant_part)

    exclusive_links(yl, y, el.at[1])
    exclusive_constants(yl, ya, y, ea.at[1])
    xl_mates = direct(xl, ID_XL, x, x_at, link_part)

    @pl.when(c == 0)
    def _():
        ea[1] = sandwich(cl[1], ea[1], ca[1])
        el[1] = mm(split(el[1]), split(cl[1]))

    ea[0] = sandwich(lp[1], ea[1], base[1])
    el[0] = mm(split(el[1]), split(lp[1]))

    z_next(fg, ID_ZF, 1, 1)
    z_next(fg, ID_ZF, 0, 1, cond=is_b)
    xa_mates = direct(xa, ID_XA, x, x_at, constant_part)
    done(xl_mates + opposite(xl, ID_XL, x, link_part))
    sends_half = both(later, edge)
    behind, ahead, across = places(x)
    z_next(fg, ID_ZF, 1, 2)
    z_next(fg, ID_ZF, 0, 2, cond=is_b)
    done(xa_mates)

    @pl.when(sends_half)
    def _():
        near_products(xl)
        zero = jnp.zeros((256, 256), F32)
        th[...] = term(xa, behind, term(xa, ahead, term(xa, x, zero)))

    @pl.when(h == 0)
    def _():
        exclusive_links(xl, x, el.at[2])
        entry = split(el[2])
        for p in (1, 0):
            link = mm(entry, split(el[p]))
            pb[...] = link.T
            gg[p] = mm(split(link), split(fg[p]))
            kk[p * 192 : p * 192 + 128, :] = gg[p, :, pl.ds(pl.multiple_of(r * 128, 128), 128)].T
            kk[p * 192 + 128 : p * 192 + 192, :] = pb[pl.ds(r * 64, 64), :]

    done(opposite(xa, ID_XA, x, constant_part))

    hop = z_at(jnp.where(r == 0, -1, 1))

    def zh(j, kind):
        if j < 2:
            part = pl.ds(c * 128 + j * 64, 64), pl.ds(pl.multiple_of(c * 128, 128), 128)
        else:
            part = pl.ds(c * 64, 64), pl.ds(128, 128)
        piece = ph.at[*part]
        if kind == 0:
            return copy(th.at[*part], piece, ID_ZH + j, hop)
        return copy(piece, piece, ID_ZH + 3 * kind + j, inward if kind == 1 else mate)

    @pl.when(sends_half)
    def _():
        th[...] = term(xa, across, th[...])
        for j in (0, 1, 2):
            zh(j, 0).start()

    exclusive_constants(xl, xa, x, ea.at[2])

    def outputs(p):
        constant = sandwich(el[p], ea[2], ea[p])
        mine = fg[p, :, pl.ds(pl.multiple_of(r * 128, 128), 128)]
        middle = mm(split(constant), split(mine))
        pb[...] = constant
        left = jnp.concatenate([middle.T, pb[pl.ds(r * 64, 64), :]], 0)
        out = mm(split(left), split(fg[p]))
        cov[p] += out[:128]
        off[p] = out[128:]

    outputs(1)

    @pl.when(both(h == 0, edge))
    def _():
        for j in (0, 1, 2):
            zh(j, 0).wait_recv()
            zh(j, 1).start()
            zh(j, 2).start()

    outputs(0)
    for sends, one in started:
        if sends is None:
            one.wait_send()
        else:

            @pl.when(sends)
            def _():
                one().wait_send()

    @pl.when(both(h == 0, jnp.logical_not(edge)))
    def _():
        for j in (0, 1, 2):
            zh(j, 1).wait_recv()
            zh(j, 2).start()

    @pl.when(h == 0)
    def _():
        for j in (0, 1, 2):
            zh(j, 2).wait_recv()
        left = split(mm(split(kk[...]), split(whole(ph[...]))))
        for p in (0, 1):
            at = slice(p * 192, p * 192 + 192)
            out = mm((left[0][at], left[1][at]), split(gg[p]))
            cov[p] += out[:128]
            off[p] += out[128:]

    for p in (0, 1):
        off[p] = off[p] * (-mask[p, r].astype(F32))

    @pl.when(sends_half)
    def _():
        for j in (0, 1, 2):
            zh(j, 0).wait_send()

    @pl.when(jnp.logical_and(h == 0, edge))
    def _():
        for j in (0, 1, 2):
            zh(j, 1).wait_send()

    @pl.when(h == 0)
    def _():
        for j in (0, 1, 2):
            zh(j, 2).wait_send()


def put_out(cov, off, cov_out, off_out, sems):
    copies = (
        pltpu.make_async_copy(cov, cov_out, sems.at[0]),
        pltpu.make_async_copy(off, off_out, sems.at[1]),
    )
    for one in copies:
        one.start()
    for one in copies:
        one.wait()


def body(fill_blocks, fill_mask, inv_diag, factor_off):
    vmem = pl.BlockSpec(memory_space=pltpu.VMEM)

    def sq(n):
        return pltpu.VMEM((n, 256, 256), F32)

    results = pl.pallas_call(
        kernel,
        name="chain",
        out_shape=(pltpu.VMEM((2, 128, 512), F32), pltpu.VMEM((2, 64, 512), F32)),
        in_specs=[pl.BlockSpec(memory_space=pltpu.HBM)] * 4,
        out_specs=(vmem, vmem),
        scratch_shapes=[
            pltpu.SMEM((2, 4), jnp.int32),
            pltpu.SMEM((2, 4), jnp.int32),
            pltpu.VMEM((2, 512, 512), F32),
            pltpu.VMEM((2, 64, 512), F32),
            pltpu.SemaphoreType.DMA((5,)),
            pltpu.VMEM((8, 256), jnp.int32),
            pltpu.VMEM((8, 256), jnp.int32),
            pltpu.VMEM((2, 512, 512), BF16),
            pltpu.VMEM((2, 512, 512), BF16),
            sq(2),
            pltpu.VMEM((2, 256, 512), F32),
            sq(2),
            sq(2),
            sq(2),
            sq(4),
            sq(4),
            sq(4),
            sq(4),
            sq(3),
            sq(3),
            pltpu.VMEM((256, 256), F32),
            pltpu.VMEM((256, 256), F32),
            pltpu.VMEM((256, 256), F32),
            sq(4),
            pltpu.VMEM((256, 256), F32),
            pltpu.VMEM((2, 256, 512), F32),
            pltpu.VMEM((384, 256), F32),
            pltpu.SemaphoreType.DMA((N_IDS,)),
            pltpu.SemaphoreType.DMA((N_IDS,)),
        ],
        compiler_params=pltpu.CompilerParams(
            collective_id=0, has_side_effects=True
        ),
    )(fill_blocks, fill_mask, inv_diag, factor_off)
    hbm = pl.BlockSpec(memory_space=pltpu.HBM)
    return pl.pallas_call(
        put_out,
        name="put_out",
        out_shape=(
            jax.ShapeDtypeStruct((2, 128, 512), F32),
            jax.ShapeDtypeStruct((2, 64, 512), F32),
        ),
        in_specs=[vmem, vmem],
        out_specs=(hbm, hbm),
        scratch_shapes=[pltpu.SemaphoreType.DMA((2,))],
        compiler_params=pltpu.CompilerParams(vmem_limit_bytes=4 << 20),
    )(*results)


def solution(mesh):
    torus = Mesh(mesh.devices.reshape(2, 4, 4, 2, mesh.shape["row"]), (*SEG, "row"))
    placed = (P(SEG, None), P(SEG, None), P(SEG, None, None), P(SEG, "row", None))
    return jax.shard_map(
        body,
        mesh=torus,
        in_specs=placed,
        out_specs=(P(SEG, "row", None), P(SEG, "row", None)),
        check_vma=False,
    )
```

```python
import jax
import jax.numpy as jnp
from jax import lax
from jax.experimental import pallas as pl
from jax.experimental.pallas import tpu as pltpu
from jax.sharding import Mesh
from jax.sharding import PartitionSpec as P

BLOCK = 64
SEG = ("seg_0", "seg_1", "seg_2", "seg_3")
F32 = jnp.float32
BF16 = jnp.bfloat16
N_IDS = 100

ID_IDX = 0
ID_ZL = 1
ID_ZF = 13
ID_CL = 25
ID_CA = 26
ID_YL = 27
ID_YA = 39
ID_XL = 51
ID_XA = 63
ID_ZL_LATE = 84
ID_ZF_LATE = 90
ID_RELAY = 99
ID_ZH = 75


def split(v):
    hi = v.astype(BF16)
    return hi, (v - hi.astype(F32)).astype(BF16)


def dot(a, b):
    return lax.dot_general(a, b, (((1,), (0,)), ((), ())), preferred_element_type=F32)


def mm(a, b):
    (ah, al), (bh, bl) = a, b
    return dot(ah, bh) + (dot(ah, bl) + dot(al, bh))


def sandwich(link, inner, added):
    left = mm(split(link.T), split(inner))
    return added + mm(split(left), split(link))


def kernel(
    blocks_hbm, mask_hbm, inv_hbm, fac_hbm, cov, off,
    blocks, mask, inv, fac, local, idx_out, idx_in, inv_h, inv_l, lp, fg, base, cl, ca, yl, ya, xl, xa,
    el, ea, ph, th, pb, rb, sm, gg, gh, gl, kh, kl, cz, ss, rs,
):
    h, x, y, c = (lax.axis_index(a) for a in SEG)
    r = lax.axis_index("row")
    z = 4 * h + r
    seg = ((h * 4 + x) * 4 + y) * 2 + c

    both = jnp.logical_and

    def z_at(d):
        zz = lax.rem(z + d + 8, 8)
        return {"seg_0": zz // 4, "row": lax.rem(zz, 4)}

    def seg_at(d):
        s = lax.rem(seg + d + 64, 64)
        return {
            "seg_0": s // 32,
            "seg_1": lax.rem(s // 8, 4),
            "seg_2": lax.rem(s // 2, 4),
            "seg_3": lax.rem(s, 2),
        }

    def y_at(d):
        return {"seg_2": lax.rem(y + d + 4, 4)}

    def x_at(d):
        return {"seg_1": lax.rem(x + d + 4, 4)}

    mate = {"seg_3": 1 - c}

    loads = [
        pltpu.make_async_copy(src, dst, local.at[i])
        for i, (src, dst) in enumerate((
            (blocks_hbm, blocks), (mask_hbm, mask), (fac_hbm, fac),
            (inv_hbm.at[c], inv.at[c]), (inv_hbm.at[1 - c], inv.at[1 - c]),
        ))
    ]
    for load in loads:
        load.start()

    barrier = pltpu.get_barrier_semaphore()

    def greet(who):
        pl.semaphore_signal(barrier, 1, device_id=who, device_id_type=pl.DeviceIdType.MESH)

    for who in (mate, z_at(1), z_at(-1), y_at(1), y_at(-1), x_at(1), x_at(-1)):
        greet(who)

    later = h == 1
    edge = jnp.logical_or(r == 0, r == 3)
    tail = both(both(x == 3, y == 3), c == 1)
    head = both(both(x == 0, y == 0), c == 0)
    plain_out, plain_in = jnp.logical_not(tail), jnp.logical_not(head)
    far_out = both(both(tail, h == 0), edge)
    far_in = both(both(head, later), edge)
    relay_in = both(both(head, later), jnp.logical_not(edge))
    across_half = {
        "seg_0": 1 - h, "seg_1": lax.rem(x + 1 + 2 * h, 4), "seg_2": lax.rem(y + 1 + 2 * h, 4),
        "seg_3": 1 - c, "row": 3 - r,
    }
    for cond, who in (
        (plain_in, seg_at(-1)), (far_in, across_half),
    ):

        @pl.when(cond)
        def _():
            greet(who)

    greetings = 7
    for cond in (plain_out, far_out):
        greetings = greetings + jnp.where(cond, 1, 0)

    started = []

    def copy(src, dst, number, who):
        return pltpu.make_async_remote_copy(
            src_ref=src, dst_ref=dst, send_sem=ss.at[number], recv_sem=rs.at[number],
            device_id=who, device_id_type=pl.DeviceIdType.MESH,
        )

    for load in loads[:3]:
        load.wait()

    lane = lax.broadcasted_iota(jnp.int32, (8, 256), 1)
    slot = lane // BLOCK

    def targets(panel):
        t = jnp.zeros((8, 256), jnp.int32)
        for s in range(4):
            t = jnp.where(slot == s, blocks[panel, s], t)
        return t * BLOCK + (lane - slot * BLOCK)

    idx_out[...] = targets(1)
    target_1 = targets(0)

    row_at = lax.broadcasted_iota(jnp.int32, (512, 256), 0)

    def chooser(t):
        return jnp.where(row_at == t[0:1, :], 1.0, 0.0).astype(BF16)

    def keep(panel):
        live = mask[panel, r].astype(F32)
        return jnp.where(seg * 2 + panel < 127, live, 0.0)

    def factor_rows(p):
        ih, il = split(inv[p])
        inv_h[p] = ih
        inv_l[p] = il
        fh, fl = split(fac[p] * keep(p))
        fg[p, pl.ds(r * 64, 64), :256] = mm((fh, fl), (ih[:, :256], il[:, :256]))
        fg[p, pl.ds(r * 64, 64), 256:] = mm((fh[:, 256:], fl[:, 256:]), (ih[256:, 256:], il[256:, 256:]))

    def local_link(p, choose):
        fh, fl = split(fg[p, pl.ds(r * 64, 64), :])
        lp[p, pl.ds(r * 64, 64), :] = dot(fh, choose) + dot(fl, choose)

    def local_base(p, choose):
        ch = dot(inv_h[p], choose)
        cl_ = dot(inv_l[p], choose)
        chh, cll = ch.astype(BF16), cl_.astype(BF16)
        cth, ctl = ch.T.astype(BF16), cl_.T.astype(BF16)
        base[p] = mm((cth, ctl), (chh, cll))

    is_a, is_b = c == 0, c == 1
    loads[3].wait()
    factor_rows(c)

    @pl.when(is_b)
    def _():
        local_link(1, chooser(target_1))

    pl.semaphore_wait(barrier, greetings)

    def begin(cond, made):
        @pl.when(cond)
        def _():
            made().start()

        started.append((cond, made))

    begin(plain_out, lambda: copy(idx_out, idx_in, ID_IDX, seg_at(1)))
    begin(far_out, lambda: copy(idx_out, idx_in, ID_IDX, across_half))
    inward = z_at(jnp.where(r == 0, 1, -1))

    @pl.when(both(head, h == 0))
    def _():
        idx_in[...] = target_1

    relay = lambda: copy(idx_in, idx_in, ID_RELAY, inward)

    def z_parts(buf, ids, p, k, up, lo, n):
        block = (r - k) if up else (r + k)
        block_in = (r - 1 - k) if up else (r + 1 + k)
        sends = jnp.logical_and(r < 3, r - k >= 0) if up else jnp.logical_and(r > 0, r + k <= 3)
        takes = (r - 1 - k >= 0) if up else (r + 1 + k <= 3)
        number = ids + p * 6 + (0 if up else 3) + k
        who = z_at(1 if up else -1)

        def made(b):
            part = buf.at[p, pl.ds(b * 64 + lo, n), :]
            return copy(part, part, number, who)

        return sends, takes, lambda: made(block), lambda: made(block_in)

    def z_send(buf, ids, p, k, lo=0, n=64, cond=None):
        for up in (True, False):
            sends, _, out, _ = z_parts(buf, ids, p, k, up, lo, n)
            if cond is not None:
                sends = both(sends, cond)

            @pl.when(sends)
            def _():
                out().start()

            started.append((sends, out))

    def z_take(buf, ids, p, k, lo=0, n=64, cond=None):
        for up in (True, False):
            _, takes, _, into = z_parts(buf, ids, p, k, up, lo, n)
            if cond is not None:
                takes = both(takes, cond)

            @pl.when(takes)
            def _():
                into().wait_recv()

    def z_next(buf, ids, p, k, lo=0, n=64, cond=None):
        z_take(buf, ids, p, k, lo, n, cond)
        if k < 2:
            z_send(buf, ids, p, k + 1, lo, n, cond)

    waits_long = both(head, later)
    units = (
        (fg, ID_ZF, 0, 0, 32, is_a), (fg, ID_ZF_LATE, 0, 32, 32, is_a),
        (lp, ID_ZL, 1, 0, 64, None),
        (lp, ID_ZL, 0, 0, 32, is_b), (lp, ID_ZL_LATE, 0, 32, 32, is_b),
    )

    def every(k):
        for buf, ids, p, lo, n, cond in units:
            z_next(buf, ids, p, k, lo, n, cond)

    for buf, ids, p, lo, n, cond in units[:2]:
        z_send(buf, ids, p, 0, lo, n, cond)
    z_send(lp, ID_ZL, 1, 0, cond=is_b)
    loads[4].wait()
    factor_rows(1 - c)

    @pl.when(is_a)
    def _():
        local_link(1, chooser(target_1))

    z_send(lp, ID_ZL, 1, 0, cond=is_a)

    @pl.when(is_b)
    def _():
        copy(idx_out, idx_in, ID_IDX, mate).wait_recv()
        local_link(0, chooser(idx_in[...]))

    for buf, ids, p, lo, n, cond in units[3:]:
        z_send(buf, ids, p, 0, lo, n, cond)
    local_base(1, chooser(target_1))
    every(0)

    @pl.when(both(is_a, plain_in))
    def _():
        copy(idx_out, idx_in, ID_IDX, mate).wait_recv()

    @pl.when(jnp.logical_not(waits_long))
    def _():
        local_base(0, chooser(idx_in[...]))

    every(1)

    @pl.when(far_in)
    def _():
        copy(idx_out, idx_in, ID_IDX, mate).wait_recv()

    begin(far_in, relay)
    for p in (0, 1):
        mine = inv[p, :, pl.ds(pl.multiple_of(r * 128, 128), 128)]
        cov[p] = mm(split(mine.T), (inv_h[p], inv_l[p]))

    @pl.when(relay_in)
    def _():
        relay().wait_recv()

    @pl.when(waits_long)
    def _():
        local_base(0, chooser(idx_in[...]))

    def choose_rows(cond, lo, n):
        @pl.when(both(is_a, cond))
        def _():
            fh, fl = split(fg[0, lo : lo + n, :])
            lp[0, lo : lo + n, :] = dot(fh, cz[...]) + dot(fl, cz[...])

    @pl.when(is_a)
    def _():
        cz[...] = chooser(idx_in[...])

    choose_rows(r == 0, 0, 192)
    choose_rows(r == 3, 64, 192)
    choose_rows(jnp.logical_not(edge), 0, 256)
    every(2)
    choose_rows(r == 0, 192, 64)
    choose_rows(r == 3, 0, 64)

    z_send(fg, ID_ZF, 1, 0)
    z_send(fg, ID_ZF, 0, 0, cond=is_b)

    link_0 = split(lp[0])
    cl[c] = mm(split(lp[1]), link_0)
    cl_copy = copy(cl.at[c], cl.at[c], ID_CL, mate)
    cl_copy.start()
    ca[c] = sandwich(lp[0], base[1], base[0])
    ca_copy = copy(ca.at[c], ca.at[c], ID_CA, mate)
    ca_copy.start()
    started.append((None, cl_copy))
    started.append((None, ca_copy))

    turn = 1 - 2 * c

    def link_part(j):
        return pl.ds(c * 128 + j * 64, 64), slice(None)

    def constant_part(j):
        if j == 0:
            at = pl.ds(pl.multiple_of(c * 128, 128), 128)
            return at, at
        return pl.ds(c * 64, 64), pl.ds(128, 128)

    def ring_send(buf, ids, at, where, part):
        for way, j in ((0, 0), (1, 1), (0, 1), (1, 0)):
            piece = buf.at[at, *part(j)]
            one = copy(piece, piece, ids + way * 2 + j, where(turn if way == 0 else -turn))
            one.start()
            started.append((None, one))

    def places(at):
        return tuple(lax.rem(at + d + 4, 4) for d in (-turn, turn, 2))

    def mated(buf, place, j, number, part):
        piece = buf.at[place, *part(j)]
        one = copy(piece, piece, number, mate)
        one.start()
        started.append((None, one))
        return one

    def direct(buf, ids, at, where, part):
        behind, ahead, _ = places(at)
        mates = []
        for way, j in ((0, 0), (1, 1), (0, 1), (1, 0)):
            place = behind if way == 0 else ahead
            piece = buf.at[place, *part(j)]
            copy(piece, piece, ids + way * 2 + j, mate).wait_recv()
            if way == j:
                onward = copy(piece, piece, ids + 4 + way, where(turn if way == 0 else -turn))
                onward.start()
                started.append((None, onward))
            mates.append(mated(buf, place, j, ids + 6 + way * 2 + j, part))
        return mates

    def opposite(buf, ids, at, part):
        across = places(at)[2]
        mates = []
        for way in (0, 1):
            piece = buf.at[across, *part(way)]
            copy(piece, piece, ids + 4 + way, mate).wait_recv()
            mates.append(mated(buf, across, way, ids + 10 + way, part))
        return mates

    def done(mates):
        for one in mates:
            one.wait_recv()

    def whole(v):
        return jnp.concatenate([v[:128], jnp.concatenate([v[:128, 128:].T, v[128:, 128:]], 1)], 0)

    rows_256 = lax.broadcasted_iota(jnp.int32, (256, 256), 0)
    eye = (rows_256 == lax.broadcasted_iota(jnp.int32, (256, 256), 1)).astype(F32)

    def near_products(buf):
        rb[0] = eye
        rb[1] = buf[0]
        low = mm(split(buf[1]), split(buf[0]))
        rb[2] = low
        rb[3] = mm(split(buf[2]), split(low))

    def term(buf, place, added):
        return sandwich(rb[place], whole(buf[place]), added)

    def exclusive_links(links, at, out):
        @pl.when(at == 3)
        def _():
            out[...] = eye

        @pl.when(at < 3)
        def _():
            out[...] = links[3]

        for i in (2, 1):

            @pl.when(at < i)
            def _():
                out[...] = mm(split(out[...]), split(links[i]))

    def exclusive_constants(links, consts, at, out):
        @pl.when(at == 3)
        def _():
            out[...] = jnp.zeros((256, 256), F32)

        @pl.when(at < 3)
        def _():
            out[...] = whole(consts[3])

        for i in (2, 1):

            @pl.when(at < i)
            def _():
                out[...] = sandwich(links[i], out[...], whole(consts[i]))

    cl_copy.wait_recv()
    yl[y] = mm(split(cl[1]), split(cl[0]))
    ring_send(yl, ID_YL, y, y_at, link_part)
    ca_copy.wait_recv()
    ya[y] = sandwich(cl[0], ca[1], ca[0])
    ring_send(ya, ID_YA, y, y_at, constant_part)

    yl_mates = direct(yl, ID_YL, y, y_at, link_part)
    ya_mates = direct(ya, ID_YA, y, y_at, constant_part)
    done(yl_mates)
    done(ya_mates)

    @pl.when(y == 0)
    def _():
        rb[2] = mm(split(yl[1]), split(yl[0]))
        sm[...] = sandwich(yl[0], whole(ya[1]), whole(ya[0]))

    @pl.when(y == 1)
    def _():
        low = mm(split(yl[1]), split(yl[0]))
        near = sandwich(yl[0], whole(ya[1]), whole(ya[0]))
        rb[3] = mm(split(yl[2]), split(low))
        sm[...] = sandwich(low, whole(ya[2]), near)

    @pl.when(y == 2)
    def _():
        rb[0] = eye
        sm[...] = sandwich(yl[1], sandwich(yl[2], whole(ya[3]), whole(ya[2])), whole(ya[1]))

    @pl.when(y == 3)
    def _():
        rb[1] = yl[0]
        sm[...] = sandwich(yl[2], whole(ya[3]), whole(ya[2]))

    done(opposite(yl, ID_YL, y, link_part))
    high = mm(split(yl[3]), split(yl[2]))
    low = mm(split(yl[1]), split(yl[0]))
    xl[x] = mm(split(high), split(low))
    ring_send(xl, ID_XL, x, x_at, link_part)
    z_next(fg, ID_ZF, 1, 0)
    z_next(fg, ID_ZF, 0, 0, cond=is_b)

    @pl.when(y == 0)
    def _():
        sm[...] = sandwich(mm(split(yl[2]), split(rb[2])), whole(ya[3]), sm[...])

    @pl.when(y == 2)
    def _():
        sm[...] = sandwich(yl[0], sm[...], jnp.zeros((256, 256), F32))

    @pl.when(y == 3)
    def _():
        sm[...] = sandwich(mm(split(yl[1]), split(yl[0])), sm[...], whole(ya[0]))

    across = places(y)[2]
    done(opposite(ya, ID_YA, y, constant_part))
    xa[x] = term(ya, across, sm[...])
    ring_send(xa, ID_XA, x, x_at, constant_part)

    exclusive_links(yl, y, el.at[1])
    exclusive_constants(yl, ya, y, ea.at[1])
    xl_mates = direct(xl, ID_XL, x, x_at, link_part)

    @pl.when(c == 0)
    def _():
        ea[1] = sandwich(cl[1], ea[1], ca[1])
        el[1] = mm(split(el[1]), split(cl[1]))

    ea[0] = sandwich(lp[1], ea[1], base[1])
    el[0] = mm(split(el[1]), split(lp[1]))

    z_next(fg, ID_ZF, 1, 1)
    z_next(fg, ID_ZF, 0, 1, cond=is_b)
    xa_mates = direct(xa, ID_XA, x, x_at, constant_part)
    done(xl_mates + opposite(xl, ID_XL, x, link_part))
    sends_half = both(later, edge)
    behind, ahead, across = places(x)
    z_next(fg, ID_ZF, 1, 2)
    z_next(fg, ID_ZF, 0, 2, cond=is_b)
    done(xa_mates)

    @pl.when(sends_half)
    def _():
        near_products(xl)
        zero = jnp.zeros((256, 256), F32)
        th[...] = term(xa, behind, term(xa, ahead, term(xa, x, zero)))

    @pl.when(h == 0)
    def _():
        exclusive_links(xl, x, el.at[2])
        entry = split(el[2])
        for p in (1, 0):
            link = mm(entry, split(el[p]))
            pb[...] = link.T
            gg[p] = mm(split(link), split(fg[p]))
            gh[p], gl[p] = split(gg[p])
            own = gg[p, :, pl.ds(pl.multiple_of(r * 128, 128), 128)].T
            at = slice(p * 192, p * 192 + 192)
            kh[at, :], kl[at, :] = split(jnp.concatenate([own, pb[pl.ds(r * 64, 64), :]], 0))

    done(opposite(xa, ID_XA, x, constant_part))

    hop = z_at(jnp.where(r == 0, -1, 1))

    def zh(j, kind):
        if j < 2:
            part = pl.ds(c * 128 + j * 64, 64), pl.ds(pl.multiple_of(c * 128, 128), 128)
        else:
            part = pl.ds(c * 64, 64), pl.ds(128, 128)
        piece = ph.at[*part]
        if kind == 0:
            return copy(th.at[*part], piece, ID_ZH + j, hop)
        return copy(piece, piece, ID_ZH + 3 * kind + j, inward if kind == 1 else mate)

    @pl.when(sends_half)
    def _():
        th[...] = term(xa, across, th[...])
        for j in (0, 1, 2):
            zh(j, 0).start()

    exclusive_constants(xl, xa, x, ea.at[2])

    def outputs(p):
        constant = sandwich(el[p], ea[2], ea[p])
        mine = fg[p, :, pl.ds(pl.multiple_of(r * 128, 128), 128)]
        middle = mm(split(constant), split(mine))
        pb[...] = constant
        left = jnp.concatenate([middle.T, pb[pl.ds(r * 64, 64), :]], 0)
        out = mm(split(left), split(fg[p]))
        cov[p] += out[:128]
        off[p] = out[128:]

    outputs(1)

    @pl.when(both(h == 0, edge))
    def _():
        for j in (0, 1, 2):
            zh(j, 0).wait_recv()
            zh(j, 1).start()
            zh(j, 2).start()

    outputs(0)
    for sends, one in started:
        if sends is None:
            one.wait_send()
        else:

            @pl.when(sends)
            def _():
                one().wait_send()

    @pl.when(both(h == 0, jnp.logical_not(edge)))
    def _():
        for j in (0, 1, 2):
            zh(j, 1).wait_recv()
            zh(j, 2).start()

    @pl.when(h == 0)
    def _():
        for j in (0, 1, 2):
            zh(j, 2).wait_recv()
        left = split(mm((kh[...], kl[...]), split(whole(ph[...]))))
        for p in (0, 1):
            at = slice(p * 192, p * 192 + 192)
            out = mm((left[0][at], left[1][at]), (gh[p], gl[p]))
            cov[p] += out[:128]
            off[p] += out[128:]

    for p in (0, 1):
        off[p] = off[p] * (-mask[p, r].astype(F32))

    @pl.when(sends_half)
    def _():
        for j in (0, 1, 2):
            zh(j, 0).wait_send()

    @pl.when(jnp.logical_and(h == 0, edge))
    def _():
        for j in (0, 1, 2):
            zh(j, 1).wait_send()

    @pl.when(h == 0)
    def _():
        for j in (0, 1, 2):
            zh(j, 2).wait_send()


def put_out(cov, off, cov_out, off_out, sems):
    copies = (
        pltpu.make_async_copy(cov, cov_out, sems.at[0]),
        pltpu.make_async_copy(off, off_out, sems.at[1]),
    )
    for one in copies:
        one.start()
    for one in copies:
        one.wait()


def body(fill_blocks, fill_mask, inv_diag, factor_off):
    vmem = pl.BlockSpec(memory_space=pltpu.VMEM)

    def sq(n):
        return pltpu.VMEM((n, 256, 256), F32)

    results = pl.pallas_call(
        kernel,
        name="chain",
        out_shape=(pltpu.VMEM((2, 128, 512), F32), pltpu.VMEM((2, 64, 512), F32)),
        in_specs=[pl.BlockSpec(memory_space=pltpu.HBM)] * 4,
        out_specs=(vmem, vmem),
        scratch_shapes=[
            pltpu.SMEM((2, 4), jnp.int32),
            pltpu.SMEM((2, 4), jnp.int32),
            pltpu.VMEM((2, 512, 512), F32),
            pltpu.VMEM((2, 64, 512), F32),
            pltpu.SemaphoreType.DMA((5,)),
            pltpu.VMEM((8, 256), jnp.int32),
            pltpu.VMEM((8, 256), jnp.int32),
            pltpu.VMEM((2, 512, 512), BF16),
            pltpu.VMEM((2, 512, 512), BF16),
            sq(2),
            pltpu.VMEM((2, 256, 512), F32),
            sq(2),
            sq(2),
            sq(2),
            sq(4),
            sq(4),
            sq(4),
            sq(4),
            sq(3),
            sq(3),
            pltpu.VMEM((256, 256), F32),
            pltpu.VMEM((256, 256), F32),
            pltpu.VMEM((256, 256), F32),
            sq(4),
            pltpu.VMEM((256, 256), F32),
            pltpu.VMEM((2, 256, 512), F32),
            pltpu.VMEM((2, 256, 512), BF16),
            pltpu.VMEM((2, 256, 512), BF16),
            pltpu.VMEM((384, 256), BF16),
            pltpu.VMEM((384, 256), BF16),
            pltpu.VMEM((512, 256), BF16),
            pltpu.SemaphoreType.DMA((N_IDS,)),
            pltpu.SemaphoreType.DMA((N_IDS,)),
        ],
        compiler_params=pltpu.CompilerParams(
            collective_id=0, has_side_effects=True
        ),
    )(fill_blocks, fill_mask, inv_diag, factor_off)
    hbm = pl.BlockSpec(memory_space=pltpu.HBM)
    return pl.pallas_call(
        put_out,
        name="put_out",
        out_shape=(
            jax.ShapeDtypeStruct((2, 128, 512), F32),
            jax.ShapeDtypeStruct((2, 64, 512), F32),
        ),
        in_specs=[vmem, vmem],
        out_specs=(hbm, hbm),
        scratch_shapes=[pltpu.SemaphoreType.DMA((2,))],
        compiler_params=pltpu.CompilerParams(vmem_limit_bytes=4 << 20),
    )(*results)


def solution(mesh):
    torus = Mesh(mesh.devices.reshape(2, 4, 4, 2, mesh.shape["row"]), (*SEG, "row"))
    placed = (P(SEG, None), P(SEG, None), P(SEG, None, None), P(SEG, "row", None))
    return jax.shard_map(
        body,
        mesh=torus,
        in_specs=placed,
        out_specs=(P(SEG, "row", None), P(SEG, "row", None)),
        check_vma=False,
    )
```

```python
import jax
import jax.numpy as jnp
from jax import lax
from jax.experimental import pallas as pl
from jax.experimental.pallas import tpu as pltpu
from jax.sharding import Mesh
from jax.sharding import PartitionSpec as P

BLOCK = 64
SEG = ("seg_0", "seg_1", "seg_2", "seg_3")
F32 = jnp.float32
BF16 = jnp.bfloat16
N_IDS = 100

ID_IDX = 0
ID_ZL = 1
ID_ZF = 13
ID_CL = 25
ID_CA = 26
ID_YL = 27
ID_YA = 39
ID_XL = 51
ID_XA = 63
ID_ZL_LATE = 84
ID_ZF_LATE = 90
ID_RELAY = 99
ID_ZH = 75


def split(v):
    hi = v.astype(BF16)
    return hi, (v - hi.astype(F32)).astype(BF16)


def dot(a, b):
    return lax.dot_general(a, b, (((1,), (0,)), ((), ())), preferred_element_type=F32)


def mm(a, b):
    (ah, al), (bh, bl) = a, b
    return dot(ah, bh) + (dot(ah, bl) + dot(al, bh))


def sandwich(link, inner, added):
    left = mm(split(link.T), split(inner))
    return added + mm(split(left), split(link))


def kernel(
    blocks_hbm, mask_hbm, inv_hbm, fac_hbm, cov, off,
    blocks, mask, inv, fac, local, idx_out, idx_in, inv_h, inv_l, lp, fg, base, cl, ca, yl, ya, xl, xa,
    el, ea, ph, th, pb, rb, sm, gg, kk, ss, rs,
):
    h, x, y, c = (lax.axis_index(a) for a in SEG)
    r = lax.axis_index("row")
    z = 4 * h + r
    seg = ((h * 4 + x) * 4 + y) * 2 + c

    both = jnp.logical_and

    def z_at(d):
        zz = lax.rem(z + d + 8, 8)
        return {"seg_0": zz // 4, "row": lax.rem(zz, 4)}

    def seg_at(d):
        s = lax.rem(seg + d + 64, 64)
        return {
            "seg_0": s // 32,
            "seg_1": lax.rem(s // 8, 4),
            "seg_2": lax.rem(s // 2, 4),
            "seg_3": lax.rem(s, 2),
        }

    def y_at(d):
        return {"seg_2": lax.rem(y + d + 4, 4)}

    def x_at(d):
        return {"seg_1": lax.rem(x + d + 4, 4)}

    mate = {"seg_3": 1 - c}

    loads = [
        pltpu.make_async_copy(src, dst, local.at[i])
        for i, (src, dst) in enumerate((
            (blocks_hbm, blocks), (mask_hbm, mask), (fac_hbm, fac),
            (inv_hbm.at[c], inv.at[c]), (inv_hbm.at[1 - c], inv.at[1 - c]),
        ))
    ]
    for load in loads:
        load.start()

    barrier = pltpu.get_barrier_semaphore()

    def greet(who):
        pl.semaphore_signal(barrier, 1, device_id=who, device_id_type=pl.DeviceIdType.MESH)

    for who in (mate, z_at(1), z_at(-1), y_at(1), y_at(-1), x_at(1), x_at(-1)):
        greet(who)

    later = h == 1
    edge = jnp.logical_or(r == 0, r == 3)
    tail = both(both(x == 3, y == 3), c == 1)
    head = both(both(x == 0, y == 0), c == 0)
    plain_out, plain_in = jnp.logical_not(tail), jnp.logical_not(head)
    far_out = both(both(tail, h == 0), edge)
    far_in = both(both(head, later), edge)
    relay_in = both(both(head, later), jnp.logical_not(edge))
    across_half = {
        "seg_0": 1 - h, "seg_1": lax.rem(x + 1 + 2 * h, 4), "seg_2": lax.rem(y + 1 + 2 * h, 4),
        "seg_3": 1 - c, "row": 3 - r,
    }
    for cond, who in (
        (plain_in, seg_at(-1)), (far_in, across_half),
    ):

        @pl.when(cond)
        def _():
            greet(who)

    greetings = 7
    for cond in (plain_out, far_out):
        greetings = greetings + jnp.where(cond, 1, 0)

    started = []

    def copy(src, dst, number, who):
        return pltpu.make_async_remote_copy(
            src_ref=src, dst_ref=dst, send_sem=ss.at[number], recv_sem=rs.at[number],
            device_id=who, device_id_type=pl.DeviceIdType.MESH,
        )

    for load in loads[:3]:
        load.wait()

    lane = lax.broadcasted_iota(jnp.int32, (8, 256), 1)
    slot = lane // BLOCK

    def targets(panel):
        t = jnp.zeros((8, 256), jnp.int32)
        for s in range(4):
            t = jnp.where(slot == s, blocks[panel, s], t)
        return t * BLOCK + (lane - slot * BLOCK)

    idx_out[...] = targets(1)
    target_1 = targets(0)

    row_at = lax.broadcasted_iota(jnp.int32, (512, 256), 0)

    def chooser(t):
        return jnp.where(row_at == t[0:1, :], 1.0, 0.0).astype(BF16)

    def keep(panel):
        live = mask[panel, r].astype(F32)
        return jnp.where(seg * 2 + panel < 127, live, 0.0)

    def factor_rows(p):
        ih, il = split(inv[p])
        inv_h[p] = ih
        inv_l[p] = il
        fh, fl = split(fac[p] * keep(p))
        fg[p, pl.ds(r * 64, 64), :256] = mm((fh, fl), (ih[:, :256], il[:, :256]))
        fg[p, pl.ds(r * 64, 64), 256:] = mm((fh[:, 256:], fl[:, 256:]), (ih[256:, 256:], il[256:, 256:]))

    def local_link(p, choose):
        fh, fl = split(fg[p, pl.ds(r * 64, 64), :])
        lp[p, pl.ds(r * 64, 64), :] = dot(fh, choose) + dot(fl, choose)

    def local_base(p, choose):
        ch = dot(inv_h[p], choose)
        cl_ = dot(inv_l[p], choose)
        chh, cll = ch.astype(BF16), cl_.astype(BF16)
        cth, ctl = ch.T.astype(BF16), cl_.T.astype(BF16)
        base[p] = mm((cth, ctl), (chh, cll))

    is_a, is_b = c == 0, c == 1
    loads[3].wait()
    factor_rows(c)

    @pl.when(is_b)
    def _():
        local_link(1, chooser(target_1))

    pl.semaphore_wait(barrier, greetings)

    def begin(cond, made):
        @pl.when(cond)
        def _():
            made().start()

        started.append((cond, made))

    begin(plain_out, lambda: copy(idx_out, idx_in, ID_IDX, seg_at(1)))
    begin(far_out, lambda: copy(idx_out, idx_in, ID_IDX, across_half))
    inward = z_at(jnp.where(r == 0, 1, -1))

    @pl.when(both(head, h == 0))
    def _():
        idx_in[...] = target_1

    relay = lambda: copy(idx_in, idx_in, ID_RELAY, inward)

    def z_parts(buf, ids, p, k, up, lo, n):
        block = (r - k) if up else (r + k)
        block_in = (r - 1 - k) if up else (r + 1 + k)
        sends = jnp.logical_and(r < 3, r - k >= 0) if up else jnp.logical_and(r > 0, r + k <= 3)
        takes = (r - 1 - k >= 0) if up else (r + 1 + k <= 3)
        number = ids + p * 6 + (0 if up else 3) + k
        who = z_at(1 if up else -1)

        def made(b):
            part = buf.at[p, pl.ds(b * 64 + lo, n), :]
            return copy(part, part, number, who)

        return sends, takes, lambda: made(block), lambda: made(block_in)

    def z_send(buf, ids, p, k, lo=0, n=64, cond=None):
        for up in (True, False):
            sends, _, out, _ = z_parts(buf, ids, p, k, up, lo, n)
            if cond is not None:
                sends = both(sends, cond)

            @pl.when(sends)
            def _():
                out().start()

            started.append((sends, out))

    def z_take(buf, ids, p, k, lo=0, n=64, cond=None):
        for up in (True, False):
            _, takes, _, into = z_parts(buf, ids, p, k, up, lo, n)
            if cond is not None:
                takes = both(takes, cond)

            @pl.when(takes)
            def _():
                into().wait_recv()

    def z_next(buf, ids, p, k, lo=0, n=64, cond=None):
        z_take(buf, ids, p, k, lo, n, cond)
        if k < 2:
            z_send(buf, ids, p, k + 1, lo, n, cond)

    waits_long = both(head, later)
    units = (
        (fg, ID_ZF, 0, 0, 32, is_a), (fg, ID_ZF_LATE, 0, 32, 32, is_a),
        (lp, ID_ZL, 1, 0, 64, None),
        (lp, ID_ZL, 0, 0, 32, is_b), (lp, ID_ZL_LATE, 0, 32, 32, is_b),
    )

    def every(k):
        for buf, ids, p, lo, n, cond in units:
            z_next(buf, ids, p, k, lo, n, cond)

    for buf, ids, p, lo, n, cond in units[:2]:
        z_send(buf, ids, p, 0, lo, n, cond)
    z_send(lp, ID_ZL, 1, 0, cond=is_b)
    loads[4].wait()
    factor_rows(1 - c)

    @pl.when(is_a)
    def _():
        local_link(1, chooser(target_1))

    z_send(lp, ID_ZL, 1, 0, cond=is_a)

    @pl.when(is_b)
    def _():
        copy(idx_out, idx_in, ID_IDX, mate).wait_recv()
        local_link(0, chooser(idx_in[...]))

    for buf, ids, p, lo, n, cond in units[3:]:
        z_send(buf, ids, p, 0, lo, n, cond)
    local_base(1, chooser(target_1))
    every(0)

    @pl.when(both(is_a, plain_in))
    def _():
        copy(idx_out, idx_in, ID_IDX, mate).wait_recv()

    @pl.when(jnp.logical_not(waits_long))
    def _():
        local_base(0, chooser(idx_in[...]))

    every(1)

    @pl.when(far_in)
    def _():
        copy(idx_out, idx_in, ID_IDX, mate).wait_recv()

    begin(far_in, relay)
    for p in (0, 1):
        mine = inv[p, :, pl.ds(pl.multiple_of(r * 128, 128), 128)]
        cov[p] = mm(split(mine.T), (inv_h[p], inv_l[p]))

    @pl.when(relay_in)
    def _():
        relay().wait_recv()

    @pl.when(waits_long)
    def _():
        local_base(0, chooser(idx_in[...]))

    every(2)

    @pl.when(is_a)
    def _():
        fh, fl = split(fg[0])
        choose = chooser(idx_in[...])
        lp[0] = dot(fh, choose) + dot(fl, choose)


    link_0 = split(lp[0])
    cl[c] = mm(split(lp[1]), link_0)
    cl_copy = copy(cl.at[c], cl.at[c], ID_CL, mate)
    cl_copy.start()
    ca[c] = sandwich(lp[0], base[1], base[0])
    ca_copy = copy(ca.at[c], ca.at[c], ID_CA, mate)
    ca_copy.start()
    started.append((None, cl_copy))
    started.append((None, ca_copy))

    turn = 1 - 2 * c

    def link_part(j):
        return pl.ds(c * 128 + j * 64, 64), slice(None)

    def constant_part(j):
        if j == 0:
            at = pl.ds(pl.multiple_of(c * 128, 128), 128)
            return at, at
        return pl.ds(c * 64, 64), pl.ds(128, 128)

    def ring_send(buf, ids, at, where, part):
        for way, j in ((0, 0), (1, 1), (0, 1), (1, 0)):
            piece = buf.at[at, *part(j)]
            one = copy(piece, piece, ids + way * 2 + j, where(turn if way == 0 else -turn))
            one.start()
            started.append((None, one))

    def places(at):
        return tuple(lax.rem(at + d + 4, 4) for d in (-turn, turn, 2))

    def mated(buf, place, j, number, part):
        piece = buf.at[place, *part(j)]
        one = copy(piece, piece, number, mate)
        one.start()
        started.append((None, one))
        return one

    def direct(buf, ids, at, where, part):
        behind, ahead, _ = places(at)
        mates = []
        for way, j in ((0, 0), (1, 1), (0, 1), (1, 0)):
            place = behind if way == 0 else ahead
            piece = buf.at[place, *part(j)]
            copy(piece, piece, ids + way * 2 + j, mate).wait_recv()
            if way == j:
                onward = copy(piece, piece, ids + 4 + way, where(turn if way == 0 else -turn))
                onward.start()
                started.append((None, onward))
            mates.append(mated(buf, place, j, ids + 6 + way * 2 + j, part))
        return mates

    def opposite(buf, ids, at, part):
        across = places(at)[2]
        mates = []
        for way in (0, 1):
            piece = buf.at[across, *part(way)]
            copy(piece, piece, ids + 4 + way, mate).wait_recv()
            mates.append(mated(buf, across, way, ids + 10 + way, part))
        return mates

    def done(mates):
        for one in mates:
            one.wait_recv()

    def whole(v):
        return jnp.concatenate([v[:128], jnp.concatenate([v[:128, 128:].T, v[128:, 128:]], 1)], 0)

    rows_256 = lax.broadcasted_iota(jnp.int32, (256, 256), 0)
    eye = (rows_256 == lax.broadcasted_iota(jnp.int32, (256, 256), 1)).astype(F32)

    def near_products(buf):
        rb[0] = eye
        rb[1] = buf[0]
        low = mm(split(buf[1]), split(buf[0]))
        rb[2] = low
        rb[3] = mm(split(buf[2]), split(low))

    def term(buf, place, added):
        return sandwich(rb[place], whole(buf[place]), added)

    def exclusive_links(links, at, out):
        @pl.when(at == 3)
        def _():
            out[...] = eye

        @pl.when(at < 3)
        def _():
            out[...] = links[3]

        for i in (2, 1):

            @pl.when(at < i)
            def _():
                out[...] = mm(split(out[...]), split(links[i]))

    def exclusive_constants(links, consts, at, out):
        @pl.when(at == 3)
        def _():
            out[...] = jnp.zeros((256, 256), F32)

        @pl.when(at < 3)
        def _():
            out[...] = whole(consts[3])

        for i in (2, 1):

            @pl.when(at < i)
            def _():
                out[...] = sandwich(links[i], out[...], whole(consts[i]))

    cl_copy.wait_recv()
    yl[y] = mm(split(cl[1]), split(cl[0]))
    ring_send(yl, ID_YL, y, y_at, link_part)
    ca_copy.wait_recv()
    ya[y] = sandwich(cl[0], ca[1], ca[0])
    ring_send(ya, ID_YA, y, y_at, constant_part)
    z_send(fg, ID_ZF, 1, 0)
    z_send(fg, ID_ZF, 0, 0, cond=is_b)

    yl_mates = direct(yl, ID_YL, y, y_at, link_part)
    ya_mates = direct(ya, ID_YA, y, y_at, constant_part)
    done(yl_mates)
    done(ya_mates)

    @pl.when(y == 0)
    def _():
        rb[2] = mm(split(yl[1]), split(yl[0]))
        sm[...] = sandwich(yl[0], whole(ya[1]), whole(ya[0]))

    @pl.when(y == 1)
    def _():
        low = mm(split(yl[1]), split(yl[0]))
        near = sandwich(yl[0], whole(ya[1]), whole(ya[0]))
        rb[3] = mm(split(yl[2]), split(low))
        sm[...] = sandwich(low, whole(ya[2]), near)

    @pl.when(y == 2)
    def _():
        rb[0] = eye
        sm[...] = sandwich(yl[1], sandwich(yl[2], whole(ya[3]), whole(ya[2])), whole(ya[1]))

    @pl.when(y == 3)
    def _():
        rb[1] = yl[0]
        sm[...] = sandwich(yl[2], whole(ya[3]), whole(ya[2]))

    done(opposite(yl, ID_YL, y, link_part))
    high = mm(split(yl[3]), split(yl[2]))
    low = mm(split(yl[1]), split(yl[0]))
    xl[x] = mm(split(high), split(low))
    ring_send(xl, ID_XL, x, x_at, link_part)
    z_next(fg, ID_ZF, 1, 0)
    z_next(fg, ID_ZF, 0, 0, cond=is_b)

    @pl.when(y == 0)
    def _():
        sm[...] = sandwich(mm(split(yl[2]), split(rb[2])), whole(ya[3]), sm[...])

    @pl.when(y == 2)
    def _():
        sm[...] = sandwich(yl[0], sm[...], jnp.zeros((256, 256), F32))

    @pl.when(y == 3)
    def _():
        sm[...] = sandwich(mm(split(yl[1]), split(yl[0])), sm[...], whole(ya[0]))

    across = places(y)[2]
    done(opposite(ya, ID_YA, y, constant_part))
    xa[x] = term(ya, across, sm[...])
    ring_send(xa, ID_XA, x, x_at, constant_part)

    exclusive_links(yl, y, el.at[1])
    exclusive_constants(yl, ya, y, ea.at[1])
    xl_mates = direct(xl, ID_XL, x, x_at, link_part)

    @pl.when(c == 0)
    def _():
        ea[1] = sandwich(cl[1], ea[1], ca[1])
        el[1] = mm(split(el[1]), split(cl[1]))

    ea[0] = sandwich(lp[1], ea[1], base[1])
    el[0] = mm(split(el[1]), split(lp[1]))

    z_next(fg, ID_ZF, 1, 1)
    z_next(fg, ID_ZF, 0, 1, cond=is_b)
    xa_mates = direct(xa, ID_XA, x, x_at, constant_part)
    done(xl_mates + opposite(xl, ID_XL, x, link_part))
    sends_half = both(later, edge)
    behind, ahead, across = places(x)
    z_next(fg, ID_ZF, 1, 2)
    z_next(fg, ID_ZF, 0, 2, cond=is_b)
    done(xa_mates)

    @pl.when(sends_half)
    def _():
        near_products(xl)
        zero = jnp.zeros((256, 256), F32)
        th[...] = term(xa, behind, term(xa, ahead, term(xa, x, zero)))

    @pl.when(h == 0)
    def _():
        exclusive_links(xl, x, el.at[2])
        entry = split(el[2])
        for p in (1, 0):
            link = mm(entry, split(el[p]))
            pb[...] = link.T
            gg[p] = mm(split(link), split(fg[p]))
            kk[p * 192 : p * 192 + 128, :] = gg[p, :, pl.ds(pl.multiple_of(r * 128, 128), 128)].T
            kk[p * 192 + 128 : p * 192 + 192, :] = pb[pl.ds(r * 64, 64), :]

    done(opposite(xa, ID_XA, x, constant_part))

    hop = z_at(jnp.where(r == 0, -1, 1))

    def zh(j, kind):
        if j < 2:
            part = pl.ds(c * 128 + j * 64, 64), pl.ds(pl.multiple_of(c * 128, 128), 128)
        else:
            part = pl.ds(c * 64, 64), pl.ds(128, 128)
        piece = ph.at[*part]
        if kind == 0:
            return copy(th.at[*part], piece, ID_ZH + j, hop)
        return copy(piece, piece, ID_ZH + 3 * kind + j, inward if kind == 1 else mate)

    @pl.when(sends_half)
    def _():
        th[...] = term(xa, across, th[...])
        for j in (0, 1, 2):
            zh(j, 0).start()

    exclusive_constants(xl, xa, x, ea.at[2])

    def outputs(p):
        constant = sandwich(el[p], ea[2], ea[p])
        mine = fg[p, :, pl.ds(pl.multiple_of(r * 128, 128), 128)]
        middle = mm(split(constant), split(mine))
        pb[...] = constant
        left = jnp.concatenate([middle.T, pb[pl.ds(r * 64, 64), :]], 0)
        out = mm(split(left), split(fg[p]))
        cov[p] += out[:128]
        off[p] = out[128:]

    outputs(1)

    @pl.when(both(h == 0, edge))
    def _():
        for j in (0, 1, 2):
            zh(j, 0).wait_recv()
            zh(j, 1).start()
            zh(j, 2).start()

    outputs(0)
    for sends, one in started:
        if sends is None:
            one.wait_send()
        else:

            @pl.when(sends)
            def _():
                one().wait_send()

    @pl.when(both(h == 0, jnp.logical_not(edge)))
    def _():
        for j in (0, 1, 2):
            zh(j, 1).wait_recv()
            zh(j, 2).start()

    @pl.when(h == 0)
    def _():
        for j in (0, 1, 2):
            zh(j, 2).wait_recv()
        left = split(mm(split(kk[...]), split(whole(ph[...]))))
        for p in (0, 1):
            at = slice(p * 192, p * 192 + 192)
            out = mm((left[0][at], left[1][at]), split(gg[p]))
            cov[p] += out[:128]
            off[p] += out[128:]

    for p in (0, 1):
        off[p] = off[p] * (-mask[p, r].astype(F32))

    @pl.when(sends_half)
    def _():
        for j in (0, 1, 2):
            zh(j, 0).wait_send()

    @pl.when(jnp.logical_and(h == 0, edge))
    def _():
        for j in (0, 1, 2):
            zh(j, 1).wait_send()

    @pl.when(h == 0)
    def _():
        for j in (0, 1, 2):
            zh(j, 2).wait_send()


def put_out(cov, off, cov_out, off_out, sems):
    copies = [
        pltpu.make_async_copy(src.at[p], dst.at[p], sems.at[2 * i + p])
        for i, (src, dst) in enumerate(((cov, cov_out), (off, off_out)))
        for p in (0, 1)
    ]
    for one in copies:
        one.start()
    for one in copies:
        one.wait()


def body(fill_blocks, fill_mask, inv_diag, factor_off):
    vmem = pl.BlockSpec(memory_space=pltpu.VMEM)

    def sq(n):
        return pltpu.VMEM((n, 256, 256), F32)

    results = pl.pallas_call(
        kernel,
        name="chain",
        out_shape=(pltpu.VMEM((2, 128, 512), F32), pltpu.VMEM((2, 64, 512), F32)),
        in_specs=[pl.BlockSpec(memory_space=pltpu.HBM)] * 4,
        out_specs=(vmem, vmem),
        scratch_shapes=[
            pltpu.SMEM((2, 4), jnp.int32),
            pltpu.SMEM((2, 4), jnp.int32),
            pltpu.VMEM((2, 512, 512), F32),
            pltpu.VMEM((2, 64, 512), F32),
            pltpu.SemaphoreType.DMA((5,)),
            pltpu.VMEM((8, 256), jnp.int32),
            pltpu.VMEM((8, 256), jnp.int32),
            pltpu.VMEM((2, 512, 512), BF16),
            pltpu.VMEM((2, 512, 512), BF16),
            sq(2),
            pltpu.VMEM((2, 256, 512), F32),
            sq(2),
            sq(2),
            sq(2),
            sq(4),
            sq(4),
            sq(4),
            sq(4),
            sq(3),
            sq(3),
            pltpu.VMEM((256, 256), F32),
            pltpu.VMEM((256, 256), F32),
            pltpu.VMEM((256, 256), F32),
            sq(4),
            pltpu.VMEM((256, 256), F32),
            pltpu.VMEM((2, 256, 512), F32),
            pltpu.VMEM((384, 256), F32),
            pltpu.SemaphoreType.DMA((N_IDS,)),
            pltpu.SemaphoreType.DMA((N_IDS,)),
        ],
        compiler_params=pltpu.CompilerParams(
            collective_id=0, has_side_effects=True
        ),
    )(fill_blocks, fill_mask, inv_diag, factor_off)
    hbm = pl.BlockSpec(memory_space=pltpu.HBM)
    return pl.pallas_call(
        put_out,
        name="put_out",
        out_shape=(
            jax.ShapeDtypeStruct((2, 128, 512), F32),
            jax.ShapeDtypeStruct((2, 64, 512), F32),
        ),
        in_specs=[vmem, vmem],
        out_specs=(hbm, hbm),
        scratch_shapes=[pltpu.SemaphoreType.DMA((4,))],
        compiler_params=pltpu.CompilerParams(vmem_limit_bytes=4 << 20),
    )(*results)


def solution(mesh):
    torus = Mesh(mesh.devices.reshape(2, 4, 4, 2, mesh.shape["row"]), (*SEG, "row"))
    placed = (P(SEG, None), P(SEG, None), P(SEG, None, None), P(SEG, "row", None))
    return jax.shard_map(
        body,
        mesh=torus,
        in_specs=placed,
        out_specs=(P(SEG, "row", None), P(SEG, "row", None)),
        check_vma=False,
    )
```

```python
import jax
import jax.numpy as jnp
from jax import lax
from jax.experimental import pallas as pl
from jax.experimental.pallas import tpu as pltpu
from jax.sharding import Mesh
from jax.sharding import PartitionSpec as P

BLOCK = 64
SEG = ("seg_0", "seg_1", "seg_2", "seg_3")
F32 = jnp.float32
BF16 = jnp.bfloat16
N_IDS = 100

ID_IDX = 0
ID_ZL = 1
ID_ZF = 13
ID_CL = 25
ID_CA = 26
ID_YL = 27
ID_YA = 39
ID_XL = 51
ID_XA = 63
ID_ZL_LATE = 84
ID_ZF_LATE = 90
ID_RELAY = 99
ID_ZH = 75


def split(v):
    hi = v.astype(BF16)
    return hi, (v - hi.astype(F32)).astype(BF16)


def dot(a, b):
    return lax.dot_general(a, b, (((1,), (0,)), ((), ())), preferred_element_type=F32)


def mm(a, b):
    (ah, al), (bh, bl) = a, b
    return dot(ah, bh) + (dot(ah, bl) + dot(al, bh))


def sandwich(link, inner, added):
    left = mm(split(link.T), split(inner))
    return added + mm(split(left), split(link))


def kernel(
    blocks_hbm, mask_hbm, inv_hbm, fac_hbm, cov, off,
    blocks, mask, inv, fac, local, idx_out, idx_in, inv_h, inv_l, lp, fg, base, cl, ca, yl, ya, xl, xa,
    el, ea, ph, th, pb, rb, sm, gg, kk, ss, rs,
):
    h, x, y, c = (lax.axis_index(a) for a in SEG)
    r = lax.axis_index("row")
    z = 4 * h + r
    seg = ((h * 4 + x) * 4 + y) * 2 + c

    both = jnp.logical_and

    def z_at(d):
        zz = lax.rem(z + d + 8, 8)
        return {"seg_0": zz // 4, "row": lax.rem(zz, 4)}

    def seg_at(d):
        s = lax.rem(seg + d + 64, 64)
        return {
            "seg_0": s // 32,
            "seg_1": lax.rem(s // 8, 4),
            "seg_2": lax.rem(s // 2, 4),
            "seg_3": lax.rem(s, 2),
        }

    def y_at(d):
        return {"seg_2": lax.rem(y + d + 4, 4)}

    def x_at(d):
        return {"seg_1": lax.rem(x + d + 4, 4)}

    mate = {"seg_3": 1 - c}

    loads = [
        pltpu.make_async_copy(src, dst, local.at[i])
        for i, (src, dst) in enumerate((
            (blocks_hbm, blocks), (mask_hbm, mask), (fac_hbm, fac),
            (inv_hbm.at[c], inv.at[c]), (inv_hbm.at[1 - c], inv.at[1 - c]),
        ))
    ]
    for load in loads:
        load.start()

    barrier = pltpu.get_barrier_semaphore()

    def greet(who):
        pl.semaphore_signal(barrier, 1, device_id=who, device_id_type=pl.DeviceIdType.MESH)

    for who in (mate, z_at(1), z_at(-1), y_at(1), y_at(-1), x_at(1), x_at(-1)):
        greet(who)

    later = h == 1
    edge = jnp.logical_or(r == 0, r == 3)
    tail = both(both(x == 3, y == 3), c == 1)
    head = both(both(x == 0, y == 0), c == 0)
    plain_out, plain_in = jnp.logical_not(tail), jnp.logical_not(head)
    far_out = both(both(tail, h == 0), edge)
    far_in = both(both(head, later), edge)
    relay_in = both(both(head, later), jnp.logical_not(edge))
    across_half = {
        "seg_0": 1 - h, "seg_1": lax.rem(x + 1 + 2 * h, 4), "seg_2": lax.rem(y + 1 + 2 * h, 4),
        "seg_3": 1 - c, "row": 3 - r,
    }
    for cond, who in (
        (plain_in, seg_at(-1)), (far_in, across_half),
    ):

        @pl.when(cond)
        def _():
            greet(who)

    greetings = 7
    for cond in (plain_out, far_out):
        greetings = greetings + jnp.where(cond, 1, 0)

    started = []

    def copy(src, dst, number, who):
        return pltpu.make_async_remote_copy(
            src_ref=src, dst_ref=dst, send_sem=ss.at[number], recv_sem=rs.at[number],
            device_id=who, device_id_type=pl.DeviceIdType.MESH,
        )

    for load in loads[:3]:
        load.wait()

    lane = lax.broadcasted_iota(jnp.int32, (8, 256), 1)
    slot = lane // BLOCK

    def targets(panel):
        t = jnp.zeros((8, 256), jnp.int32)
        for s in range(4):
            t = jnp.where(slot == s, blocks[panel, s], t)
        return t * BLOCK + (lane - slot * BLOCK)

    idx_out[...] = targets(1)
    target_1 = targets(0)

    row_at = lax.broadcasted_iota(jnp.int32, (512, 256), 0)

    def chooser(t):
        return jnp.where(row_at == t[0:1, :], 1.0, 0.0).astype(BF16)

    def keep(panel):
        live = mask[panel, r].astype(F32)
        return jnp.where(seg * 2 + panel < 127, live, 0.0)

    def factor_rows(p):
        ih, il = split(inv[p])
        inv_h[p] = ih
        inv_l[p] = il
        fh, fl = split(fac[p] * keep(p))
        fg[p, pl.ds(r * 64, 64), :256] = mm((fh, fl), (ih[:, :256], il[:, :256]))
        fg[p, pl.ds(r * 64, 64), 256:] = mm((fh[:, 256:], fl[:, 256:]), (ih[256:, 256:], il[256:, 256:]))

    def local_link(p, choose):
        fh, fl = split(fg[p, pl.ds(r * 64, 64), :])
        lp[p, pl.ds(r * 64, 64), :] = dot(fh, choose) + dot(fl, choose)

    def local_base(p, choose):
        ch = dot(inv_h[p], choose)
        cl_ = dot(inv_l[p], choose)
        chh, cll = ch.astype(BF16), cl_.astype(BF16)
        cth, ctl = ch.T.astype(BF16), cl_.T.astype(BF16)
        base[p] = mm((cth, ctl), (chh, cll))

    is_a, is_b = c == 0, c == 1
    loads[3].wait()
    factor_rows(c)

    @pl.when(is_b)
    def _():
        local_link(1, chooser(target_1))

    pl.semaphore_wait(barrier, greetings)

    def begin(cond, made):
        @pl.when(cond)
        def _():
            made().start()

        started.append((cond, made))

    begin(plain_out, lambda: copy(idx_out, idx_in, ID_IDX, seg_at(1)))
    begin(far_out, lambda: copy(idx_out, idx_in, ID_IDX, across_half))
    inward = z_at(jnp.where(r == 0, 1, -1))

    @pl.when(both(head, h == 0))
    def _():
        idx_in[...] = target_1

    relay = lambda: copy(idx_in, idx_in, ID_RELAY, inward)

    def z_parts(buf, ids, p, k, up, lo, n):
        block = (r - k) if up else (r + k)
        block_in = (r - 1 - k) if up else (r + 1 + k)
        sends = jnp.logical_and(r < 3, r - k >= 0) if up else jnp.logical_and(r > 0, r + k <= 3)
        takes = (r - 1 - k >= 0) if up else (r + 1 + k <= 3)
        number = ids + p * 6 + (0 if up else 3) + k
        who = z_at(1 if up else -1)

        def made(b):
            part = buf.at[p, pl.ds(b * 64 + lo, n), :]
            return copy(part, part, number, who)

        return sends, takes, lambda: made(block), lambda: made(block_in)

    def z_send(buf, ids, p, k, lo=0, n=64, cond=None):
        for up in (True, False):
            sends, _, out, _ = z_parts(buf, ids, p, k, up, lo, n)
            if cond is not None:
                sends = both(sends, cond)

            @pl.when(sends)
            def _():
                out().start()

            started.append((sends, out))

    def z_take(buf, ids, p, k, lo=0, n=64, cond=None):
        for up in (True, False):
            _, takes, _, into = z_parts(buf, ids, p, k, up, lo, n)
            if cond is not None:
                takes = both(takes, cond)

            @pl.when(takes)
            def _():
                into().wait_recv()

    def z_next(buf, ids, p, k, lo=0, n=64, cond=None):
        z_take(buf, ids, p, k, lo, n, cond)
        if k < 2:
            z_send(buf, ids, p, k + 1, lo, n, cond)

    waits_long = both(head, later)
    units = (
        (fg, ID_ZF, 0, 0, 32, is_a), (fg, ID_ZF_LATE, 0, 32, 32, is_a),
        (lp, ID_ZL, 1, 0, 64, None),
        (lp, ID_ZL, 0, 0, 32, is_b), (lp, ID_ZL_LATE, 0, 32, 32, is_b),
    )

    def every(k):
        for buf, ids, p, lo, n, cond in units:
            z_next(buf, ids, p, k, lo, n, cond)

    for buf, ids, p, lo, n, cond in units[:2]:
        z_send(buf, ids, p, 0, lo, n, cond)
    z_send(lp, ID_ZL, 1, 0, cond=is_b)
    loads[4].wait()
    factor_rows(1 - c)

    @pl.when(is_a)
    def _():
        local_link(1, chooser(target_1))

    z_send(lp, ID_ZL, 1, 0, cond=is_a)

    @pl.when(is_b)
    def _():
        copy(idx_out, idx_in, ID_IDX, mate).wait_recv()
        local_link(0, chooser(idx_in[...]))

    for buf, ids, p, lo, n, cond in units[3:]:
        z_send(buf, ids, p, 0, lo, n, cond)
    local_base(1, chooser(target_1))
    every(0)

    @pl.when(both(is_a, plain_in))
    def _():
        copy(idx_out, idx_in, ID_IDX, mate).wait_recv()

    @pl.when(jnp.logical_not(waits_long))
    def _():
        local_base(0, chooser(idx_in[...]))

    every(1)

    @pl.when(far_in)
    def _():
        copy(idx_out, idx_in, ID_IDX, mate).wait_recv()

    begin(far_in, relay)
    for p in (0, 1):
        mine = inv[p, :, pl.ds(pl.multiple_of(r * 128, 128), 128)]
        cov[p] = mm(split(mine.T), (inv_h[p], inv_l[p]))

    @pl.when(relay_in)
    def _():
        relay().wait_recv()

    @pl.when(waits_long)
    def _():
        local_base(0, chooser(idx_in[...]))

    every(2)

    @pl.when(is_a)
    def _():
        fh, fl = split(fg[0])
        choose = chooser(idx_in[...])
        lp[0] = dot(fh, choose) + dot(fl, choose)


    link_0 = split(lp[0])
    cl[c] = mm(split(lp[1]), link_0)
    cl_copy = copy(cl.at[c], cl.at[c], ID_CL, mate)
    cl_copy.start()
    ca[c] = sandwich(lp[0], base[1], base[0])
    ca_copy = copy(ca.at[c], ca.at[c], ID_CA, mate)
    ca_copy.start()
    started.append((None, cl_copy))
    started.append((None, ca_copy))

    turn = 1 - 2 * c

    def link_part(j):
        return pl.ds(c * 128 + j * 64, 64), slice(None)

    def constant_part(j):
        if j == 0:
            at = pl.ds(pl.multiple_of(c * 128, 128), 128)
            return at, at
        return pl.ds(c * 64, 64), pl.ds(128, 128)

    def ring_send(buf, ids, at, where, part):
        for way, j in ((0, 0), (1, 1), (0, 1), (1, 0)):
            piece = buf.at[at, *part(j)]
            one = copy(piece, piece, ids + way * 2 + j, where(turn if way == 0 else -turn))
            one.start()
            started.append((None, one))

    def places(at):
        return tuple(lax.rem(at + d + 4, 4) for d in (-turn, turn, 2))

    def mated(buf, place, j, number, part):
        piece = buf.at[place, *part(j)]
        one = copy(piece, piece, number, mate)
        one.start()
        started.append((None, one))
        return one

    def direct(buf, ids, at, where, part):
        behind, ahead, _ = places(at)
        mates = []
        for way, j in ((0, 0), (1, 1), (0, 1), (1, 0)):
            place = behind if way == 0 else ahead
            piece = buf.at[place, *part(j)]
            copy(piece, piece, ids + way * 2 + j, mate).wait_recv()
            if way == j:
                onward = copy(piece, piece, ids + 4 + way, where(turn if way == 0 else -turn))
                onward.start()
                started.append((None, onward))
            mates.append(mated(buf, place, j, ids + 6 + way * 2 + j, part))
        return mates

    def opposite(buf, ids, at, part):
        across = places(at)[2]
        mates = []
        for way in (0, 1):
            piece = buf.at[across, *part(way)]
            copy(piece, piece, ids + 4 + way, mate).wait_recv()
            mates.append(mated(buf, across, way, ids + 10 + way, part))
        return mates

    def done(mates):
        for one in mates:
            one.wait_recv()

    def whole(v):
        return jnp.concatenate([v[:128], jnp.concatenate([v[:128, 128:].T, v[128:, 128:]], 1)], 0)

    rows_256 = lax.broadcasted_iota(jnp.int32, (256, 256), 0)
    eye = (rows_256 == lax.broadcasted_iota(jnp.int32, (256, 256), 1)).astype(F32)

    def near_products(buf):
        rb[0] = eye
        rb[1] = buf[0]
        low = mm(split(buf[1]), split(buf[0]))
        rb[2] = low
        rb[3] = mm(split(buf[2]), split(low))

    def term(buf, place, added):
        return sandwich(rb[place], whole(buf[place]), added)

    def exclusive_links(links, at, out):
        @pl.when(at == 3)
        def _():
            out[...] = eye

        @pl.when(at < 3)
        def _():
            out[...] = links[3]

        for i in (2, 1):

            @pl.when(at < i)
            def _():
                out[...] = mm(split(out[...]), split(links[i]))

    def exclusive_constants(links, consts, at, out):
        @pl.when(at == 3)
        def _():
            out[...] = jnp.zeros((256, 256), F32)

        @pl.when(at < 3)
        def _():
            out[...] = whole(consts[3])

        for i in (2, 1):

            @pl.when(at < i)
            def _():
                out[...] = sandwich(links[i], out[...], whole(consts[i]))

    cl_copy.wait_recv()
    yl[y] = mm(split(cl[1]), split(cl[0]))
    ring_send(yl, ID_YL, y, y_at, link_part)
    ca_copy.wait_recv()
    ya[y] = sandwich(cl[0], ca[1], ca[0])
    ring_send(ya, ID_YA, y, y_at, constant_part)

    yl_mates = direct(yl, ID_YL, y, y_at, link_part)
    ya_mates = direct(ya, ID_YA, y, y_at, constant_part)
    z_send(fg, ID_ZF, 1, 0)
    z_send(fg, ID_ZF, 0, 0, cond=is_b)
    done(yl_mates)
    done(ya_mates)

    @pl.when(y == 0)
    def _():
        rb[2] = mm(split(yl[1]), split(yl[0]))
        sm[...] = sandwich(yl[0], whole(ya[1]), whole(ya[0]))

    @pl.when(y == 1)
    def _():
        low = mm(split(yl[1]), split(yl[0]))
        near = sandwich(yl[0], whole(ya[1]), whole(ya[0]))
        rb[3] = mm(split(yl[2]), split(low))
        sm[...] = sandwich(low, whole(ya[2]), near)

    @pl.when(y == 2)
    def _():
        rb[0] = eye
        sm[...] = sandwich(yl[1], sandwich(yl[2], whole(ya[3]), whole(ya[2])), whole(ya[1]))

    @pl.when(y == 3)
    def _():
        rb[1] = yl[0]
        sm[...] = sandwich(yl[2], whole(ya[3]), whole(ya[2]))

    done(opposite(yl, ID_YL, y, link_part))
    high = mm(split(yl[3]), split(yl[2]))
    low = mm(split(yl[1]), split(yl[0]))
    xl[x] = mm(split(high), split(low))
    ring_send(xl, ID_XL, x, x_at, link_part)

    @pl.when(y == 0)
    def _():
        sm[...] = sandwich(mm(split(yl[2]), split(rb[2])), whole(ya[3]), sm[...])

    @pl.when(y == 2)
    def _():
        sm[...] = sandwich(yl[0], sm[...], jnp.zeros((256, 256), F32))

    @pl.when(y == 3)
    def _():
        sm[...] = sandwich(mm(split(yl[1]), split(yl[0])), sm[...], whole(ya[0]))

    across = places(y)[2]
    done(opposite(ya, ID_YA, y, constant_part))
    xa[x] = term(ya, across, sm[...])
    ring_send(xa, ID_XA, x, x_at, constant_part)

    exclusive_links(yl, y, el.at[1])
    exclusive_constants(yl, ya, y, ea.at[1])
    xl_mates = direct(xl, ID_XL, x, x_at, link_part)
    z_next(fg, ID_ZF, 1, 0)
    z_next(fg, ID_ZF, 0, 0, cond=is_b)

    @pl.when(c == 0)
    def _():
        ea[1] = sandwich(cl[1], ea[1], ca[1])
        el[1] = mm(split(el[1]), split(cl[1]))

    ea[0] = sandwich(lp[1], ea[1], base[1])
    el[0] = mm(split(el[1]), split(lp[1]))

    z_next(fg, ID_ZF, 1, 1)
    z_next(fg, ID_ZF, 0, 1, cond=is_b)
    xa_mates = direct(xa, ID_XA, x, x_at, constant_part)
    done(xl_mates + opposite(xl, ID_XL, x, link_part))
    sends_half = both(later, edge)
    behind, ahead, across = places(x)
    z_next(fg, ID_ZF, 1, 2)
    z_next(fg, ID_ZF, 0, 2, cond=is_b)
    done(xa_mates)

    @pl.when(sends_half)
    def _():
        near_products(xl)
        zero = jnp.zeros((256, 256), F32)
        th[...] = term(xa, behind, term(xa, ahead, term(xa, x, zero)))

    @pl.when(h == 0)
    def _():
        exclusive_links(xl, x, el.at[2])
        entry = split(el[2])
        for p in (1, 0):
            link = mm(entry, split(el[p]))
            pb[...] = link.T
            gg[p] = mm(split(link), split(fg[p]))
            kk[p * 192 : p * 192 + 128, :] = gg[p, :, pl.ds(pl.multiple_of(r * 128, 128), 128)].T
            kk[p * 192 + 128 : p * 192 + 192, :] = pb[pl.ds(r * 64, 64), :]

    done(opposite(xa, ID_XA, x, constant_part))

    hop = z_at(jnp.where(r == 0, -1, 1))

    def zh(j, kind):
        if j < 2:
            part = pl.ds(c * 128 + j * 64, 64), pl.ds(pl.multiple_of(c * 128, 128), 128)
        else:
            part = pl.ds(c * 64, 64), pl.ds(128, 128)
        piece = ph.at[*part]
        if kind == 0:
            return copy(th.at[*part], piece, ID_ZH + j, hop)
        return copy(piece, piece, ID_ZH + 3 * kind + j, inward if kind == 1 else mate)

    @pl.when(sends_half)
    def _():
        th[...] = term(xa, across, th[...])
        for j in (0, 1, 2):
            zh(j, 0).start()

    exclusive_constants(xl, xa, x, ea.at[2])

    def outputs(p):
        constant = sandwich(el[p], ea[2], ea[p])
        mine = fg[p, :, pl.ds(pl.multiple_of(r * 128, 128), 128)]
        middle = mm(split(constant), split(mine))
        pb[...] = constant
        left = jnp.concatenate([middle.T, pb[pl.ds(r * 64, 64), :]], 0)
        out = mm(split(left), split(fg[p]))
        cov[p] += out[:128]
        off[p] = out[128:]

    outputs(1)

    @pl.when(both(h == 0, edge))
    def _():
        for j in (0, 1, 2):
            zh(j, 0).wait_recv()
            zh(j, 1).start()
            zh(j, 2).start()

    outputs(0)
    for sends, one in started:
        if sends is None:
            one.wait_send()
        else:

            @pl.when(sends)
            def _():
                one().wait_send()

    @pl.when(both(h == 0, jnp.logical_not(edge)))
    def _():
        for j in (0, 1, 2):
            zh(j, 1).wait_recv()
            zh(j, 2).start()

    @pl.when(h == 0)
    def _():
        for j in (0, 1, 2):
            zh(j, 2).wait_recv()
        left = split(mm(split(kk[...]), split(whole(ph[...]))))
        for p in (0, 1):
            at = slice(p * 192, p * 192 + 192)
            out = mm((left[0][at], left[1][at]), split(gg[p]))
            cov[p] += out[:128]
            off[p] += out[128:]

    for p in (0, 1):
        off[p] = off[p] * (-mask[p, r].astype(F32))

    @pl.when(sends_half)
    def _():
        for j in (0, 1, 2):
            zh(j, 0).wait_send()

    @pl.when(jnp.logical_and(h == 0, edge))
    def _():
        for j in (0, 1, 2):
            zh(j, 1).wait_send()

    @pl.when(h == 0)
    def _():
        for j in (0, 1, 2):
            zh(j, 2).wait_send()


def put_out(cov, off, cov_out, off_out, sems):
    copies = [
        pltpu.make_async_copy(src.at[p], dst.at[p], sems.at[2 * i + p])
        for i, (src, dst) in enumerate(((cov, cov_out), (off, off_out)))
        for p in (0, 1)
    ]
    for one in copies:
        one.start()
    for one in copies:
        one.wait()


def body(fill_blocks, fill_mask, inv_diag, factor_off):
    vmem = pl.BlockSpec(memory_space=pltpu.VMEM)

    def sq(n):
        return pltpu.VMEM((n, 256, 256), F32)

    results = pl.pallas_call(
        kernel,
        name="chain",
        out_shape=(pltpu.VMEM((2, 128, 512), F32), pltpu.VMEM((2, 64, 512), F32)),
        in_specs=[pl.BlockSpec(memory_space=pltpu.HBM)] * 4,
        out_specs=(vmem, vmem),
        scratch_shapes=[
            pltpu.SMEM((2, 4), jnp.int32),
            pltpu.SMEM((2, 4), jnp.int32),
            pltpu.VMEM((2, 512, 512), F32),
            pltpu.VMEM((2, 64, 512), F32),
            pltpu.SemaphoreType.DMA((5,)),
            pltpu.VMEM((8, 256), jnp.int32),
            pltpu.VMEM((8, 256), jnp.int32),
            pltpu.VMEM((2, 512, 512), BF16),
            pltpu.VMEM((2, 512, 512), BF16),
            sq(2),
            pltpu.VMEM((2, 256, 512), F32),
            sq(2),
            sq(2),
            sq(2),
            sq(4),
            sq(4),
            sq(4),
            sq(4),
            sq(3),
            sq(3),
            pltpu.VMEM((256, 256), F32),
            pltpu.VMEM((256, 256), F32),
            pltpu.VMEM((256, 256), F32),
            sq(4),
            pltpu.VMEM((256, 256), F32),
            pltpu.VMEM((2, 256, 512), F32),
            pltpu.VMEM((384, 256), F32),
            pltpu.SemaphoreType.DMA((N_IDS,)),
            pltpu.SemaphoreType.DMA((N_IDS,)),
        ],
        compiler_params=pltpu.CompilerParams(
            collective_id=0, has_side_effects=True
        ),
    )(fill_blocks, fill_mask, inv_diag, factor_off)
    hbm = pl.BlockSpec(memory_space=pltpu.HBM)
    return pl.pallas_call(
        put_out,
        name="put_out",
        out_shape=(
            jax.ShapeDtypeStruct((2, 128, 512), F32),
            jax.ShapeDtypeStruct((2, 64, 512), F32),
        ),
        in_specs=[vmem, vmem],
        out_specs=(hbm, hbm),
        scratch_shapes=[pltpu.SemaphoreType.DMA((4,))],
        compiler_params=pltpu.CompilerParams(vmem_limit_bytes=4 << 20),
    )(*results)


def solution(mesh):
    torus = Mesh(mesh.devices.reshape(2, 4, 4, 2, mesh.shape["row"]), (*SEG, "row"))
    placed = (P(SEG, None), P(SEG, None), P(SEG, None, None), P(SEG, "row", None))
    return jax.shard_map(
        body,
        mesh=torus,
        in_specs=placed,
        out_specs=(P(SEG, "row", None), P(SEG, "row", None)),
        check_vma=False,
    )
```
